32 devices in a mesh: dp: 8 (over y, x, core), ka: 4 (over z).
Axes of the slice: x: 2, y: 2, z: 4, core: 2. Of those that a mesh axis runs over, the one named last changes fastest.
Arguments:
- feats: bfloat16 [16384, 256], P('dp'), may hold values from -6 to 6
- coords: float32 [3, 16384], P(None, 'dp'), may hold values from 0 to 1
- cell_ids: int32 [8, 2048], P('dp'), may hold values from 0 to 7, never falling along the last dimension, each value on 1 to 1024 neighbouring positions
- recip: float32 [8, 8, 9], P('dp'), may hold values from 0.05 to 0.35
- kvec: int32 [3, 512], P(None, 'ka'), may hold values from -4 to 4
- w_in: bfloat16 [256, 256], replicated, may hold values from -0.375 to 0.375
- w_out: bfloat16 [256, 256], replicated, may hold values from -0.375 to 0.375
- kfilt: float32 [512, 256], P('ka'), may hold values from -3 to 3
- spread: float32 [256], replicated, may hold values from 0.02 to 0.5
- cotan: bfloat16 [16384, 256], P('dp'), may hold values from -6 to 6
Outputs:
- mixed: bfloat16 [16384, 256], P('dp')
- feat_grad: bfloat16 [16384, 256], P('dp')
- grad_w_in: float32 [256, 256], replicated
- grad_w_out: float32 [256, 256], replicated
- grad_kfilt: float32 [512, 256], P('ka')
The draws below stay inside these ranges and needn't reach their ends.
Inputs may be any that keep to these rules, and one draw needn't show every extreme that they name: `cell_ids`: within each row, cell numbers never fall; each of the 8 cells holds 1 to 1024 atoms, and one holds exactly 1024.
All inputs are finite; a program needn't handle non-finite values.
Results may differ from the reference program's by a relative error of at most 0.0056.
The reference program's roundings to bfloat16 on the way (of `projected`, `activated`, `message_grad` and `update`) count: a program that leaves them out, or rounds other values in their place, can miss the bound.
Values may be sent and summed in bfloat16 or wider, within the bound.
No kernel may reach another device: no remote copies, remote signals or barrier semaphores. Data moves between devices by JAX's collectives and lax.ppermute only.
A program may use at most 64 MiB of HBM per device.

```python
import math
import jax
import jax.numpy as jnp
import numpy as np
from jax import lax

C = 256
ATOM_DEV = 2048
CELL_DEV = 8
MOST = 1024
K = 512
ATOMS = 16384
N_DP = 8


def touch_ends(array, rng, low, largest):
    dims = array.shape
    spot = [jax.random.randint(jax.random.fold_in(rng, axis), (), 0, dims[axis]) for axis in range(len(dims))]
    array = array.at[tuple(spot)].set(low)
    longest = dims.index(max(dims))
    spot[longest] = (spot[longest] + 1) % dims[longest]
    return array.at[tuple(spot)].set(largest)


def level_of(key, dims, pieces, least, top_value):
    loudness = 1.0
    for position, shards_of in pieces:
        steps = jax.random.uniform(jax.random.fold_in(jax.random.fold_in(key, 6), position), (shards_of,), jnp.float32, least / len(pieces), top_value / len(pieces))
        loudness = loudness * jnp.repeat(jnp.exp(steps), dims[position] // shards_of).reshape((-1,) + (1,) * (len(dims) - 1 - position))
    return loudness


def split_up(amount, total, bound, slope):
    weights = [(1 << 20) // math.isqrt(standing ** slope) + 1 for standing in range(2, amount + 1)]
    spare, given = total - bound - (amount - 1), [1] * (amount - 1)
    while spare > 0:
        free = [i for i in range(amount - 1) if given[i] < bound]
        pool, budget = sum([weights[i] for i in free]), spare
        for i in free:
            more = min(bound - given[i], max(1, budget * weights[i] // pool), spare)
            given[i] = given[i] + more
            spare = spare - more
    return np.array([bound] + given)


def uneven_parts(rng, number_of, total, most, slope):
    if number_of == 2:
        one = jax.random.randint(rng, (), max(1, total - most), min(most, total - 1) + 1)
        return jnp.stack([one, total - one])
    sizes = jnp.asarray(split_up(number_of, total, most, slope), jnp.int32)
    twos = (number_of - 1) // 2
    source_of, receiver = sizes[1:1 + 2 * twos:2], sizes[2:2 + 2 * twos:2]
    slack = jnp.minimum(source_of - 1, most - receiver)
    passed = jax.random.randint(jax.random.fold_in(rng, 1), (twos,), 0, 1 << 20) % (slack + 1)
    sizes = sizes.at[1:1 + 2 * twos:2].set(source_of - passed).at[2:2 + 2 * twos:2].set(receiver + passed)
    return sizes[jax.random.permutation(jax.random.fold_in(rng, 2), number_of)]


def centred(rng, shape, scale, reach, shards=(), kind=jnp.bfloat16):
    drawn = jax.random.normal(rng, shape, jnp.float32) * scale
    if len(shards) > 0:
        drawn = level_of(rng, shape, shards, -0.22, 0.18) * drawn
    return jnp.clip(drawn, min=-reach, max=reach).astype(kind)


def setup_inputs(seed: int = 0) -> dict:
    key_of = jax.random.split(jax.random.key(seed), 11)
    feats = centred(key_of[0], (ATOMS, C), 1.0, 6.0, ((0, 8),))
    coords = jnp.clip(1.0 * jax.random.uniform(key_of[1], (3, ATOMS), jnp.float32) ** level_of(key_of[1], (3, ATOMS), ((1, 8),), -0.2, 0.2), 0.0, 1.0)
    cell_ids = jax.vmap(lambda own: jnp.searchsorted(jnp.cumsum(uneven_parts(own, CELL_DEV, ATOM_DEV, MOST, 2)), jnp.arange(ATOM_DEV), side="right"))(jax.random.split(key_of[2], N_DP)).reshape((N_DP, ATOM_DEV)).astype(jnp.int32)
    recip = jnp.clip(0.05 + 0.29999999 * jax.random.uniform(key_of[3], (N_DP, CELL_DEV, 9), jnp.float32) ** level_of(key_of[3], (N_DP, CELL_DEV, 9), ((0, 8),), -0.2, 0.2), 0.05, 0.35)
    kvec = touch_ends(jax.random.randint(key_of[4], (3, K), -4, 5), jax.random.fold_in(key_of[4], 1), -4, 4).astype(jnp.int32)
    w_in = centred(key_of[5], (C, C), C ** -0.5, 0.375)
    w_out = centred(key_of[6], (C, C), C ** -0.5, 0.375)
    kfilt = centred(key_of[7], (K, C), 0.5, 3.0, ((0, 4),), jnp.float32)
    spread = jnp.clip(jnp.exp(jax.random.uniform(key_of[8], (C,), jnp.float32, math.log(0.02), math.log(0.5))), 0.02, 0.5)
    cotan = centred(key_of[9], (ATOMS, C), 1.0, 6.0, ((0, 8),))
    return dict(feats=feats, coords=coords, cell_ids=cell_ids, recip=recip, kvec=kvec, w_in=w_in, w_out=w_out, kfilt=kfilt, spread=spread, cotan=cotan)


TWO_PI = 6.283185307179586

def phases(fractional, lattice):
    indices = lattice.astype(jnp.float32)
    phase_angle = fractional[0][:, None] * indices[0][None, :] + fractional[1][:, None] * indices[1][None, :]
    phase_angle = TWO_PI * (phase_angle + fractional[2][:, None] * indices[2][None, :])
    return (jnp.cos(phase_angle).astype(jnp.bfloat16), jnp.sin(phase_angle).astype(jnp.bfloat16))

def envelope(recip_rows, lattice, spread):
    indices = lattice.astype(jnp.float32)
    squared = jnp.zeros((recip_rows.shape[0], indices.shape[1]), jnp.float32)
    for row_index in range(3):
        component = recip_rows[:, 3 * row_index][:, None] * indices[0][None, :]
        component = component + recip_rows[:, 3 * row_index + 1][:, None] * indices[1][None, :]
        component = component + recip_rows[:, 3 * row_index + 2][:, None] * indices[2][None, :]
        squared = squared + component * component
    return jnp.exp(-squared[:, :, None] * spread[None, None, :])

def silu_slope(values):
    sigma = jax.nn.sigmoid(values)
    return sigma * (1.0 + values * (1.0 - sigma))

def padded(table, extra):
    return jnp.concatenate([table, jnp.zeros((extra,) + table.shape[1:], table.dtype)], axis=0)

def cell_layout(cell_rows, cell_total):
    numbers = jnp.arange(cell_total, dtype=jnp.int32)
    counts = lax.optimization_barrier(jnp.sum((cell_rows[None, :] == numbers[:, None]).astype(jnp.int32), axis=1))
    offsets = lax.optimization_barrier(jnp.sum((cell_rows[None, :] < numbers[:, None]).astype(jnp.int32), axis=1))
    return (counts, offsets)

def structure_pass(projected, cosines, sines, cell_rows, filters):
    atom_count = projected.shape[0]
    counts, offsets = cell_layout(cell_rows, filters.shape[0])
    proj_pad = padded(projected, MOST)
    cos_pad = padded(cosines, MOST)
    sin_pad = padded(sines, MOST)
    rows_pad = jnp.concatenate([cell_rows, jnp.full((MOST,), -1, jnp.int32)])
    message = jnp.zeros((atom_count + MOST, projected.shape[1]), jnp.float32)
    real_parts = []
    imag_parts = []
    for cell_index in range(filters.shape[0]):
        offset = offsets[cell_index]
        member = lax.dynamic_slice_in_dim(rows_pad, offset, MOST, 0) == cell_index
        member_half = member.astype(jnp.bfloat16)[:, None]
        cos_rows = lax.dynamic_slice_in_dim(cos_pad, offset, MOST, 0)
        sin_rows = lax.dynamic_slice_in_dim(sin_pad, offset, MOST, 0)
        proj_rows = lax.dynamic_slice_in_dim(proj_pad, offset, MOST, 0)
        real_part = jnp.dot((cos_rows * member_half).T, proj_rows, preferred_element_type=jnp.float32)
        imag_part = jnp.dot((sin_rows * member_half).T, proj_rows, preferred_element_type=jnp.float32)
        scale = 1.0 / counts[cell_index].astype(jnp.float32)
        weight_re = (filters[cell_index] * real_part * scale).astype(jnp.bfloat16)
        weight_im = (filters[cell_index] * imag_part * scale).astype(jnp.bfloat16)
        contrib = jnp.dot(cos_rows, weight_re, preferred_element_type=jnp.float32)
        contrib = contrib + jnp.dot(sin_rows, weight_im, preferred_element_type=jnp.float32)
        contrib = contrib * member.astype(jnp.float32)[:, None]
        previous = lax.dynamic_slice_in_dim(message, offset, MOST, 0)
        message = lax.dynamic_update_slice_in_dim(message, previous + contrib, offset, 0)
        real_parts.append(real_part)
        imag_parts.append(imag_part)
    return (message[:atom_count], real_parts, imag_parts)

def adjoint_pass(message_grad, cosines, sines, cell_rows, filters, shapes, real_parts, imag_parts):
    atom_count = message_grad.shape[0]
    counts, offsets = cell_layout(cell_rows, filters.shape[0])
    grad_pad = padded(message_grad, MOST)
    cos_pad = padded(cosines, MOST)
    sin_pad = padded(sines, MOST)
    rows_pad = jnp.concatenate([cell_rows, jnp.full((MOST,), -1, jnp.int32)])
    update = jnp.zeros((atom_count + MOST, message_grad.shape[1]), jnp.float32)
    filter_grad = jnp.zeros(filters.shape[1:], jnp.float32)
    for cell_index in range(filters.shape[0]):
        offset = offsets[cell_index]
        member = lax.dynamic_slice_in_dim(rows_pad, offset, MOST, 0) == cell_index
        member_half = member.astype(jnp.bfloat16)[:, None]
        cos_rows = lax.dynamic_slice_in_dim(cos_pad, offset, MOST, 0)
        sin_rows = lax.dynamic_slice_in_dim(sin_pad, offset, MOST, 0)
        grad_rows = lax.dynamic_slice_in_dim(grad_pad, offset, MOST, 0)
        scale = 1.0 / counts[cell_index].astype(jnp.float32)
        back_re = jnp.dot((cos_rows * member_half).T, grad_rows, preferred_element_type=jnp.float32) * scale
        back_im = jnp.dot((sin_rows * member_half).T, grad_rows, preferred_element_type=jnp.float32) * scale
        source_re = (filters[cell_index] * back_re).astype(jnp.bfloat16)
        source_im = (filters[cell_index] * back_im).astype(jnp.bfloat16)
        contrib = jnp.dot(cos_rows, source_re, preferred_element_type=jnp.float32)
        contrib = contrib + jnp.dot(sin_rows, source_im, preferred_element_type=jnp.float32)
        contrib = contrib * member.astype(jnp.float32)[:, None]
        previous = lax.dynamic_slice_in_dim(update, offset, MOST, 0)
        update = lax.dynamic_update_slice_in_dim(update, previous + contrib, offset, 0)
        filter_grad = filter_grad + shapes[cell_index] * (real_parts[cell_index] * back_re + imag_parts[cell_index] * back_im)
    return (update[:atom_count], filter_grad)

def reference(feats, coords, cell_ids, recip, kvec, w_in, w_out, kfilt, spread, cotan):
    feat_blocks = feats.reshape(N_DP, ATOM_DEV, C)
    cot_blocks = cotan.reshape(N_DP, ATOM_DEV, C)
    frac_blocks = jnp.transpose(coords.reshape(3, N_DP, ATOM_DEV), (1, 0, 2))

    def one_block(carry, inputs):
        feat_rows, cot_rows, frac_rows, cell_rows, recip_rows = inputs
        projected = jnp.dot(feat_rows, w_in, preferred_element_type=jnp.float32).astype(jnp.bfloat16)
        cosines, sines = phases(frac_rows, kvec)
        shapes = envelope(recip_rows, kvec, spread)
        filters = kfilt[None] * shapes
        message, real_parts, imag_parts = structure_pass(projected, cosines, sines, cell_rows, filters)
        activated = jax.nn.silu(message).astype(jnp.bfloat16)
        mixed = (feat_rows.astype(jnp.float32) + jnp.dot(activated, w_out, preferred_element_type=jnp.float32)).astype(jnp.bfloat16)
        act_grad = jnp.dot(cot_rows, w_out.T, preferred_element_type=jnp.float32)
        message_grad = (act_grad * silu_slope(message)).astype(jnp.bfloat16)
        update, filter_grad = adjoint_pass(message_grad, cosines, sines, cell_rows, filters, shapes, real_parts, imag_parts)
        update = update.astype(jnp.bfloat16)
        feat_grad = (cot_rows.astype(jnp.float32) + jnp.dot(update, w_in.T, preferred_element_type=jnp.float32)).astype(jnp.bfloat16)
        grad_in = carry[0] + jnp.dot(feat_rows.T, update, preferred_element_type=jnp.float32)
        grad_out = carry[1] + jnp.dot(activated.T, cot_rows, preferred_element_type=jnp.float32)
        return ((grad_in, grad_out, carry[2] + filter_grad), (mixed, feat_grad))
    start_carry = (jnp.zeros((C, C), jnp.float32), jnp.zeros((C, C), jnp.float32), jnp.zeros(kfilt.shape, jnp.float32))
    sums, outputs = lax.scan(one_block, start_carry, (feat_blocks, cot_blocks, frac_blocks, cell_ids, recip))
    raw_in, raw_out, raw_kfilt = sums
    mean_weights = (jnp.sum(raw_in * raw_in) + jnp.sum(raw_out * raw_out)) / (2 * C * C)
    mean_filter = jnp.sum(raw_kfilt * raw_kfilt) / (raw_kfilt.shape[0] * C)
    weight_scale = lax.rsqrt(mean_weights + 1e-06)
    filter_scale = lax.rsqrt(mean_filter + 1e-06)
    mixed = outputs[0].reshape(N_DP * ATOM_DEV, C)
    feat_grad = outputs[1].reshape(N_DP * ATOM_DEV, C)
    return (mixed, feat_grad, raw_in * weight_scale, raw_out * weight_scale, raw_kfilt * filter_scale)
```

```python
import functools

import jax
import jax.numpy as jnp
from jax import lax
from jax.experimental import pallas as pl
from jax.experimental.pallas import tpu as pltpu
from jax.sharding import PartitionSpec as P

F32 = jnp.float32
BF16 = jnp.bfloat16
LANES = 128
COS_TERMS = (
    0.9999999890590228,
    -19.73920449945383,
    64.93911745989081,
    -85.45013953079767,
    60.167630950263465,
    -25.967599245923743,
    6.52865815775625,
)
SIN_TERMS = (
    6.283184916495428,
    -41.34158923268831,
    81.59994332977429,
    -76.61447253115396,
    41.34288235413569,
    -12.471243534350362,
)
ROUNDER = 12582912.0


def mm(lhs, rhs, lhs_dim=1, rhs_dim=0):
    return lax.dot_general(
        lhs, rhs, (((lhs_dim,), (rhs_dim,)), ((), ())), preferred_element_type=F32
    )


def horner(terms, square):
    value = terms[-1] * square + terms[-2]
    for term in terms[-3::-1]:
        value = value * square + term
    return value


def partner(me, step, count):
    if count & (count - 1) == 0:
        return me ^ step
    return lax.rem(me + step, count)


def routes(step, count):
    if count & (count - 1) == 0:
        return [(i, i ^ step) for i in range(count)]
    return [(i, (i + step) % count) for i in range(count)]


def tile_of(size, most):
    tile = most
    while size % tile:
        tile //= 2
    return tile


def block_kernel(n_ka, n_dp, *refs):
    bounds, me_ref, feats_hbm, cotan_hbm, coords, ids, recip, spread = refs[:8]
    kvecs = refs[8 : 8 + n_ka]
    kfilts = refs[8 + n_ka : 8 + 2 * n_ka]
    w_in, w_out = refs[8 + 2 * n_ka : 10 + 2 * n_ka]
    mixed_hbm, fgrad_hbm, pieces, own_piece = refs[10 + 2 * n_ka : 14 + 2 * n_ka]
    (
        feats, cotan, kcols, krows, kfilt_t, spread_col, waves, proj_t, mess_t, mgrad_t,
        total, factors, filter_grad, raw_in_t, raw_out, mixed, fgrad, weights, sems,
    ) = refs[14 + 2 * n_ka :]
    atoms, chan = feats.shape
    own = kvecs[0].shape[1]
    k_all = own * n_ka
    cells = recip.shape[0]
    tile = tile_of(atoms, 256)
    tiles = atoms // tile

    feats_in = pltpu.make_async_copy(feats_hbm, feats, sems.at[0])
    feats_in.start()
    cotan_in = pltpu.make_async_copy(cotan_hbm, cotan, sems.at[1])
    cotan_in.start()

    for j in range(n_ka):
        rows = kvecs[j][...].astype(F32)
        rows = jnp.concatenate([rows, jnp.zeros((5, own), F32)], axis=0)
        krows[:, j * own : (j + 1) * own] = rows
        kcols[j * own : (j + 1) * own, :] = rows.T
        kfilt_t[:, j * own : (j + 1) * own] = kfilts[j][...].T
    spread_col[...] = jnp.broadcast_to(spread[...], (8, chan)).T

    wide = tile_of(atoms, 1024)

    def phase_rows(i, carry):
        row = pl.multiple_of(i * 16, 16)
        kv = kcols[pl.ds(row, 16), :]
        for start in range(0, atoms, wide):
            frac = coords[:, start : start + wide]
            turns = kv[:, 0:1] * frac[0:1, :] + kv[:, 1:2] * frac[1:2, :]
            turns = turns + kv[:, 2:3] * frac[2:3, :]
            turns = turns - ((turns + ROUNDER) - ROUNDER)
            square = turns * turns
            waves[pl.ds(row, 16), start : start + wide] = horner(COS_TERMS, square).astype(BF16)
            waves[pl.ds(pl.multiple_of(k_all + row, 16), 16), start : start + wide] = (
                horner(SIN_TERMS, square) * turns
            ).astype(BF16)
        return carry

    lax.fori_loop(0, k_all // 16, phase_rows, 0)

    feats_in.wait()

    def project(t, carry):
        at = pl.ds(pl.multiple_of(t * tile, tile), tile)
        proj_t[:, at] = mm(w_in[...], feats[at, :], 0, 1).astype(BF16)
        return carry

    lax.fori_loop(0, tiles, project, 0)

    lattice = krows[...]

    def shape_of(cell):
        squared = jnp.zeros((1, k_all), F32)
        line = recip[pl.ds(cell, 1), :]
        for r in range(3):
            part = line[:, 3 * r : 3 * r + 1] * lattice[0:1, :]
            part = part + line[:, 3 * r + 1 : 3 * r + 2] * lattice[1:2, :]
            part = part + line[:, 3 * r + 2 : 3 * r + 3] * lattice[2:3, :]
            squared = squared + part * part
        return jnp.exp(-squared * spread_col[:, 0:1])

    def span(cell):
        first = bounds[1, cell]
        count = bounds[0, cell]
        return lax.div(first, tile), lax.div(first + count + (tile - 1), tile), count

    def gather(cell, source):
        low, high, count = span(cell)
        total[...] = jnp.zeros_like(total)

        def step(t, carry):
            at = pl.ds(pl.multiple_of(t * tile, tile), tile)
            member = (ids[:, at] == cell).astype(F32).astype(BF16)
            total[...] += mm(source[:, at] * member, waves[:, at], 1, 1)
            return carry

        lax.fori_loop(low, high, step, 0)
        return low, high, 1.0 / jnp.full((1, 1), count, jnp.int32).astype(F32)

    def spread_back(cell, low, high):
        def step(t, carry):
            at = pl.ds(pl.multiple_of(t * tile, tile), tile)
            member = ids[:, at] == cell
            value = mm(weights[...], waves[:, at])
            mess_t[:, at] = jnp.where(member, value, mess_t[:, at])
            return carry

        lax.fori_loop(low, high, step, 0)

    def forward_cell(cell, carry):
        low, high, scale = gather(cell, proj_t)
        filt = kfilt_t[...] * shape_of(cell)
        real, imag = total[:, :k_all], total[:, k_all:]
        factors[cell] = total[...]
        weights[:, :k_all] = (filt * real * scale).astype(BF16)
        weights[:, k_all:] = (filt * imag * scale).astype(BF16)
        spread_back(cell, low, high)
        return carry

    lax.fori_loop(0, cells, forward_cell, 0)

    cotan_in.wait()
    raw_out[...] = jnp.zeros_like(raw_out)

    def middle(t, carry):
        at = pl.ds(pl.multiple_of(t * tile, tile), tile)
        message = mess_t[:, at]
        sigma = jax.nn.sigmoid(message)
        activated = (message * sigma).astype(BF16)
        cot = cotan[at, :]
        act_grad = mm(w_out[...], cot, 1, 1)
        mgrad_t[:, at] = (act_grad * (sigma * (1.0 + message * (1.0 - sigma)))).astype(BF16)
        raw_out[...] += mm(activated, cot)
        mixed[at, :] = (feats[at, :].astype(F32) + mm(activated.T, w_out[...])).astype(BF16)
        return carry

    lax.fori_loop(0, tiles, middle, 0)
    mixed_out = pltpu.make_async_copy(mixed, mixed_hbm, sems.at[2])
    mixed_out.start()

    filter_grad[...] = jnp.zeros_like(filter_grad)

    def backward_cell(cell, carry):
        low, high, scale = gather(cell, mgrad_t)
        shape = shape_of(cell)
        filt = kfilt_t[...] * shape
        real = total[:, :k_all] * scale
        imag = total[:, k_all:] * scale
        weights[:, :k_all] = (filt * real).astype(BF16)
        weights[:, k_all:] = (filt * imag).astype(BF16)
        filter_grad[...] += shape * (
            factors[cell, :, :k_all] * real + factors[cell, :, k_all:] * imag
        )
        spread_back(cell, low, high)
        return carry

    lax.fori_loop(0, cells, backward_cell, 0)

    raw_in_t[...] = jnp.zeros_like(raw_in_t)

    def last(t, carry):
        at = pl.ds(pl.multiple_of(t * tile, tile), tile)
        update = mess_t[:, at].astype(BF16)
        raw_in_t[...] += mm(update, feats[at, :])
        fgrad[at, :] = (cotan[at, :].astype(F32) + mm(update.T, w_in[...], 1, 1)).astype(BF16)
        return carry

    lax.fori_loop(0, tiles, last, 0)
    fgrad_out = pltpu.make_async_copy(fgrad, fgrad_hbm, sems.at[3])
    fgrad_out.start()

    me = me_ref[0]
    rows = chan // n_dp
    for s in range(n_dp):
        at = pl.ds(pl.multiple_of(partner(me, s, n_dp) * rows, rows), rows)
        dest = own_piece if s == 0 else pieces.at[s - 1]
        dest[:, :chan] = raw_in_t[at, :].astype(dest.dtype)
        dest[:, chan : 2 * chan] = raw_out[at, :].astype(dest.dtype)
        dest[:, 2 * chan :] = filter_grad[at, :].astype(dest.dtype)
    mixed_out.wait()
    fgrad_out.wait()


def block_call(n_ka, n_dp, bounds, me, feats, cotan, coords, ids, recip, spread, kvecs, kfilts, w_in, w_out):
    atoms, chan = feats.shape
    own = kvecs[0].shape[1]
    k_all = own * n_ka
    cells = recip.shape[0]
    rows = chan // n_dp
    width = 2 * chan + k_all
    vmem = pl.BlockSpec(memory_space=pltpu.VMEM)
    smem = pl.BlockSpec(memory_space=pltpu.SMEM)
    hbm = pl.BlockSpec(memory_space=pl.ANY)
    return pl.pallas_call(
        functools.partial(block_kernel, n_ka, n_dp),
        out_shape=(
            jax.ShapeDtypeStruct((atoms, chan), BF16),
            jax.ShapeDtypeStruct((atoms, chan), BF16),
            jax.ShapeDtypeStruct((n_dp - 1, rows, width), BF16),
            jax.ShapeDtypeStruct((rows, width), F32),
        ),
        in_specs=[smem, smem, hbm, hbm] + [vmem] * (6 + 2 * n_ka),
        out_specs=(hbm, hbm, vmem, vmem),
        scratch_shapes=[
            pltpu.VMEM((atoms, chan), BF16),
            pltpu.VMEM((atoms, chan), BF16),
            pltpu.VMEM((k_all, 8), F32),
            pltpu.VMEM((8, k_all), F32),
            pltpu.VMEM((chan, k_all), F32),
            pltpu.VMEM((chan, 8), F32),
            pltpu.VMEM((2 * k_all, atoms), BF16),
            pltpu.VMEM((chan, atoms), BF16),
            pltpu.VMEM((chan, atoms), F32),
            pltpu.VMEM((chan, atoms), BF16),
            pltpu.VMEM((chan, 2 * k_all), F32),
            pltpu.VMEM((cells, chan, 2 * k_all), F32),
            pltpu.VMEM((chan, k_all), F32),
            pltpu.VMEM((chan, chan), F32),
            pltpu.VMEM((chan, chan), F32),
            pltpu.VMEM((atoms, chan), BF16),
            pltpu.VMEM((atoms, chan), BF16),
            pltpu.VMEM((chan, 2 * k_all), BF16),
            pltpu.SemaphoreType.DMA((4,)),
        ],
        name="block",
    )(bounds, me, feats, cotan, coords, ids, recip, spread, *kvecs, *kfilts, w_in, w_out)


def sum_kernel(chan, own, piece, *refs):
    parts, out = refs[:-1], refs[-1]
    value = piece[...]
    for part in parts:
        value = value + part[...].astype(F32)
    weight_part = value[:, : 2 * chan]
    filter_part = value[:, 2 * chan :]
    out[:, : 2 * chan + own] = value[:, : 2 * chan + own]
    weight_squares = jnp.sum(weight_part * weight_part, axis=1, keepdims=True)
    filter_squares = jnp.sum(filter_part * filter_part, axis=1, keepdims=True)
    lane = lax.broadcasted_iota(jnp.int32, (value.shape[0], LANES), 1)
    out[:, 2 * chan + own :] = jnp.where(lane < LANES // 2, weight_squares, filter_squares)


def final_kernel(chan, own, n_ka, n_dp, me_ref, *refs):
    parts = refs[:n_dp]
    g_in, g_out, g_filt, raw_in_t, filt_t = refs[n_dp:]
    me = me_ref[0]
    rows = chan // n_dp
    squares = parts[0][:, 2 * chan + own :]
    for part in parts[1:]:
        squares = squares + part[:, 2 * chan + own :]
    squares = jnp.sum(squares, axis=0, keepdims=True)
    weight_scale = lax.rsqrt(squares[:, 0:1] / (2 * chan * chan) + 1e-06)
    filter_scale = lax.rsqrt(
        squares[:, LANES // 2 : LANES // 2 + 1] / (own * n_ka * chan) + 1e-06
    )
    for s in range(n_dp):
        at = pl.ds(pl.multiple_of(partner(me, s, n_dp) * rows, rows), rows)
        raw_in_t[at, :] = parts[s][:, :chan] * weight_scale
        g_out[at, :] = parts[s][:, chan : 2 * chan] * weight_scale
        filt_t[at, :] = parts[s][:, 2 * chan : 2 * chan + own] * filter_scale
    g_in[...] = raw_in_t[...].T
    g_filt[...] = filt_t[...].T


def body(feats, coords, cell_ids, recip, kvec, w_in, w_out, kfilt, spread, cotan):
    n_ka = lax.axis_size("ka")
    n_dp = lax.axis_size("dp")
    chan = feats.shape[1]
    own = kvec.shape[1]
    kvecs = [kvec] + [lax.ppermute(kvec, "ka", routes(s, n_ka)) for s in range(1, n_ka)]
    kfilts = [kfilt] + [lax.ppermute(kfilt, "ka", routes(s, n_ka)) for s in range(1, n_ka)]
    me = lax.axis_index("dp").astype(jnp.int32).reshape(1)
    numbers = jnp.arange(recip.shape[1], dtype=jnp.int32)[:, None]
    bounds = jnp.stack(
        [
            jnp.sum((cell_ids == numbers).astype(jnp.int32), axis=1),
            jnp.sum((cell_ids < numbers).astype(jnp.int32), axis=1),
        ]
    )
    mixed, feat_grad, pieces, piece = block_call(
        n_ka, n_dp, bounds, me, feats, cotan, coords, cell_ids, recip[0], spread[None], kvecs,
        kfilts, w_in, w_out,
    )
    parts = [lax.ppermute(pieces[s - 1], "dp", routes(s, n_dp)) for s in range(1, n_dp)]
    rows = piece.shape[0]
    summed = pl.pallas_call(
        functools.partial(sum_kernel, chan, own),
        out_shape=jax.ShapeDtypeStruct((rows, 2 * chan + own + LANES), F32),
        name="sum",
    )(piece, *parts)
    shares = [summed] + [lax.ppermute(summed, "dp", routes(s, n_dp)) for s in range(1, n_dp)]
    vmem = pl.BlockSpec(memory_space=pltpu.VMEM)
    grads = pl.pallas_call(
        functools.partial(final_kernel, chan, own, n_ka, n_dp),
        out_shape=(
            jax.ShapeDtypeStruct((chan, chan), F32),
            jax.ShapeDtypeStruct((chan, chan), F32),
            jax.ShapeDtypeStruct((own, chan), F32),
        ),
        in_specs=[pl.BlockSpec(memory_space=pltpu.SMEM)] + [vmem] * n_dp,
        scratch_shapes=[pltpu.VMEM((chan, chan), F32), pltpu.VMEM((chan, own), F32)],
        name="final",
    )(me, *shares)
    return (mixed, feat_grad, *grads)


def solution(mesh):
    placed = (
        P("dp", None),
        P(None, "dp"),
        P("dp", None),
        P("dp", None, None),
        P(None, "ka"),
        P(),
        P(),
        P("ka", None),
        P(),
        P("dp", None),
    )
    return jax.shard_map(
        body,
        mesh=mesh,
        in_specs=placed,
        out_specs=(P("dp", None), P("dp", None), P(), P(), P("ka", None)),
        check_vma=False,
    )
```

```python
import functools

import jax
import jax.numpy as jnp
from jax import lax
from jax.experimental import pallas as pl
from jax.experimental.pallas import tpu as pltpu
from jax.sharding import PartitionSpec as P

F32 = jnp.float32
BF16 = jnp.bfloat16
LANES = 128
TILE = 256
MOST = 1024
LIMIT = 24 << 20
SMALL = 6 << 20
FLOPS_PER_MICRO = 1 << 30
LOG2_E = 1.4426950408889634
COS_TERMS = (
    0.9999999890590228,
    -19.73920449945383,
    64.93911745989081,
    -85.45013953079767,
    60.167630950263465,
    -25.967599245923743,
    6.52865815775625,
)
SIN_TERMS = (
    6.283184916495428,
    -41.34158923268831,
    81.59994332977429,
    -76.61447253115396,
    41.34288235413569,
    -12.471243534350362,
)
ROUNDER = 12582912.0


def mm(lhs, rhs, lhs_dim=1, rhs_dim=0):
    return lax.dot_general(
        lhs, rhs, (((lhs_dim,), (rhs_dim,)), ((), ())), preferred_element_type=F32
    )


def horner(terms, square):
    value = terms[-1] * square + terms[-2]
    for term in terms[-3::-1]:
        value = value * square + term
    return value


def routes(step, count):
    if count & (count - 1) == 0:
        return [(i, i ^ step) for i in range(count)]
    return [(i, (i + step) % count) for i in range(count)]


def tile_of(size, most):
    tile = most
    while size % tile:
        tile //= 2
    return tile


def column_to_lanes(row):
    return jnp.broadcast_to(row, (8, row.shape[1])).T


def span_of(bounds, cell):
    first = bounds[1, cell]
    start = lax.div(first, LANES) * LANES
    count = bounds[0, cell]
    steps = lax.div(first - start + count + (TILE - 1), TILE)
    return pl.multiple_of(start, LANES), steps, count


def most_steps(atoms):
    return -(-(min(MOST, atoms) + LANES - 1) // TILE)


def by_steps(steps, most, action):
    for n in range(1, most + 1):
        pl.when(steps == n)(functools.partial(action, n))


def gather_cell(cell, start, steps, most, ids, source, waves, store):
    def action(n):
        at = pl.ds(start, n * TILE)
        member = (ids[:, at] == cell).astype(F32).astype(BF16)
        store(mm(source[:, at] * member, waves[:, at], 1, 1))

    by_steps(steps, most, action)


def spread_cell(cell, start, steps, most, ids, weights, waves, out):
    def action(n):
        for t in range(n):
            at = pl.ds(pl.multiple_of(start + t * TILE, LANES), TILE)
            value = mm(weights[...], waves[:, at])
            out[:, at] = jnp.where(ids[:, at] == cell, value, out[:, at])

    by_steps(steps, most, action)


def inverse_count(count):
    return 1.0 / jnp.full((1, 1), count, jnp.int32).astype(F32)


def shape_of(cell, quad, width_cols):
    exponent = quad[pl.ds(cell, 1), :] * width_cols[:, 0:1]
    return jnp.exp2(exponent)


def waves_kernel(n_ka, *refs):
    bounds, feats, coords, ids_in, recip, w_in = refs[:6]
    kvecs = refs[6 : 6 + n_ka]
    waves, factors, quad, ids, kcols, proj_t = refs[6 + n_ka :]
    atoms, chan = feats.shape
    own = kvecs[0].shape[1]
    k_all = own * n_ka
    cells = recip.shape[0]

    rows = jnp.concatenate([k[...] for k in kvecs], axis=1).astype(F32)
    rows = jnp.concatenate([rows, jnp.zeros((5, k_all), F32)], axis=0)
    kcols[...] = rows.T
    squared = jnp.zeros((cells, k_all), F32)
    for r in range(3):
        part = recip[:, 3 * r : 3 * r + 1] * rows[0:1, :]
        part = part + recip[:, 3 * r + 1 : 3 * r + 2] * rows[1:2, :]
        part = part + recip[:, 3 * r + 2 : 3 * r + 3] * rows[2:3, :]
        squared = squared + part * part
    quad[...] = squared
    ids[:, :atoms] = ids_in[...]
    ids[:, atoms:] = jnp.full((1, LANES), -1, jnp.int32)
    waves[:, atoms:] = jnp.zeros((2 * k_all, LANES), BF16)
    proj_t[:, atoms:] = jnp.zeros((chan, LANES), BF16)

    wide = tile_of(atoms, 1024)

    def phase_rows(i, carry):
        row = pl.multiple_of(i * 16, 16)
        kv = kcols[pl.ds(row, 16), :]
        for start in range(0, atoms, wide):
            frac = coords[:, start : start + wide]
            turns = kv[:, 0:1] * frac[0:1, :] + kv[:, 1:2] * frac[1:2, :]
            turns = turns + kv[:, 2:3] * frac[2:3, :]
            turns = turns - ((turns + ROUNDER) - ROUNDER)
            square = turns * turns
            waves[pl.ds(row, 16), start : start + wide] = horner(COS_TERMS, square).astype(BF16)
            waves[pl.ds(pl.multiple_of(k_all + row, 16), 16), start : start + wide] = (
                horner(SIN_TERMS, square) * turns
            ).astype(BF16)
        return carry

    lax.fori_loop(0, k_all // 16, phase_rows, 0)

    def project(t, carry):
        at = pl.ds(pl.multiple_of(t * TILE, TILE), TILE)
        proj_t[:, at] = mm(w_in[...], feats[at, :], 0, 1).astype(BF16)
        return carry

    lax.fori_loop(0, atoms // TILE, project, 0)

    def cell_step(cell, carry):
        start, steps, _ = span_of(bounds, cell)

        def store(value):
            factors[cell] = value

        gather_cell(cell, start, steps, most_steps(atoms), ids, proj_t, waves, store)
        return carry

    lax.fori_loop(0, cells, cell_step, 0)


def message_kernel(n_ka, *refs):
    bounds, ids, quad, waves, factors, spread, cotan, w_out = refs[:8]
    kfilts = refs[8 : 8 + n_ka]
    act_t, mgrad_t, raw_out, raw_half, filt_t, width_cols, weights, mess_t = refs[8 + n_ka :]
    atoms, chan = cotan.shape
    own = kfilts[0].shape[0]
    k_all = own * n_ka
    cells = quad.shape[0]
    for j in range(n_ka):
        filt_t[:, j * own : (j + 1) * own] = kfilts[j][...].T
    width_cols[...] = column_to_lanes(spread[...] * (-LOG2_E))

    def cell_step(cell, carry):
        start, steps, count = span_of(bounds, cell)
        filt = filt_t[...] * (shape_of(cell, quad, width_cols) * inverse_count(count))
        weights[:, :k_all] = (filt * factors[cell, :, :k_all]).astype(BF16)
        weights[:, k_all:] = (filt * factors[cell, :, k_all:]).astype(BF16)
        spread_cell(cell, start, steps, most_steps(atoms), ids, weights, waves, mess_t)
        return carry

    lax.fori_loop(0, cells, cell_step, 0)

    mgrad_t[:, atoms:] = jnp.zeros((chan, LANES), BF16)
    raw_out[...] = jnp.zeros_like(raw_out)

    def middle(t, carry):
        at = pl.ds(pl.multiple_of(t * TILE, TILE), TILE)
        message = mess_t[:, at]
        sigma = jax.nn.sigmoid(message)
        activated = (message * sigma).astype(BF16)
        act_t[:, at] = activated
        cot = cotan[at, :]
        act_grad = mm(w_out[...], cot, 1, 1)
        mgrad_t[:, at] = (act_grad * (sigma * (1.0 + message * (1.0 - sigma)))).astype(BF16)
        raw_out[...] += mm(activated, cot)
        return carry

    lax.fori_loop(0, atoms // TILE, middle, 0)
    raw_half[...] = raw_out[...].astype(BF16)


def adjoint_kernel(n_ka, *refs):
    bounds, ids, quad, waves, factors, mgrad_t, spread = refs[:7]
    kfilts = refs[7 : 7 + n_ka]
    weights, filter_grad, filter_half, filt_t, width_cols, total, grad_t = refs[7 + n_ka :]
    chan = mgrad_t.shape[0]
    atoms = mgrad_t.shape[1] - LANES
    own = kfilts[0].shape[0]
    k_all = own * n_ka
    cells = quad.shape[0]
    for j in range(n_ka):
        filt_t[:, j * own : (j + 1) * own] = kfilts[j][...].T
    width_cols[...] = column_to_lanes(spread[...] * (-LOG2_E))
    grad_t[...] = jnp.zeros_like(grad_t)

    def cell_step(cell, carry):
        start, steps, count = span_of(bounds, cell)

        def store(value):
            total[...] = value

        gather_cell(cell, start, steps, most_steps(atoms), ids, mgrad_t, waves, store)
        scaled = shape_of(cell, quad, width_cols) * inverse_count(count)
        filt = filt_t[...] * scaled
        weights[cell, :, :k_all] = (filt * total[:, :k_all]).astype(BF16)
        weights[cell, :, k_all:] = (filt * total[:, k_all:]).astype(BF16)
        grad_t[...] += scaled[:, :own] * (
            factors[cell, :, :own] * total[:, :own]
            + factors[cell, :, k_all : k_all + own] * total[:, k_all : k_all + own]
        )
        return carry

    lax.fori_loop(0, cells, cell_step, 0)
    result = grad_t[...].T
    filter_grad[...] = result
    filter_half[...] = result.astype(BF16)


def update_kernel(bounds, ids, waves, weights, feats, update_t, raw_in_t, total_t):
    cells, chan, _ = weights.shape
    atoms = feats.shape[0]

    def cell_step(cell, carry):
        start, steps, _ = span_of(bounds, cell)
        spread_cell(
            cell, start, steps, most_steps(atoms), ids, weights.at[cell], waves, total_t
        )
        return carry

    lax.fori_loop(0, cells, cell_step, 0)
    raw_in_t[...] = jnp.zeros_like(raw_in_t)

    def last(t, carry):
        at = pl.ds(pl.multiple_of(t * TILE, TILE), TILE)
        update = total_t[:, at].astype(BF16)
        update_t[:, at] = update
        raw_in_t[...] += mm(update, feats[at, :])
        return carry

    lax.fori_loop(0, atoms // TILE, last, 0)


def residual_kernel(transposed, base, values_t, weight, out):
    rows = base.shape[0]

    def step(t, carry):
        at = pl.ds(pl.multiple_of(t * TILE, TILE), TILE)
        value = mm(values_t[:, at].T, weight[...], 1, 1 if transposed else 0)
        out[at, :] = (base[at, :].astype(F32) + value).astype(BF16)
        return carry

    lax.fori_loop(0, rows // TILE, step, 0)


def chip_kernel(raw_in_t, other_in, out_sum, out_near, filt_sum, filt_near, in_sum, in_half, w_sum, f_sum, f_squares):
    value = raw_in_t[...] + other_in[...]
    in_sum[...] = value
    in_half[...] = value.astype(BF16)
    w_sum[...] = out_sum[...] + out_near[...]
    filt = filt_sum[...] + filt_near[...]
    f_sum[...] = filt
    f_squares[...] = jnp.broadcast_to(
        jnp.sum(jnp.sum(filt * filt, axis=0, keepdims=True), axis=1, keepdims=True),
        f_squares.shape,
    )


def total_of(first, others):
    value = first[...]
    for other in others:
        value = value + other[...].astype(F32)
    return value


def add_kernel(*refs):
    refs[-1][...] = total_of(refs[0], refs[1:-1])


def final_kernel(n_chip, n_ka, *refs):
    in_parts = refs[:n_chip]
    raw_out, filt = refs[n_chip : n_chip + 2]
    squares = refs[n_chip + 2 : n_chip + 2 + n_ka]
    g_in, g_out, g_filt = refs[n_chip + 2 + n_ka :]
    raw_in = total_of(in_parts[0], in_parts[1:])
    out = raw_out[...]
    both = raw_in * raw_in + out * out
    weight_squares = jnp.sum(jnp.sum(both, axis=0, keepdims=True), axis=1, keepdims=True)
    weight_scale = lax.rsqrt(weight_squares / (2 * raw_in.size) + 1e-06)
    filter_squares = total_of(squares[0], squares[1:])[0:1, 0:1]
    filter_scale = lax.rsqrt(filter_squares / (n_ka * filt.size) + 1e-06)
    g_in[...] = (raw_in * weight_scale).T
    g_out[...] = out * weight_scale
    g_filt[...] = filt[...] * filter_scale


def call(kernel, name, operands, smem, outs, scratch=(), limit=SMALL, micros=2):
    vmem = pl.BlockSpec(memory_space=pltpu.VMEM)
    return pl.pallas_call(
        kernel,
        out_shape=tuple(jax.ShapeDtypeStruct(*o) for o in outs),
        in_specs=[pl.BlockSpec(memory_space=pltpu.SMEM)] * smem + [vmem] * (len(operands) - smem),
        out_specs=tuple(vmem for _ in outs),
        scratch_shapes=list(scratch),
        compiler_params=pltpu.CompilerParams(vmem_limit_bytes=limit),
        cost_estimate=pl.CostEstimate(
            flops=micros * FLOPS_PER_MICRO, bytes_accessed=0, transcendentals=0
        ),
        name=name,
    )(*operands)


def body(feats, coords, cell_ids, recip, kvec, w_in, w_out, kfilt, spread, cotan):
    n_ka = lax.axis_size("ka")
    n_dp = lax.axis_size("dp")
    atoms, chan = feats.shape
    own = kvec.shape[1]
    k_all = own * n_ka
    cells = recip.shape[1]
    long = atoms + LANES
    recip, spread = recip[0], spread[None]
    kvecs = [kvec] + [lax.ppermute(kvec, "ka", routes(s, n_ka)) for s in range(1, n_ka)]
    kfilts = [kfilt] + [lax.ppermute(kfilt, "ka", routes(s, n_ka)) for s in range(1, n_ka)]
    numbers = jnp.arange(cells, dtype=jnp.int32)[:, None]
    bounds = jnp.stack(
        [
            jnp.sum((cell_ids == numbers).astype(jnp.int32), axis=1),
            jnp.sum((cell_ids < numbers).astype(jnp.int32), axis=1),
        ]
    )
    vm = pltpu.VMEM
    waves, factors, quad, ids = call(
        functools.partial(waves_kernel, n_ka),
        "waves",
        (bounds, feats, coords, cell_ids, recip, w_in, *kvecs),
        1,
        [((2 * k_all, long), BF16), ((cells, chan, 2 * k_all), F32), ((cells, k_all), F32), ((1, long), jnp.int32)],
        [vm((k_all, 8), F32), vm((chan, long), BF16)],
        LIMIT,
        8,
    )
    act_t, mgrad_t, raw_out, raw_half = call(
        functools.partial(message_kernel, n_ka),
        "message",
        (bounds, ids, quad, waves, factors, spread, cotan, w_out, *kfilts),
        1,
        [((chan, atoms), BF16), ((chan, long), BF16), ((chan, chan), F32), ((chan, chan), BF16)],
        [vm((chan, k_all), F32), vm((chan, 8), F32), vm((chan, 2 * k_all), BF16), vm((chan, long), F32)],
        LIMIT,
        8,
    )
    chips = [2 * s for s in range(1, n_dp // 2)]
    out_parts = [lax.ppermute(raw_half, "dp", routes(s, n_dp)) for s in chips]
    weights, filter_grad, filter_half = call(
        functools.partial(adjoint_kernel, n_ka),
        "adjoint",
        (bounds, ids, quad, waves, factors, mgrad_t, spread, *kfilts),
        1,
        [((cells, chan, 2 * k_all), BF16), ((own, chan), F32), ((own, chan), BF16)],
        [vm((chan, k_all), F32), vm((chan, 8), F32), vm((chan, 2 * k_all), F32), vm((chan, own), F32)],
        LIMIT,
        8,
    )
    filt_parts = [lax.ppermute(filter_half, "dp", routes(s, n_dp)) for s in chips]
    (out_sum,) = call(add_kernel, "outsum", (raw_out, *out_parts), 0, [((chan, chan), F32)])
    out_near = lax.ppermute(out_sum, "dp", routes(1, n_dp))
    update_t, raw_in_t = call(
        update_kernel,
        "update",
        (bounds, ids, waves, weights, feats),
        1,
        [((chan, atoms), BF16), ((chan, chan), F32)],
        [vm((chan, long), F32)],
        LIMIT,
        8,
    )
    other_in = lax.ppermute(raw_in_t, "dp", routes(1, n_dp))
    (filt_sum,) = call(add_kernel, "filtsum", (filter_grad, *filt_parts), 0, [((own, chan), F32)])
    filt_near = lax.ppermute(filt_sum, "dp", routes(1, n_dp))
    (feat_grad,) = call(
        functools.partial(residual_kernel, True), "featgrad", (cotan, update_t, w_in), 0,
        [((atoms, chan), BF16)],
    )
    in_sum, in_half, w_sum, f_sum, f_squares = call(
        chip_kernel,
        "chip",
        (raw_in_t, other_in, out_sum, out_near, filt_sum, filt_near),
        0,
        [((chan, chan), F32), ((chan, chan), BF16), ((chan, chan), F32), ((own, chan), F32), ((8, LANES), F32)],
    )
    squares = [f_squares] + [lax.ppermute(f_squares, "ka", routes(s, n_ka)) for s in range(1, n_ka)]
    in_parts = [in_sum] + [lax.ppermute(in_half, "dp", routes(s, n_dp)) for s in chips]
    (mixed,) = call(
        functools.partial(residual_kernel, False), "mixed", (feats, act_t, w_out), 0,
        [((atoms, chan), BF16)],
    )
    grads = call(
        functools.partial(final_kernel, len(in_parts), n_ka),
        "final",
        (*in_parts, w_sum, f_sum, *squares),
        0,
        [((chan, chan), F32), ((chan, chan), F32), ((own, chan), F32)],
    )
    return (mixed, feat_grad, *grads)


def solution(mesh):
    placed = (
        P("dp", None),
        P(None, "dp"),
        P("dp", None),
        P("dp", None, None),
        P(None, "ka"),
        P(),
        P(),
        P("ka", None),
        P(),
        P("dp", None),
    )
    return jax.shard_map(
        body,
        mesh=mesh,
        in_specs=placed,
        out_specs=(P("dp", None), P("dp", None), P(), P(), P("ka", None)),
        check_vma=False,
    )
```

```python
import functools

import jax
import jax.numpy as jnp
from jax import lax
from jax.experimental import pallas as pl
from jax.experimental.pallas import tpu as pltpu
from jax.sharding import PartitionSpec as P


F32 = jnp.float32
BF16 = jnp.bfloat16
LANES = 128
TILE = 256
MOST = 1024
LIMIT = 24 << 20
SMALL = 6 << 20
PREPARE = 16 << 20
FLOPS_PER_MICRO = 1 << 30
LOG2_E = 1.4426950408889634
COS_TERMS = (
    0.9999999890590228,
    -19.73920449945383,
    64.93911745989081,
    -85.45013953079767,
    60.167630950263465,
    -25.967599245923743,
    6.52865815775625,
)
SIN_TERMS = (
    6.283184916495428,
    -41.34158923268831,
    81.59994332977429,
    -76.61447253115396,
    41.34288235413569,
    -12.471243534350362,
)
ROUNDER = 12582912.0


def mm(lhs, rhs, lhs_dim=1, rhs_dim=0):
    return lax.dot_general(
        lhs, rhs, (((lhs_dim,), (rhs_dim,)), ((), ())), preferred_element_type=F32
    )


def horner(terms, square):
    value = terms[-1] * square + terms[-2]
    for term in terms[-3::-1]:
        value = value * square + term
    return value


def routes(step, count):
    if count & (count - 1) == 0:
        return [(i, i ^ step) for i in range(count)]
    return [(i, (i + step) % count) for i in range(count)]


def tile_of(size, most):
    tile = most
    while size % tile:
        tile //= 2
    return tile


def column_to_lanes(row):
    return jnp.broadcast_to(row, (8, row.shape[1])).T


def span_of(bounds, cell):
    first = bounds[1, cell]
    start = lax.div(first, LANES) * LANES
    count = bounds[0, cell]
    steps = lax.div(first - start + count + (TILE - 1), TILE)
    return pl.multiple_of(start, LANES), steps, count


def most_steps(atoms):
    return -(-(min(MOST, atoms) + LANES - 1) // TILE)


def by_steps(steps, most, action):
    for n in range(1, most + 1):
        pl.when(steps == n)(functools.partial(action, n))


def gather_cell(cell, start, steps, most, ids, source, waves, store):
    def action(n):
        at = pl.ds(start, n * TILE)
        member = (ids[:, at] == cell).astype(F32).astype(BF16)
        store(mm(source[:, at] * member, waves[:, at], 1, 1))

    by_steps(steps, most, action)


def spread_cell(cell, start, steps, most, ids, weights, waves, out):
    def action(n):
        for t in range(n):
            at = pl.ds(pl.multiple_of(start + t * TILE, LANES), TILE)
            value = mm(weights[...], waves[:, at])
            out[:, at] = jnp.where(ids[:, at] == cell, value, out[:, at])

    by_steps(steps, most, action)


def inverse_count(count):
    return 1.0 / jnp.full((1, 1), count, jnp.int32).astype(F32)


def shape_of(cell, quad, width_cols, first, size):
    exponent = quad[pl.ds(cell, 1), :][:, first : first + size] * width_cols[:, 0:1]
    return jnp.exp2(exponent)


def fill_waves(waves, base, kcols, coords):
    own = kcols.shape[0]
    atoms = coords.shape[1]
    wide = tile_of(atoms, 1024)

    def phase_rows(i, carry):
        row = pl.multiple_of(i * 16, 16)
        kv = kcols[pl.ds(row, 16), :]
        for start in range(0, atoms, wide):
            frac = coords[:, start : start + wide]
            turns = kv[:, 0:1] * frac[0:1, :] + kv[:, 1:2] * frac[1:2, :]
            turns = turns + kv[:, 2:3] * frac[2:3, :]
            turns = turns - ((turns + ROUNDER) - ROUNDER)
            square = turns * turns
            waves[pl.ds(pl.multiple_of(base + row, 16), 16), start : start + wide] = horner(
                COS_TERMS, square
            ).astype(BF16)
            waves[pl.ds(pl.multiple_of(base + own + row, 16), 16), start : start + wide] = (
                horner(SIN_TERMS, square) * turns
            ).astype(BF16)
        return carry

    lax.fori_loop(0, own // 16, phase_rows, 0)


def vector_columns(kvec):
    rows = kvec[...].astype(F32)
    return jnp.concatenate([rows, jnp.zeros((5, rows.shape[1]), F32)], axis=0).T


def prepare_kernel(
    feats_hbm, coords_hbm, ids_hbm, recip_hbm, kvec_hbm, w_in_hbm,
    waves, proj_t, ids, coords, recip, kvec, feats, w_in, kcols, sems,
):
    atoms, chan = feats.shape
    moves = (
        (kvec_hbm, kvec),
        (coords_hbm, coords),
        (w_in_hbm, w_in),
        (feats_hbm, feats),
        (ids_hbm, ids.at[:, :atoms]),
        (recip_hbm, recip),
    )
    copies = [pltpu.make_async_copy(a, b, sems.at[i]) for i, (a, b) in enumerate(moves)]
    for copy in copies:
        copy.start()
    ids[:, atoms:] = jnp.full((1, LANES), -1, jnp.int32)
    waves[:, atoms:] = jnp.zeros((waves.shape[0], LANES), BF16)
    proj_t[:, atoms:] = jnp.zeros((chan, LANES), BF16)
    copies[0].wait()
    copies[1].wait()
    kcols[...] = vector_columns(kvec)
    fill_waves(waves, 0, kcols, coords)
    copies[2].wait()
    copies[3].wait()

    def project(t, carry):
        at = pl.ds(pl.multiple_of(t * TILE, TILE), TILE)
        proj_t[:, at] = mm(w_in[...], feats[at, :], 0, 1).astype(BF16)
        return carry

    lax.fori_loop(0, atoms // TILE, project, 0)
    copies[4].wait()
    copies[5].wait()


def waves_kernel(n_ka, *refs):
    bounds, own_waves, proj_t, ids, coords, recip = refs[:6]
    kvecs = refs[6 : 6 + n_ka]
    waves, factors, quad, kcols = refs[6 + n_ka :]
    atoms = coords.shape[1]
    own = kvecs[0].shape[1]
    cells = recip.shape[0]
    waves[: 2 * own, :] = own_waves[...]
    waves[2 * own :, atoms:] = jnp.zeros((2 * own * (n_ka - 1), LANES), BF16)
    for j in range(1, n_ka):
        kcols[...] = vector_columns(kvecs[j])
        fill_waves(waves, 2 * own * j, kcols, coords)
    for j in range(n_ka):
        rows = kvecs[j][...].astype(F32)
        squared = jnp.zeros((cells, own), F32)
        for r in range(3):
            part = recip[:, 3 * r : 3 * r + 1] * rows[0:1, :]
            part = part + recip[:, 3 * r + 1 : 3 * r + 2] * rows[1:2, :]
            part = part + recip[:, 3 * r + 2 : 3 * r + 3] * rows[2:3, :]
            squared = squared + part * part
        quad[:, own * j : own * (j + 1)] = squared

    def cell_step(cell, carry):
        start, steps, _ = span_of(bounds, cell)

        def store(value):
            factors[cell] = value

        gather_cell(cell, start, steps, most_steps(atoms), ids, proj_t, waves, store)
        return carry

    lax.fori_loop(0, cells, cell_step, 0)


def message_kernel(n_ka, *refs):
    bounds, ids, quad, waves, factors, spread, cotan, w_out = refs[:8]
    kfilts = refs[8 : 8 + n_ka]
    act_t, mgrad_t, raw_out, raw_half, filt_t, width_cols, weights, mess_t = refs[8 + n_ka :]
    atoms, chan = cotan.shape
    own = kfilts[0].shape[0]
    cells = quad.shape[0]
    for j in range(n_ka):
        filt_t[:, j * own : (j + 1) * own] = kfilts[j][...].T
    width_cols[...] = column_to_lanes(spread[...] * (-LOG2_E))

    def cell_step(cell, carry):
        start, steps, count = span_of(bounds, cell)
        inverse = inverse_count(count)
        for j in range(n_ka):
            scaled = shape_of(cell, quad, width_cols, j * own, own) * inverse
            filt = filt_t[:, own * j : own * (j + 1)] * scaled
            for at in (slice(2 * own * j, own * (2 * j + 1)), slice(own * (2 * j + 1), 2 * own * (j + 1))):
                weights[:, at] = (filt * factors[cell, :, at]).astype(BF16)
        spread_cell(cell, start, steps, most_steps(atoms), ids, weights, waves, mess_t)
        return carry

    lax.fori_loop(0, cells, cell_step, 0)

    mgrad_t[:, atoms:] = jnp.zeros((chan, LANES), BF16)
    raw_out[...] = jnp.zeros_like(raw_out)

    def middle(t, carry):
        at = pl.ds(pl.multiple_of(t * TILE, TILE), TILE)
        message = mess_t[:, at]
        sigma = jax.nn.sigmoid(message)
        activated = (message * sigma).astype(BF16)
        act_t[:, at] = activated
        cot = cotan[at, :]
        act_grad = mm(w_out[...], cot, 1, 1)
        mgrad_t[:, at] = (act_grad * (sigma * (1.0 + message * (1.0 - sigma)))).astype(BF16)
        raw_out[...] += mm(activated, cot)
        return carry

    lax.fori_loop(0, atoms // TILE, middle, 0)
    raw_half[...] = raw_out[...].astype(BF16)


def adjoint_kernel(n_ka, *refs):
    bounds, ids, quad, waves, factors, mgrad_t, spread = refs[:7]
    kfilts = refs[7 : 7 + n_ka]
    weights, filter_grad, filter_half, filt_t, width_cols, total, grad_t = refs[7 + n_ka :]
    atoms = mgrad_t.shape[1] - LANES
    own = kfilts[0].shape[0]
    cells = quad.shape[0]
    for j in range(n_ka):
        filt_t[:, j * own : (j + 1) * own] = kfilts[j][...].T
    width_cols[...] = column_to_lanes(spread[...] * (-LOG2_E))
    grad_t[...] = jnp.zeros_like(grad_t)

    def cell_step(cell, carry):
        start, steps, count = span_of(bounds, cell)

        def store(value):
            total[...] = value

        gather_cell(cell, start, steps, most_steps(atoms), ids, mgrad_t, waves, store)
        inverse = inverse_count(count)
        for j in range(n_ka):
            scaled = shape_of(cell, quad, width_cols, j * own, own) * inverse
            filt = filt_t[:, own * j : own * (j + 1)] * scaled
            real = slice(2 * own * j, own * (2 * j + 1))
            imag = slice(own * (2 * j + 1), 2 * own * (j + 1))
            weights[cell, :, real] = (filt * total[:, real]).astype(BF16)
            weights[cell, :, imag] = (filt * total[:, imag]).astype(BF16)
            if j == 0:
                grad_t[...] += scaled * (
                    factors[cell, :, real] * total[:, real] + factors[cell, :, imag] * total[:, imag]
                )
        return carry

    lax.fori_loop(0, cells, cell_step, 0)
    result = grad_t[...].T
    filter_grad[...] = result
    filter_half[...] = result.astype(BF16)


def update_kernel(bounds, ids, waves, weights, feats, update_t, raw_in_t, total_t):
    cells, _, _ = weights.shape
    atoms = feats.shape[0]

    def cell_step(cell, carry):
        start, steps, _ = span_of(bounds, cell)
        spread_cell(
            cell, start, steps, most_steps(atoms), ids, weights.at[cell], waves, total_t
        )
        return carry

    lax.fori_loop(0, cells, cell_step, 0)
    raw_in_t[...] = jnp.zeros_like(raw_in_t)

    def last(t, carry):
        at = pl.ds(pl.multiple_of(t * TILE, TILE), TILE)
        update = total_t[:, at].astype(BF16)
        update_t[:, at] = update
        raw_in_t[...] += mm(update, feats[at, :])
        return carry

    lax.fori_loop(0, atoms // TILE, last, 0)


def residual_kernel(transposed, base, values_t, weight, out):
    value = mm(values_t[...].T, weight[...], 1, 1 if transposed else 0)
    out[...] = (base[...].astype(F32) + value).astype(BF16)


def residual(transposed, base, values_t, weight):
    rows, chan = base.shape
    step = tile_of(rows, 512)
    by_rows = pl.BlockSpec((step, chan), lambda i: (i, 0))
    return pl.pallas_call(
        functools.partial(residual_kernel, transposed),
        out_shape=jax.ShapeDtypeStruct((rows, chan), BF16),
        grid=(rows // step,),
        in_specs=[
            by_rows,
            pl.BlockSpec((chan, step), lambda i: (0, i)),
            pl.BlockSpec((chan, chan), lambda i: (0, 0)),
        ],
        out_specs=by_rows,
        compiler_params=pltpu.CompilerParams(vmem_limit_bytes=SMALL),
        cost_estimate=pl.CostEstimate(
            flops=2 * FLOPS_PER_MICRO, bytes_accessed=0, transcendentals=0
        ),
    )(base, values_t, weight)


def join_kernel(raw_in_t, filt, *refs):
    pack = refs[-1]
    chan = raw_in_t.shape[0]
    pack[:chan, :] = raw_in_t[...]
    pack[chan:, :] = total_of(filt, refs[:-1])


def chip_kernel(pack, near, out_sum, out_near, in_sum, in_half, w_sum, f_sum, f_squares):
    chan = out_sum.shape[0]
    value = pack[:chan, :] + near[:chan, :]
    in_sum[...] = value
    in_half[...] = value.astype(BF16)
    w_sum[...] = out_sum[...] + out_near[...]
    filt = pack[chan:, :] + near[chan:, :]
    f_sum[...] = filt
    f_squares[...] = jnp.broadcast_to(
        jnp.sum(jnp.sum(filt * filt, axis=0, keepdims=True), axis=1, keepdims=True),
        f_squares.shape,
    )


def total_of(first, others):
    value = first[...]
    for other in others:
        value = value + other[...].astype(F32)
    return value


def add_kernel(*refs):
    refs[-1][...] = total_of(refs[0], refs[1:-1])


def final_kernel(n_chip, n_ka, *refs):
    in_parts = refs[:n_chip]
    raw_out, filt = refs[n_chip : n_chip + 2]
    squares = refs[n_chip + 2 : n_chip + 2 + n_ka]
    g_in, g_out, g_filt = refs[n_chip + 2 + n_ka :]
    raw_in = total_of(in_parts[0], in_parts[1:])
    out = raw_out[...]
    both = raw_in * raw_in + out * out
    weight_squares = jnp.sum(jnp.sum(both, axis=0, keepdims=True), axis=1, keepdims=True)
    weight_scale = lax.rsqrt(weight_squares / (2 * raw_in.size) + 1e-06)
    filter_squares = total_of(squares[0], squares[1:])[0:1, 0:1]
    filter_scale = lax.rsqrt(filter_squares / (n_ka * filt.size) + 1e-06)
    g_in[...] = (raw_in * weight_scale).T
    g_out[...] = out * weight_scale
    g_filt[...] = filt[...] * filter_scale


def call(kernel, operands, smem, outs, scratch=(), limit=SMALL, micros=2, space=pltpu.VMEM):
    vmem = pl.BlockSpec(memory_space=pltpu.VMEM)
    return pl.pallas_call(
        kernel,
        out_shape=tuple(jax.ShapeDtypeStruct(*o) for o in outs),
        in_specs=[pl.BlockSpec(memory_space=pltpu.SMEM)] * smem + [pl.BlockSpec(memory_space=space)] * (len(operands) - smem),
        out_specs=tuple(vmem for _ in outs),
        scratch_shapes=list(scratch),
        compiler_params=pltpu.CompilerParams(vmem_limit_bytes=limit),
        cost_estimate=pl.CostEstimate(
            flops=micros * FLOPS_PER_MICRO, bytes_accessed=0, transcendentals=0
        ),
    )(*operands)


def send(value, axis, step):
    return lax.ppermute(value, axis, routes(step, lax.axis_size(axis)))


def block(feats, coords, cell_ids, recip, kvec, w_in, w_out, kfilt, spread, cotan):
    n_ka = lax.axis_size("ka")
    n_dp = lax.axis_size("dp")
    atoms, chan = feats.shape
    own = kvec.shape[1]
    k_all = own * n_ka
    cells = recip.shape[1]
    long = atoms + LANES
    recip, spread = recip[0], spread[None]
    others = range(1, n_ka)
    chips = range(2, n_dp, 2)
    vm = pltpu.VMEM
    kvecs = [send(kvec, "ka", s) for s in others]
    kfilts = [kfilt] + [send(kfilt, "ka", s) for s in others]
    numbers = jnp.arange(cells, dtype=jnp.int32)[:, None]
    bounds = jnp.stack(
        [
            jnp.sum((cell_ids == numbers).astype(jnp.int32), axis=1),
            jnp.sum((cell_ids < numbers).astype(jnp.int32), axis=1),
        ]
    )
    held = [
        pltpu.with_memory_space_constraint(x, pltpu.HBM)
        for x in (feats, coords, cell_ids, recip, kvec, w_in)
    ]
    waves, proj_t, ids, coords, recip, kvec = call(
        prepare_kernel,
        held,
        0,
        [
            ((2 * own, long), BF16),
            ((chan, long), BF16),
            ((1, long), jnp.int32),
            (coords.shape, F32),
            (recip.shape, F32),
            (kvec.shape, jnp.int32),
        ],
        [
            vm((atoms, chan), BF16),
            vm((chan, chan), BF16),
            vm((own, 8), F32),
            pltpu.SemaphoreType.DMA((6,)),
        ],
        PREPARE,
        4,
        pltpu.HBM,
    )
    waves, factors, quad = call(
        functools.partial(waves_kernel, n_ka),
        (bounds, waves, proj_t, ids, coords, recip, kvec, *kvecs),
        1,
        [((2 * k_all, long), BF16), ((cells, chan, 2 * k_all), F32), ((cells, k_all), F32)],
        [vm((own, 8), F32)],
        LIMIT,
        8,
    )
    act_t, mgrad_t, raw_out, raw_half = call(
        functools.partial(message_kernel, n_ka),
        (bounds, ids, quad, waves, factors, spread, cotan, w_out, *kfilts),
        1,
        [((chan, atoms), BF16), ((chan, long), BF16), ((chan, chan), F32), ((chan, chan), BF16)],
        [vm((chan, k_all), F32), vm((chan, 8), F32), vm((chan, 2 * k_all), BF16), vm((chan, long), F32)],
        LIMIT,
        8,
    )
    out_parts = [send(raw_half, "dp", s) for s in chips]
    weights, filter_grad, filter_half = call(
        functools.partial(adjoint_kernel, n_ka),
        (bounds, ids, quad, waves, factors, mgrad_t, spread, *kfilts),
        1,
        [((cells, chan, 2 * k_all), BF16), ((own, chan), F32), ((own, chan), BF16)],
        [vm((chan, k_all), F32), vm((chan, 8), F32), vm((chan, 2 * k_all), F32), vm((chan, own), F32)],
        LIMIT,
        8,
    )
    filt_parts = [send(filter_half, "dp", s) for s in chips]
    (out_sum,) = call(add_kernel, (raw_out, *out_parts), 0, [((chan, chan), F32)])
    out_near = send(out_sum, "dp", 1)
    update_t, raw_in_t = call(
        update_kernel,
        (bounds, ids, waves, weights, feats),
        1,
        [((chan, atoms), BF16), ((chan, chan), F32)],
        [vm((chan, long), F32)],
        LIMIT,
        8,
    )
    (pack,) = call(
        join_kernel, (raw_in_t, filter_grad, *filt_parts), 0, [((chan + own, chan), F32)]
    )
    near = send(pack, "dp", 1)
    feat_grad = residual(True, cotan, update_t, w_in)
    in_sum, in_half, w_sum, f_sum, f_squares = call(
        chip_kernel,
        (pack, near, out_sum, out_near),
        0,
        [
            ((chan, chan), F32),
            ((chan, chan), BF16),
            ((chan, chan), F32),
            ((own, chan), F32),
            ((8, LANES), F32),
        ],
    )
    squares = [f_squares] + [send(f_squares, "ka", s) for s in others]
    in_parts = [in_sum] + [send(in_half, "dp", s) for s in chips]
    mixed = residual(False, feats, act_t, w_out)
    grads = call(
        functools.partial(final_kernel, len(in_parts), n_ka),
        (*in_parts, w_sum, f_sum, *squares),
        0,
        [((chan, chan), F32), ((chan, chan), F32), ((own, chan), F32)],
    )
    return (mixed, feat_grad, *grads)


def solution(mesh):
    placed = (
        P("dp", None),
        P(None, "dp"),
        P("dp", None),
        P("dp", None, None),
        P(None, "ka"),
        P(),
        P(),
        P("ka", None),
        P(),
        P("dp", None),
    )
    return jax.shard_map(
        block,
        mesh=mesh,
        in_specs=placed,
        out_specs=(P("dp", None), P("dp", None), P(), P(), P("ka", None)),
        check_vma=False,
    )
```

```python
import functools

import jax
import jax.numpy as jnp
from jax import lax
from jax.experimental import pallas as pl
from jax.experimental.pallas import tpu as pltpu
from jax.sharding import PartitionSpec as P


F32 = jnp.float32
BF16 = jnp.bfloat16
LANES = 128
TILE = 256
MOST = 1024
LIMIT = 24 << 20
SMALL = 6 << 20
FLOPS_PER_MICRO = 1 << 30
LOG2_E = 1.4426950408889634
COS_TERMS = (
    0.9999999890590228,
    -19.73920449945383,
    64.93911745989081,
    -85.45013953079767,
    60.167630950263465,
    -25.967599245923743,
    6.52865815775625,
)
SIN_TERMS = (
    6.283184916495428,
    -41.34158923268831,
    81.59994332977429,
    -76.61447253115396,
    41.34288235413569,
    -12.471243534350362,
)
ROUNDER = 12582912.0


def mm(lhs, rhs, lhs_dim=1, rhs_dim=0):
    return lax.dot_general(
        lhs, rhs, (((lhs_dim,), (rhs_dim,)), ((), ())), preferred_element_type=F32
    )


def horner(terms, square):
    value = terms[-1] * square + terms[-2]
    for term in terms[-3::-1]:
        value = value * square + term
    return value


def routes(step, count):
    if count & (count - 1) == 0:
        return [(i, i ^ step) for i in range(count)]
    return [(i, (i + step) % count) for i in range(count)]


def tile_of(size, most):
    tile = most
    while size % tile:
        tile //= 2
    return tile


def column_to_lanes(row):
    return jnp.broadcast_to(row, (8, row.shape[1])).T


def span_of(bounds, cell):
    first = bounds[1, cell]
    start = lax.div(first, LANES) * LANES
    count = bounds[0, cell]
    steps = lax.div(first - start + count + (TILE - 1), TILE)
    return pl.multiple_of(start, LANES), steps, count


def most_steps(atoms):
    return -(-(min(MOST, atoms) + LANES - 1) // TILE)


def by_steps(steps, most, action):
    for n in range(1, most + 1):
        pl.when(steps == n)(functools.partial(action, n))


def gather_cell(cell, start, steps, most, ids, source, waves, store):
    def action(n):
        at = pl.ds(start, n * TILE)
        member = (ids[:, at] == cell).astype(F32).astype(BF16)
        store(mm(source[:, at] * member, waves[:, at], 1, 1))

    by_steps(steps, most, action)


def spread_cell(cell, start, steps, most, ids, weights, waves, out):
    def action(n):
        for t in range(n):
            at = pl.ds(pl.multiple_of(start + t * TILE, LANES), TILE)
            value = mm(weights[...], waves[:, at])
            out[:, at] = jnp.where(ids[:, at] == cell, value, out[:, at])

    by_steps(steps, most, action)


def inverse_count(count):
    return 1.0 / jnp.full((1, 1), count, jnp.int32).astype(F32)


def shape_of(cell, quad, width_cols, first, size):
    exponent = quad[pl.ds(cell, 1), :][:, first : first + size] * width_cols[:, 0:1]
    return jnp.exp2(exponent)


def fill_waves(waves, base, kcols, coords):
    own = kcols.shape[0]
    atoms = coords.shape[1]
    wide = tile_of(atoms, 1024)

    def phase_rows(i, carry):
        row = pl.multiple_of(i * 16, 16)
        kv = kcols[pl.ds(row, 16), :]
        for start in range(0, atoms, wide):
            frac = coords[:, start : start + wide]
            turns = kv[:, 0:1] * frac[0:1, :] + kv[:, 1:2] * frac[1:2, :]
            turns = turns + kv[:, 2:3] * frac[2:3, :]
            turns = turns - ((turns + ROUNDER) - ROUNDER)
            square = turns * turns
            waves[pl.ds(pl.multiple_of(base + row, 16), 16), start : start + wide] = horner(
                COS_TERMS, square
            ).astype(BF16)
            waves[pl.ds(pl.multiple_of(base + own + row, 16), 16), start : start + wide] = (
                horner(SIN_TERMS, square) * turns
            ).astype(BF16)
        return carry

    lax.fori_loop(0, own // 16, phase_rows, 0)


def vector_columns(kvec):
    rows = kvec[...].astype(F32)
    if rows.shape[0] == 3:
        rows = jnp.concatenate([rows, jnp.zeros((5, rows.shape[1]), F32)], axis=0)
    return rows.T


def start_copies(sems, *moves):
    copies = [pltpu.make_async_copy(a, b, sems.at[i]) for i, (a, b) in enumerate(moves)]
    for copy in copies:
        copy.start()
    return copies


def prepare_kernel(
    coords_hbm, ids_hbm, recip_hbm, kvec_hbm, kfilt_hbm,
    waves, ids, coords, recip, kvec, kfilt, kcols, sems,
):
    atoms = coords.shape[1]
    copies = start_copies(
        sems,
        (kvec_hbm, kvec),
        (coords_hbm, coords),
        (ids_hbm, ids.at[:, :atoms]),
        (recip_hbm, recip),
        (kfilt_hbm, kfilt),
    )
    ids[:, atoms:] = jnp.full((1, LANES), -1, jnp.int32)
    waves[:, atoms:] = jnp.zeros((waves.shape[0], LANES), BF16)
    copies[0].wait()
    copies[1].wait()
    kcols[...] = vector_columns(kvec)
    fill_waves(waves, 0, kcols, coords)
    for copy in copies[2:]:
        copy.wait()


def pair_kernel(kvec, other_kvec, kfilt, other_kfilt, kvecs, kfilts):
    count = kvec.shape[0]
    for j in range(count):
        for at, source in ((j, kvec), (j + count, other_kvec)):
            rows = source[j].astype(F32)
            if rows.shape[0] == 3:
                rows = jnp.concatenate([rows, jnp.zeros((5, rows.shape[1]), F32)], axis=0)
            kvecs[at] = rows
        kfilts[j] = kfilt[j]
        kfilts[j + count] = other_kfilt[j]


def project_kernel(coords, kvecs, feats_hbm, w_in_hbm, waves, proj_t, feats, w_in, kcols, sems):
    atoms, chan = feats.shape
    copies = start_copies(sems, (w_in_hbm, w_in), (feats_hbm, feats))
    waves[:, atoms:] = jnp.zeros((waves.shape[0], LANES), BF16)
    proj_t[:, atoms:] = jnp.zeros((chan, LANES), BF16)
    kcols[...] = vector_columns(kvecs.at[1])
    fill_waves(waves, 0, kcols, coords)
    for copy in copies:
        copy.wait()

    def project(t, carry):
        at = pl.ds(pl.multiple_of(t * TILE, TILE), TILE)
        proj_t[:, at] = mm(w_in[...], feats[at, :], 0, 1).astype(BF16)
        return carry

    lax.fori_loop(0, atoms // TILE, project, 0)


def waves_kernel(n_ka, *refs):
    bounds, first, second, proj_t, ids, coords, recip = refs[:7]
    waves, factors, quad, kcols = refs[-4:]
    kvecs = [ref.at[j] for ref in refs[7:-4] for j in range(ref.shape[0])]
    atoms = coords.shape[1]
    own = kvecs[0].shape[1]
    cells = recip.shape[0]
    waves[: 2 * own, :] = first[...]
    waves[2 * own : 4 * own, :] = second[...]
    waves[4 * own :, atoms:] = jnp.zeros((2 * own * (n_ka - 2), LANES), BF16)
    for j in range(2, n_ka):
        kcols[...] = vector_columns(kvecs[j])
        fill_waves(waves, 2 * own * j, kcols, coords)
    for j in range(n_ka):
        rows = kvecs[j][...]
        squared = jnp.zeros((cells, own), F32)
        for r in range(3):
            part = recip[:, 3 * r : 3 * r + 1] * rows[0:1, :]
            part = part + recip[:, 3 * r + 1 : 3 * r + 2] * rows[1:2, :]
            part = part + recip[:, 3 * r + 2 : 3 * r + 3] * rows[2:3, :]
            squared = squared + part * part
        quad[:, own * j : own * (j + 1)] = squared

    def cell_step(cell, carry):
        start, steps, _ = span_of(bounds, cell)

        def store(value):
            factors[cell] = value

        gather_cell(cell, start, steps, most_steps(atoms), ids, proj_t, waves, store)
        return carry

    lax.fori_loop(0, cells, cell_step, 0)


def filters_first(filt_t, kfilts):
    chunk = 0
    for ref in kfilts:
        own = ref.shape[1]
        for j in range(ref.shape[0]):
            filt_t[:, chunk * own : (chunk + 1) * own] = ref[j].T
            chunk += 1
    return own


def message_kernel(n_ka, *refs):
    bounds, ids, quad, waves, factors, spread, cotan, w_out = refs[:8]
    act_t, mgrad_t, raw_out, raw_half, filt_t, width_cols, weights, mess_t = refs[-8:]
    atoms, chan = cotan.shape
    cells = quad.shape[0]
    own = filters_first(filt_t, refs[8:-8])
    width_cols[...] = column_to_lanes(spread[...] * (-LOG2_E))

    def cell_step(cell, carry):
        start, steps, count = span_of(bounds, cell)
        inverse = inverse_count(count)
        for j in range(n_ka):
            scaled = shape_of(cell, quad, width_cols, j * own, own) * inverse
            filt = filt_t[:, own * j : own * (j + 1)] * scaled
            for at in (slice(2 * own * j, own * (2 * j + 1)), slice(own * (2 * j + 1), 2 * own * (j + 1))):
                weights[:, at] = (filt * factors[cell, :, at]).astype(BF16)
        spread_cell(cell, start, steps, most_steps(atoms), ids, weights, waves, mess_t)
        return carry

    lax.fori_loop(0, cells, cell_step, 0)

    mgrad_t[:, atoms:] = jnp.zeros((chan, LANES), BF16)
    raw_out[...] = jnp.zeros_like(raw_out)

    def middle(t, carry):
        at = pl.ds(pl.multiple_of(t * TILE, TILE), TILE)
        message = mess_t[:, at]
        sigma = jax.nn.sigmoid(message)
        activated = (message * sigma).astype(BF16)
        act_t[:, at] = activated
        cot = cotan[at, :]
        act_grad = mm(w_out[...], cot, 1, 1)
        mgrad_t[:, at] = (act_grad * (sigma * (1.0 + message * (1.0 - sigma)))).astype(BF16)
        raw_out[...] += mm(activated, cot)
        return carry

    lax.fori_loop(0, atoms // TILE, middle, 0)
    raw_half[...] = raw_out[...].astype(BF16)


def adjoint_kernel(n_ka, *refs):
    bounds, ids, quad, waves, factors, mgrad_t, spread = refs[:7]
    weights, filter_grad, filter_half, filt_t, width_cols, total, grad_t = refs[-7:]
    atoms = mgrad_t.shape[1] - LANES
    cells = quad.shape[0]
    own = filters_first(filt_t, refs[7:-7])
    width_cols[...] = column_to_lanes(spread[...] * (-LOG2_E))
    grad_t[...] = jnp.zeros_like(grad_t)

    def cell_step(cell, carry):
        start, steps, count = span_of(bounds, cell)

        def store(value):
            total[...] = value

        gather_cell(cell, start, steps, most_steps(atoms), ids, mgrad_t, waves, store)
        inverse = inverse_count(count)
        for j in range(n_ka):
            scaled = shape_of(cell, quad, width_cols, j * own, own) * inverse
            filt = filt_t[:, own * j : own * (j + 1)] * scaled
            real = slice(2 * own * j, own * (2 * j + 1))
            imag = slice(own * (2 * j + 1), 2 * own * (j + 1))
            weights[cell, :, real] = (filt * total[:, real]).astype(BF16)
            weights[cell, :, imag] = (filt * total[:, imag]).astype(BF16)
            if j == 0:
                grad_t[...] += scaled * (
                    factors[cell, :, real] * total[:, real] + factors[cell, :, imag] * total[:, imag]
                )
        return carry

    lax.fori_loop(0, cells, cell_step, 0)
    result = grad_t[...].T
    filter_grad[...] = result
    filter_half[...] = result.astype(BF16)


def update_kernel(bounds, ids, waves, weights, feats, update_t, raw_in_t, total_t):
    cells, _, _ = weights.shape
    atoms = feats.shape[0]

    def cell_step(cell, carry):
        start, steps, _ = span_of(bounds, cell)
        spread_cell(
            cell, start, steps, most_steps(atoms), ids, weights.at[cell], waves, total_t
        )
        return carry

    lax.fori_loop(0, cells, cell_step, 0)
    raw_in_t[...] = jnp.zeros_like(raw_in_t)

    def last(t, carry):
        at = pl.ds(pl.multiple_of(t * TILE, TILE), TILE)
        update = total_t[:, at].astype(BF16)
        update_t[:, at] = update
        raw_in_t[...] += mm(update, feats[at, :])
        return carry

    lax.fori_loop(0, atoms // TILE, last, 0)


def residual_kernel(transposed, base, values_t, weight, out):
    value = mm(values_t[...].T, weight[...], 1, 1 if transposed else 0)
    out[...] = (base[...].astype(F32) + value).astype(BF16)


def residual(transposed, base, values_t, weight):
    rows, chan = base.shape
    step = tile_of(rows, 512)
    by_rows = pl.BlockSpec((step, chan), lambda i: (i, 0))
    return pl.pallas_call(
        functools.partial(residual_kernel, transposed),
        out_shape=jax.ShapeDtypeStruct((rows, chan), BF16),
        grid=(rows // step,),
        in_specs=[
            by_rows,
            pl.BlockSpec((chan, step), lambda i: (0, i)),
            pl.BlockSpec((chan, chan), lambda i: (0, 0)),
        ],
        out_specs=by_rows,
        compiler_params=pltpu.CompilerParams(vmem_limit_bytes=SMALL),
        cost_estimate=pl.CostEstimate(
            flops=2 * FLOPS_PER_MICRO, bytes_accessed=0, transcendentals=0
        ),
    )(base, values_t, weight)


def join_kernel(raw_in_t, raw_out, filt, *refs):
    pack = refs[-1]
    chan = raw_in_t.shape[0]
    pack[:chan, :] = raw_in_t[...]
    pack[chan : 2 * chan, :] = total_of(raw_out, refs[0:1])
    pack[2 * chan :, :] = total_of(filt, refs[1:-1])


def chip_kernel(pack, near, in_sum, in_half, w_sum, f_sum, f_squares):
    chan = in_sum.shape[0]
    value = pack[:chan, :] + near[:chan, :]
    in_sum[...] = value
    in_half[...] = value.astype(BF16)
    w_sum[...] = pack[chan : 2 * chan, :] + near[chan : 2 * chan, :]
    filt = pack[2 * chan :, :] + near[2 * chan :, :]
    f_sum[...] = filt
    f_squares[...] = jnp.broadcast_to(
        jnp.sum(jnp.sum(filt * filt, axis=0, keepdims=True), axis=1, keepdims=True),
        f_squares.shape,
    )


def total_of(first, others):
    value = first[...]
    for other in others:
        value = value + other[...].astype(F32)
    return value


def add_kernel(first, second, *outs):
    value = first[...] + second[...].astype(F32)
    for out in outs:
        out[...] = value.astype(out.dtype)


def final_kernel(n_chip, n_ka, *refs):
    in_parts = refs[:n_chip]
    raw_out, filt, squares, g_in, g_out, g_filt = refs[n_chip:]
    raw_in = total_of(in_parts[0], in_parts[1:])
    out = raw_out[...]
    both = raw_in * raw_in + out * out
    weight_squares = jnp.sum(jnp.sum(both, axis=0, keepdims=True), axis=1, keepdims=True)
    weight_scale = lax.rsqrt(weight_squares / (2 * raw_in.size) + 1e-06)
    filter_scale = lax.rsqrt(squares[0:1, 0:1] / (n_ka * filt.size) + 1e-06)
    g_in[...] = (raw_in * weight_scale).T
    g_out[...] = out * weight_scale
    g_filt[...] = filt[...] * filter_scale


def call(kernel, operands, smem, outs, scratch=(), limit=SMALL, micros=2, space=pltpu.VMEM):
    vmem = pl.BlockSpec(memory_space=pltpu.VMEM)
    rest = len(operands) - smem
    spaces = space if isinstance(space, tuple) else (space,) * rest
    return pl.pallas_call(
        kernel,
        out_shape=tuple(jax.ShapeDtypeStruct(*o) for o in outs),
        in_specs=[pl.BlockSpec(memory_space=x) for x in (pltpu.SMEM,) * smem + spaces],
        out_specs=tuple(vmem for _ in outs),
        scratch_shapes=list(scratch),
        compiler_params=pltpu.CompilerParams(vmem_limit_bytes=limit),
        cost_estimate=pl.CostEstimate(
            flops=micros * FLOPS_PER_MICRO, bytes_accessed=0, transcendentals=0
        ),
    )(*operands)


def in_hbm(value):
    return pltpu.with_memory_space_constraint(value, pltpu.HBM)


def send(value, axis, step):
    return lax.ppermute(value, axis, routes(step, lax.axis_size(axis)))


def doubling(first, size):
    return [first << i for i in range(size.bit_length()) if first << i < size]


def block(feats, coords, cell_ids, recip, kvec, w_in, w_out, kfilt, spread, cotan):
    n_ka = lax.axis_size("ka")
    n_dp = lax.axis_size("dp")
    atoms, chan = feats.shape
    own = kvec.shape[1]
    k_all = own * n_ka
    cells = recip.shape[1]
    long = atoms + LANES
    recip, spread = recip[0], spread[None]
    chips = range(2, n_dp, 2)
    vm = pltpu.VMEM
    dma = pltpu.SemaphoreType.DMA
    near_kvec = send(kvec[None], "ka", 1)
    near_kfilt = send(kfilt[None], "ka", 1)
    numbers = jnp.arange(cells, dtype=jnp.int32)[:, None]
    bounds = jnp.stack(
        [
            jnp.sum((cell_ids == numbers).astype(jnp.int32), axis=1),
            jnp.sum((cell_ids < numbers).astype(jnp.int32), axis=1),
        ]
    )
    first, ids, coords, recip, kvec, kfilt = call(
        prepare_kernel,
        [in_hbm(x) for x in (coords, cell_ids, recip, kvec, kfilt)],
        0,
        [
            ((2 * own, long), BF16),
            ((1, long), jnp.int32),
            (coords.shape, F32),
            (recip.shape, F32),
            (kvec.shape, jnp.int32),
            (kfilt.shape, F32),
        ],
        [vm((own, 8), F32), dma((5,))],
        SMALL,
        3,
        pltpu.HBM,
    )
    kvecs, kfilts = call(
        pair_kernel,
        (kvec[None], near_kvec, kfilt[None], near_kfilt),
        0,
        [((2, 8, own), F32), ((2, own, chan), F32)],
    )
    far_kvecs, far_kfilts = [kvecs], [kfilts]
    for s in doubling(2, n_ka):
        if s > 2:
            kvecs, kfilts = call(
                pair_kernel,
                (kvecs, far_kvecs[-1], kfilts, far_kfilts[-1]),
                0,
                [((s, 8, own), F32), ((s, own, chan), F32)],
            )
        far_kvecs.append(send(kvecs, "ka", s))
        far_kfilts.append(send(kfilts, "ka", s))
    second, proj_t = call(
        project_kernel,
        (coords, far_kvecs[0], in_hbm(feats), in_hbm(w_in)),
        0,
        [((2 * own, long), BF16), ((chan, long), BF16)],
        [vm((atoms, chan), BF16), vm((chan, chan), BF16), vm((own, 8), F32), dma((2,))],
        SMALL,
        3,
        (pltpu.VMEM, pltpu.VMEM, pltpu.HBM, pltpu.HBM),
    )
    waves, factors, quad = call(
        functools.partial(waves_kernel, n_ka),
        (bounds, first, second, proj_t, ids, coords, recip, *far_kvecs),
        1,
        [((2 * k_all, long), BF16), ((cells, chan, 2 * k_all), F32), ((cells, k_all), F32)],
        [vm((own, 8), F32)],
        LIMIT,
        8,
    )
    act_t, mgrad_t, raw_out, raw_half = call(
        functools.partial(message_kernel, n_ka),
        (bounds, ids, quad, waves, factors, spread, cotan, w_out, *far_kfilts),
        1,
        [((chan, atoms), BF16), ((chan, long), BF16), ((chan, chan), F32), ((chan, chan), BF16)],
        [vm((chan, k_all), F32), vm((chan, 8), F32), vm((chan, 2 * k_all), BF16), vm((chan, long), F32)],
        LIMIT,
        8,
    )
    out_steps = doubling(2, n_dp)
    out_part = send(raw_half, "dp", out_steps[0])
    weights, filter_grad, filter_half = call(
        functools.partial(adjoint_kernel, n_ka),
        (bounds, ids, quad, waves, factors, mgrad_t, spread, *far_kfilts),
        1,
        [((cells, chan, 2 * k_all), BF16), ((own, chan), F32), ((own, chan), BF16)],
        [vm((chan, k_all), F32), vm((chan, 8), F32), vm((chan, 2 * k_all), F32), vm((chan, own), F32)],
        LIMIT,
        8,
    )
    filt_parts = [send(filter_half, "dp", s) for s in chips]
    for s in out_steps[1:]:
        raw_out, raw_half = call(
            add_kernel, (raw_out, out_part), 0, [((chan, chan), F32), ((chan, chan), BF16)]
        )
        out_part = send(raw_half, "dp", s)
    update_t, raw_in_t = call(
        update_kernel,
        (bounds, ids, waves, weights, feats),
        1,
        [((chan, atoms), BF16), ((chan, chan), F32)],
        [vm((chan, long), F32)],
        LIMIT,
        8,
    )
    (pack,) = call(
        join_kernel,
        (raw_in_t, raw_out, filter_grad, out_part, *filt_parts),
        0,
        [((2 * chan + own, chan), F32)],
    )
    near = send(pack, "dp", 1)
    feat_grad = residual(True, cotan, update_t, w_in)
    in_sum, in_half, w_sum, f_sum, squares = call(
        chip_kernel,
        (pack, near),
        0,
        [
            ((chan, chan), F32),
            ((chan, chan), BF16),
            ((chan, chan), F32),
            ((own, chan), F32),
            ((8, LANES), F32),
        ],
    )
    in_parts = [in_sum] + [send(in_half, "dp", s) for s in chips]
    for s in doubling(1, n_ka):
        (squares,) = call(add_kernel, (squares, send(squares, "ka", s)), 0, [((8, LANES), F32)])
    mixed = residual(False, feats, act_t, w_out)
    grads = call(
        functools.partial(final_kernel, len(in_parts), n_ka),
        (*in_parts, w_sum, f_sum, squares),
        0,
        [((chan, chan), F32), ((chan, chan), F32), ((own, chan), F32)],
    )
    return (mixed, feat_grad, *grads)


def solution(mesh):
    placed = (
        P("dp", None),
        P(None, "dp"),
        P("dp", None),
        P("dp", None, None),
        P(None, "ka"),
        P(),
        P(),
        P("ka", None),
        P(),
        P("dp", None),
    )
    return jax.shard_map(
        block,
        mesh=mesh,
        in_specs=placed,
        out_specs=(P("dp", None), P("dp", None), P(), P(), P("ka", None)),
        check_vma=False,
    )
```

```python
import functools

import jax
import jax.numpy as jnp
from jax import lax
from jax.experimental import pallas as pl
from jax.experimental.pallas import tpu as pltpu
from jax.sharding import PartitionSpec as P


F32 = jnp.float32
BF16 = jnp.bfloat16
LANES = 128
TILE = 256
MOST = 1024
LIMIT = 24 << 20
SMALL = 6 << 20
FLOPS_PER_MICRO = 1 << 30
LOG2_E = 1.4426950408889634
COS_TERMS = (
    0.9999999890590228,
    -19.73920449945383,
    64.93911745989081,
    -85.45013953079767,
    60.167630950263465,
    -25.967599245923743,
    6.52865815775625,
)
SIN_TERMS = (
    6.283184916495428,
    -41.34158923268831,
    81.59994332977429,
    -76.61447253115396,
    41.34288235413569,
    -12.471243534350362,
)
ROUNDER = 12582912.0


def mm(lhs, rhs, lhs_dim=1, rhs_dim=0):
    return lax.dot_general(
        lhs, rhs, (((lhs_dim,), (rhs_dim,)), ((), ())), preferred_element_type=F32
    )


def horner(terms, square):
    value = terms[-1] * square + terms[-2]
    for term in terms[-3::-1]:
        value = value * square + term
    return value


def routes(step, count):
    if count & (count - 1) == 0:
        return [(i, i ^ step) for i in range(count)]
    return [(i, (i + step) % count) for i in range(count)]


def tile_of(size, most):
    tile = most
    while size % tile:
        tile //= 2
    return tile


def column_to_lanes(row):
    return jnp.broadcast_to(row, (8, row.shape[1])).T


def span_of(bounds, cell):
    first = bounds[1, cell]
    start = lax.div(first, LANES) * LANES
    count = bounds[0, cell]
    steps = lax.div(first - start + count + (TILE - 1), TILE)
    return pl.multiple_of(start, LANES), steps, count


def most_steps(atoms):
    return -(-(min(MOST, atoms) + LANES - 1) // TILE)


def by_steps(steps, most, action):
    for n in range(1, most + 1):
        pl.when(steps == n)(functools.partial(action, n))


def gather_cell(cell, start, steps, most, ids, source, waves, store):
    def action(n):
        at = pl.ds(start, n * TILE)
        member = (ids[:, at] == cell).astype(F32).astype(BF16)
        store(mm(source[:, at] * member, waves[:, at], 1, 1))

    by_steps(steps, most, action)


def weigh(cell, n_ka, bounds, quad, filt_t, width_cols, sums, weights):
    own = filt_t.shape[1] // n_ka
    inverse = inverse_count(bounds[0, cell])
    for j in range(n_ka):
        scaled = shape_of(cell, quad, width_cols, j * own, own) * inverse
        filt = filt_t[:, own * j : own * (j + 1)] * scaled
        for half in (2 * j, 2 * j + 1):
            at = slice(own * half, own * (half + 1))
            weights[:, at] = (filt * sums[cell, :, at]).astype(BF16)


def spread_cells(n_ka, bounds, ids, quad, filt_t, width_cols, sums, waves, even, odd, out):
    cells = quad.shape[0]
    most = most_steps(out.shape[1] - LANES)

    def one(cell, weights, after, target):
        start, steps, _ = span_of(bounds, cell)

        def action(n):
            if after is not None:
                weigh(after, n_ka, bounds, quad, filt_t, width_cols, sums, target)
            for t in range(n):
                at = pl.ds(pl.multiple_of(start + t * TILE, LANES), TILE)
                value = mm(weights[...], waves[:, at])
                out[:, at] = jnp.where(ids[:, at] == cell, value, out[:, at])

        by_steps(steps, most, action)

    weigh(0, n_ka, bounds, quad, filt_t, width_cols, sums, even)

    def two(i, carry):
        one(2 * i, even, jnp.minimum(2 * i + 1, cells - 1), odd)
        one(2 * i + 1, odd, jnp.minimum(2 * i + 2, cells - 1), even)
        return carry

    lax.fori_loop(0, cells // 2, two, 0)
    if cells % 2:
        one(cells - 1, even, None, None)


def inverse_count(count):
    return 1.0 / jnp.full((1, 1), count, jnp.int32).astype(F32)


def shape_of(cell, quad, width_cols, first, size):
    exponent = quad[pl.ds(cell, 1), :][:, first : first + size] * width_cols[:, 0:1]
    return jnp.exp2(exponent)


def fill_waves(waves, base, kcols, coords):
    own = kcols.shape[0]
    atoms = coords.shape[1]
    wide = tile_of(atoms, 1024)

    def phase_rows(i, carry):
        row = pl.multiple_of(i * 16, 16)
        kv = kcols[pl.ds(row, 16), :]
        for start in range(0, atoms, wide):
            frac = coords[:, start : start + wide]
            turns = kv[:, 0:1] * frac[0:1, :] + kv[:, 1:2] * frac[1:2, :]
            turns = turns + kv[:, 2:3] * frac[2:3, :]
            turns = turns - ((turns + ROUNDER) - ROUNDER)
            square = turns * turns
            waves[pl.ds(pl.multiple_of(base + row, 16), 16), start : start + wide] = horner(
                COS_TERMS, square
            ).astype(BF16)
            waves[pl.ds(pl.multiple_of(base + own + row, 16), 16), start : start + wide] = (
                horner(SIN_TERMS, square) * turns
            ).astype(BF16)
        return carry

    lax.fori_loop(0, own // 16, phase_rows, 0)


def vector_columns(kvec):
    rows = kvec[...].astype(F32)
    if rows.shape[0] == 3:
        rows = jnp.concatenate([rows, jnp.zeros((5, rows.shape[1]), F32)], axis=0)
    return rows.T


def start_copies(sems, *moves):
    copies = [pltpu.make_async_copy(a, b, sems.at[i]) for i, (a, b) in enumerate(moves)]
    for copy in copies:
        copy.start()
    return copies


def prepare_kernel(
    coords_hbm, ids_hbm, recip_hbm, kvec_hbm, kfilt_hbm,
    waves, ids, coords, recip, kvec, kfilt, kcols, sems,
):
    atoms = coords.shape[1]
    copies = start_copies(
        sems,
        (kvec_hbm, kvec),
        (coords_hbm, coords),
        (ids_hbm, ids.at[:, :atoms]),
        (recip_hbm, recip),
        (kfilt_hbm, kfilt),
    )
    ids[:, atoms:] = jnp.full((1, LANES), -1, jnp.int32)
    waves[:, atoms:] = jnp.zeros((waves.shape[0], LANES), BF16)
    copies[0].wait()
    copies[1].wait()
    kcols[...] = vector_columns(kvec)
    fill_waves(waves, 0, kcols, coords)
    for copy in copies[2:]:
        copy.wait()


def pair_kernel(kvec, other_kvec, kfilt, other_kfilt, kvecs, kfilts):
    count = kvec.shape[0]
    for j in range(count):
        for at, source in ((j, kvec), (j + count, other_kvec)):
            rows = source[j].astype(F32)
            if rows.shape[0] == 3:
                rows = jnp.concatenate([rows, jnp.zeros((5, rows.shape[1]), F32)], axis=0)
            kvecs[at] = rows
        kfilts[j] = kfilt[j]
        kfilts[j + count] = other_kfilt[j]


def project_kernel(coords, kvecs, feats_hbm, w_in_hbm, waves, proj_t, feats, w_in, kcols, sems):
    atoms, chan = feats.shape
    copies = start_copies(sems, (w_in_hbm, w_in), (feats_hbm, feats))
    waves[:, atoms:] = jnp.zeros((waves.shape[0], LANES), BF16)
    proj_t[:, atoms:] = jnp.zeros((chan, LANES), BF16)
    kcols[...] = vector_columns(kvecs.at[1])
    fill_waves(waves, 0, kcols, coords)
    for copy in copies:
        copy.wait()

    def project(t, carry):
        at = pl.ds(pl.multiple_of(t * TILE, TILE), TILE)
        proj_t[:, at] = mm(w_in[...], feats[at, :], 0, 1).astype(BF16)
        return carry

    lax.fori_loop(0, atoms // TILE, project, 0)


def waves_kernel(n_ka, *refs):
    bounds, first, second, proj_t, ids, coords, recip = refs[:7]
    waves, factors, quad, kcols = refs[-4:]
    kvecs = [ref.at[j] for ref in refs[7:-4] for j in range(ref.shape[0])]
    atoms = coords.shape[1]
    own = kvecs[0].shape[1]
    cells = recip.shape[0]
    waves[: 2 * own, :] = first[...]
    waves[2 * own : 4 * own, :] = second[...]
    waves[4 * own :, atoms:] = jnp.zeros((2 * own * (n_ka - 2), LANES), BF16)
    for j in range(2, n_ka):
        kcols[...] = vector_columns(kvecs[j])
        fill_waves(waves, 2 * own * j, kcols, coords)
    for j in range(n_ka):
        rows = kvecs[j][...]
        squared = jnp.zeros((cells, own), F32)
        for r in range(3):
            part = recip[:, 3 * r : 3 * r + 1] * rows[0:1, :]
            part = part + recip[:, 3 * r + 1 : 3 * r + 2] * rows[1:2, :]
            part = part + recip[:, 3 * r + 2 : 3 * r + 3] * rows[2:3, :]
            squared = squared + part * part
        quad[:, own * j : own * (j + 1)] = squared

    def cell_step(cell, carry):
        start, steps, _ = span_of(bounds, cell)

        def store(value):
            factors[cell] = value

        gather_cell(cell, start, steps, most_steps(atoms), ids, proj_t, waves, store)
        return carry

    lax.fori_loop(0, cells, cell_step, 0)


def filters_first(filt_t, kfilts):
    chunk = 0
    for ref in kfilts:
        own = ref.shape[1]
        for j in range(ref.shape[0]):
            filt_t[:, chunk * own : (chunk + 1) * own] = ref[j].T
            chunk += 1
    return own


def message_kernel(n_ka, *refs):
    bounds, ids, quad, waves, factors, spread, cotan, w_out = refs[:8]
    act_t, mgrad_t, raw_out, raw_half, filt_t, width_cols, even, odd, mess_t = refs[-9:]
    atoms, chan = cotan.shape
    filters_first(filt_t, refs[8:-9])
    width_cols[...] = column_to_lanes(spread[...] * (-LOG2_E))
    spread_cells(n_ka, bounds, ids, quad, filt_t, width_cols, factors, waves, even, odd, mess_t)
    mgrad_t[:, atoms:] = jnp.zeros((chan, LANES), BF16)
    raw_out[...] = jnp.zeros_like(raw_out)

    def middle(t, carry):
        at = pl.ds(pl.multiple_of(t * TILE, TILE), TILE)
        message = mess_t[:, at]
        sigma = jax.nn.sigmoid(message)
        activated = (message * sigma).astype(BF16)
        act_t[:, at] = activated
        cot = cotan[at, :]
        act_grad = mm(w_out[...], cot, 1, 1)
        mgrad_t[:, at] = (act_grad * (sigma * (1.0 + message * (1.0 - sigma)))).astype(BF16)
        raw_out[...] += mm(activated, cot)
        return carry

    lax.fori_loop(0, atoms // TILE, middle, 0)
    raw_half[...] = raw_out[...].astype(BF16)


def adjoint_kernel(n_ka, *refs):
    bounds, ids, quad, waves, factors, mgrad_t, spread = refs[:7]
    sums, filter_grad, filter_half, width_cols, grad_t = refs[7:]
    atoms = mgrad_t.shape[1] - LANES
    cells, k_all = quad.shape
    own = k_all // n_ka
    width_cols[...] = column_to_lanes(spread[...] * (-LOG2_E))
    grad_t[...] = jnp.zeros_like(grad_t)

    def cell_step(cell, carry):
        start, steps, count = span_of(bounds, cell)

        def store(value):
            sums[cell] = value

        gather_cell(cell, start, steps, most_steps(atoms), ids, mgrad_t, waves, store)
        scaled = shape_of(cell, quad, width_cols, 0, own) * inverse_count(count)
        grad_t[...] += scaled * (
            factors[cell, :, :own] * sums[cell, :, :own]
            + factors[cell, :, own : 2 * own] * sums[cell, :, own : 2 * own]
        )
        return carry

    lax.fori_loop(0, cells, cell_step, 0)
    result = grad_t[...].T
    filter_grad[...] = result
    filter_half[...] = result.astype(BF16)


def update_kernel(n_ka, *refs):
    bounds, ids, quad, waves, sums, spread = refs[:6]
    update_t = refs[-11]
    filt_t, width_cols, even, odd, total_t, sems = refs[-6:]
    copies = start_copies(sems, *zip(refs[-15:-11], refs[-10:-6]))
    atoms = update_t.shape[1]
    filters_first(filt_t, refs[6:-15])
    width_cols[...] = column_to_lanes(spread[...] * (-LOG2_E))
    spread_cells(n_ka, bounds, ids, quad, filt_t, width_cols, sums, waves, even, odd, total_t)
    update_t[...] = total_t[:, :atoms].astype(BF16)
    for copy in copies:
        copy.wait()


def gradient_kernel(update_t, feats, raw_in_t):
    raw_in_t[...] = mm(update_t[...], feats[...])


def residual_kernel(transposed, base, values_t, weight, out):
    value = mm(values_t[...].T, weight[...], 1, 1 if transposed else 0)
    out[...] = (base[...].astype(F32) + value).astype(BF16)


def residual(transposed, base, values_t, weight):
    rows, chan = base.shape
    step = tile_of(rows, 512)
    by_rows = pl.BlockSpec((step, chan), lambda i: (i, 0))
    return pl.pallas_call(
        functools.partial(residual_kernel, transposed),
        out_shape=jax.ShapeDtypeStruct((rows, chan), BF16),
        grid=(rows // step,),
        in_specs=[
            by_rows,
            pl.BlockSpec((chan, step), lambda i: (0, i)),
            pl.BlockSpec((chan, chan), lambda i: (0, 0)),
        ],
        out_specs=by_rows,
        compiler_params=pltpu.CompilerParams(vmem_limit_bytes=SMALL),
        cost_estimate=pl.CostEstimate(
            flops=2 * FLOPS_PER_MICRO, bytes_accessed=0, transcendentals=0
        ),
    )(base, values_t, weight)


def join_kernel(raw_in_t, raw_out, other_out, pack):
    chan = raw_in_t.shape[0]
    pack[:chan, :] = raw_in_t[...]
    pack[chan:, :] = total_of(raw_out, (other_out,))


def filter_kernel(*refs):
    refs[-1][...] = total_of(refs[0], refs[1:-1])


def squares_kernel(filt, near, f_sum, f_squares):
    value = filt[...] + near[...]
    f_sum[...] = value
    f_squares[...] = jnp.broadcast_to(
        jnp.sum(jnp.sum(value * value, axis=0, keepdims=True), axis=1, keepdims=True),
        f_squares.shape,
    )


def chip_kernel(pack, near, in_sum, in_half, w_sum):
    chan = in_sum.shape[0]
    value = pack[:chan, :] + near[:chan, :]
    in_sum[...] = value
    in_half[...] = value.astype(BF16)
    w_sum[...] = pack[chan:, :] + near[chan:, :]


def total_of(first, others):
    value = first[...]
    for other in others:
        value = value + other[...].astype(F32)
    return value


def add_kernel(first, second, *outs):
    value = first[...] + second[...].astype(F32)
    for out in outs:
        out[...] = value.astype(out.dtype)


def final_kernel(n_chip, n_ka, *refs):
    in_parts = refs[:n_chip]
    raw_out, filt, squares, g_in, g_out, g_filt = refs[n_chip:]
    raw_in = total_of(in_parts[0], in_parts[1:])
    out = raw_out[...]
    both = raw_in * raw_in + out * out
    weight_squares = jnp.sum(jnp.sum(both, axis=0, keepdims=True), axis=1, keepdims=True)
    weight_scale = lax.rsqrt(weight_squares / (2 * raw_in.size) + 1e-06)
    filter_scale = lax.rsqrt(squares[0:1, 0:1] / (n_ka * filt.size) + 1e-06)
    g_in[...] = (raw_in * weight_scale).T
    g_out[...] = out * weight_scale
    g_filt[...] = filt[...] * filter_scale


def call(kernel, operands, smem, outs, scratch=(), limit=SMALL, micros=2, space=pltpu.VMEM):
    vmem = pl.BlockSpec(memory_space=pltpu.VMEM)
    rest = len(operands) - smem
    spaces = space if isinstance(space, tuple) else (space,) * rest
    return pl.pallas_call(
        kernel,
        out_shape=tuple(jax.ShapeDtypeStruct(*o) for o in outs),
        in_specs=[pl.BlockSpec(memory_space=x) for x in (pltpu.SMEM,) * smem + spaces],
        out_specs=tuple(vmem for _ in outs),
        scratch_shapes=list(scratch),
        compiler_params=pltpu.CompilerParams(vmem_limit_bytes=limit),
        cost_estimate=pl.CostEstimate(
            flops=micros * FLOPS_PER_MICRO, bytes_accessed=0, transcendentals=0
        ),
    )(*operands)


def in_hbm(value):
    return pltpu.with_memory_space_constraint(value, pltpu.HBM)


def send(value, axis, step):
    return lax.ppermute(value, axis, routes(step, lax.axis_size(axis)))


def doubling(first, size):
    return [first << i for i in range(size.bit_length()) if first << i < size]


def block(feats, coords, cell_ids, recip, kvec, w_in, w_out, kfilt, spread, cotan):
    n_ka = lax.axis_size("ka")
    n_dp = lax.axis_size("dp")
    atoms, chan = feats.shape
    own = kvec.shape[1]
    k_all = own * n_ka
    cells = recip.shape[1]
    long = atoms + LANES
    recip, spread = recip[0], spread[None]
    chips = range(2, n_dp, 2)
    vm = pltpu.VMEM
    dma = pltpu.SemaphoreType.DMA
    near_kvec = send(kvec[None], "ka", 1)
    near_kfilt = send(kfilt[None], "ka", 1)
    numbers = jnp.arange(cells, dtype=jnp.int32)[:, None]
    bounds = jnp.stack(
        [
            jnp.sum((cell_ids == numbers).astype(jnp.int32), axis=1),
            jnp.sum((cell_ids < numbers).astype(jnp.int32), axis=1),
        ]
    )
    first, ids, coords, recip, kvec, kfilt = call(
        prepare_kernel,
        [in_hbm(x) for x in (coords, cell_ids, recip, kvec, kfilt)],
        0,
        [
            ((2 * own, long), BF16),
            ((1, long), jnp.int32),
            (coords.shape, F32),
            (recip.shape, F32),
            (kvec.shape, jnp.int32),
            (kfilt.shape, F32),
        ],
        [vm((own, 8), F32), dma((5,))],
        SMALL,
        3,
        pltpu.HBM,
    )
    kvecs, kfilts = call(
        pair_kernel,
        (kvec[None], near_kvec, kfilt[None], near_kfilt),
        0,
        [((2, 8, own), F32), ((2, own, chan), F32)],
    )
    far_kvecs, far_kfilts = [kvecs], [kfilts]
    for s in doubling(2, n_ka):
        if s > 2:
            kvecs, kfilts = call(
                pair_kernel,
                (kvecs, far_kvecs[-1], kfilts, far_kfilts[-1]),
                0,
                [((s, 8, own), F32), ((s, own, chan), F32)],
            )
        far_kvecs.append(send(kvecs, "ka", s))
        far_kfilts.append(send(kfilts, "ka", s))
    second, proj_t = call(
        project_kernel,
        (coords, far_kvecs[0], in_hbm(feats), in_hbm(w_in)),
        0,
        [((2 * own, long), BF16), ((chan, long), BF16)],
        [vm((atoms, chan), BF16), vm((chan, chan), BF16), vm((own, 8), F32), dma((2,))],
        SMALL,
        3,
        (pltpu.VMEM, pltpu.VMEM, pltpu.HBM, pltpu.HBM),
    )
    waves, factors, quad = call(
        functools.partial(waves_kernel, n_ka),
        (bounds, first, second, proj_t, ids, coords, recip, *far_kvecs),
        1,
        [((2 * k_all, long), BF16), ((cells, chan, 2 * k_all), F32), ((cells, k_all), F32)],
        [vm((own, 8), F32)],
        LIMIT,
        8,
    )
    halves = [vm((chan, 2 * k_all), BF16)] * 2
    act_t, mgrad_t, raw_out, raw_half = call(
        functools.partial(message_kernel, n_ka),
        (bounds, ids, quad, waves, factors, spread, cotan, w_out, *far_kfilts),
        1,
        [((chan, atoms), BF16), ((chan, long), BF16), ((chan, chan), F32), ((chan, chan), BF16)],
        [vm((chan, k_all), F32), vm((chan, 8), F32), *halves, vm((chan, long), F32)],
        LIMIT,
        8,
    )
    out_steps = doubling(2, n_dp)
    out_part = send(raw_half, "dp", out_steps[0])
    sums, filter_grad, filter_half = call(
        functools.partial(adjoint_kernel, n_ka),
        (bounds, ids, quad, waves, factors, mgrad_t, spread),
        1,
        [((cells, chan, 2 * k_all), F32), ((own, chan), F32), ((own, chan), BF16)],
        [vm((chan, 8), F32), vm((chan, own), F32)],
        LIMIT,
        6,
    )
    filt_parts = [send(filter_half, "dp", s) for s in chips]
    for s in out_steps[1:]:
        raw_out, raw_half = call(
            add_kernel, (raw_out, out_part), 0, [((chan, chan), F32), ((chan, chan), BF16)]
        )
        out_part = send(raw_half, "dp", s)
    held = (feats, cotan, w_in, w_out)
    update_t, feats, cotan, w_in, w_out = call(
        functools.partial(update_kernel, n_ka),
        (bounds, ids, quad, waves, sums, spread, *far_kfilts, *map(in_hbm, held)),
        1,
        [((chan, atoms), BF16), *((x.shape, BF16) for x in held)],
        [vm((chan, k_all), F32), vm((chan, 8), F32), *halves, vm((chan, long), F32), dma((4,))],
        LIMIT,
        8,
        (pltpu.VMEM,) * (5 + len(far_kfilts)) + (pltpu.HBM,) * 4,
    )
    (filt_sum,) = call(filter_kernel, (filter_grad, *filt_parts), 0, [((own, chan), F32)])
    filt_near = send(filt_sum, "dp", 1)
    (raw_in_t,) = call(gradient_kernel, (update_t, feats), 0, [((chan, chan), F32)])
    (pack,) = call(join_kernel, (raw_in_t, raw_out, out_part), 0, [((2 * chan, chan), F32)])
    near = send(pack, "dp", 1)
    f_sum, squares = call(
        squares_kernel, (filt_sum, filt_near), 0, [((own, chan), F32), ((8, LANES), F32)]
    )
    square_steps = doubling(1, n_ka)
    square_part = send(squares, "ka", square_steps[0])
    feat_grad = residual(True, cotan, update_t, w_in)
    in_sum, in_half, w_sum = call(
        chip_kernel,
        (pack, near),
        0,
        [((chan, chan), F32), ((chan, chan), BF16), ((chan, chan), F32)],
    )
    in_parts = [in_sum] + [send(in_half, "dp", s) for s in chips]
    for s in square_steps[1:] + [0]:
        (squares,) = call(add_kernel, (squares, square_part), 0, [((8, LANES), F32)])
        if s:
            square_part = send(squares, "ka", s)
    mixed = residual(False, feats, act_t, w_out)
    grads = call(
        functools.partial(final_kernel, len(in_parts), n_ka),
        (*in_parts, w_sum, f_sum, squares),
        0,
        [((chan, chan), F32), ((chan, chan), F32), ((own, chan), F32)],
    )
    return (mixed, feat_grad, *grads)


def solution(mesh):
    placed = (
        P("dp", None),
        P(None, "dp"),
        P("dp", None),
        P("dp", None, None),
        P(None, "ka"),
        P(),
        P(),
        P("ka", None),
        P(),
        P("dp", None),
    )
    return jax.shard_map(
        block,
        mesh=mesh,
        in_specs=placed,
        out_specs=(P("dp", None), P("dp", None), P(), P(), P("ka", None)),
        check_vma=False,
    )
```

```python
import functools

import jax
import jax.numpy as jnp
from jax import lax
from jax.experimental import pallas as pl
from jax.experimental.pallas import tpu as pltpu
from jax.sharding import PartitionSpec as P


F32 = jnp.float32
BF16 = jnp.bfloat16
LANES = 128
TILE = 256
MOST = 1024
LIMIT = 24 << 20
SMALL = 6 << 20
FLOPS_PER_MICRO = 1 << 30
LOG2_E = 1.4426950408889634
COS_TERMS = (
    0.9999999890590228,
    -19.73920449945383,
    64.93911745989081,
    -85.45013953079767,
    60.167630950263465,
    -25.967599245923743,
    6.52865815775625,
)
SIN_TERMS = (
    6.283184916495428,
    -41.34158923268831,
    81.59994332977429,
    -76.61447253115396,
    41.34288235413569,
    -12.471243534350362,
)
ROUNDER = 12582912.0


def mm(lhs, rhs, lhs_dim=1, rhs_dim=0):
    return lax.dot_general(
        lhs, rhs, (((lhs_dim,), (rhs_dim,)), ((), ())), preferred_element_type=F32
    )


def horner(terms, square):
    value = terms[-1] * square + terms[-2]
    for term in terms[-3::-1]:
        value = value * square + term
    return value


def routes(step, count):
    if count & (count - 1) == 0:
        return [(i, i ^ step) for i in range(count)]
    return [(i, (i + step) % count) for i in range(count)]


def tile_of(size, most):
    tile = most
    while size % tile:
        tile //= 2
    return tile


def column_to_lanes(row):
    return jnp.broadcast_to(row, (8, row.shape[1])).T


def span_of(bounds, cell):
    first = bounds[1, cell]
    start = lax.div(first, LANES) * LANES
    count = bounds[0, cell]
    steps = lax.div(first - start + count + (TILE - 1), TILE)
    return pl.multiple_of(start, LANES), steps, count


def most_steps(atoms):
    return -(-(min(MOST, atoms) + LANES - 1) // TILE)


def by_steps(steps, most, action):
    for n in range(1, most + 1):
        pl.when(steps == n)(functools.partial(action, n))


def weigh(cell, n_ka, bounds, quad, filt_t, width_cols, sums, weights):
    own = filt_t.shape[1] // n_ka
    inverse = inverse_count(bounds[0, cell])
    for j in range(n_ka):
        scaled = shape_of(cell, quad, width_cols, j * own, own) * inverse
        filt = filt_t[:, own * j : own * (j + 1)] * scaled
        for half in (2 * j, 2 * j + 1):
            at = slice(own * half, own * (half + 1))
            weights[:, at] = (filt * sums[cell, :, at]).astype(BF16)


def spread_cells(n_ka, bounds, ids, quad, filt_t, width_cols, sums, waves, even, odd, out):
    cells = quad.shape[0]
    most = most_steps(out.shape[1] - LANES)

    def one(cell, weights, after, target):
        start, steps, _ = span_of(bounds, cell)

        def action(n):
            if after is not None:
                weigh(after, n_ka, bounds, quad, filt_t, width_cols, sums, target)
            for t in range(n):
                at = pl.ds(pl.multiple_of(start + t * TILE, LANES), TILE)
                value = mm(weights[...], waves[:, at])
                out[:, at] = jnp.where(ids[:, at] == cell, value, out[:, at])

        by_steps(steps, most, action)

    weigh(0, n_ka, bounds, quad, filt_t, width_cols, sums, even)

    def two(i, carry):
        one(2 * i, even, jnp.minimum(2 * i + 1, cells - 1), odd)
        one(2 * i + 1, odd, jnp.minimum(2 * i + 2, cells - 1), even)
        return carry

    lax.fori_loop(0, cells // 2, two, 0)
    if cells % 2:
        one(cells - 1, even, None, None)


def inverse_count(count):
    return 1.0 / jnp.full((1, 1), count, jnp.int32).astype(F32)


def shape_of(cell, quad, width_cols, first, size):
    exponent = quad[pl.ds(cell, 1), :][:, first : first + size] * width_cols[:, 0:1]
    return jnp.exp2(exponent)


def fill_slice(waves, base, own, kcols, first, row, coords):
    atoms = coords.shape[1]
    wide = tile_of(atoms, 1024)
    row = pl.multiple_of(row, 16)
    kv = kcols[pl.ds(pl.multiple_of(first + row, 16), 16), :]
    for start in range(0, atoms, wide):
        frac = coords[:, start : start + wide]
        turns = kv[:, 0:1] * frac[0:1, :] + kv[:, 1:2] * frac[1:2, :]
        turns = turns + kv[:, 2:3] * frac[2:3, :]
        turns = turns - ((turns + ROUNDER) - ROUNDER)
        square = turns * turns
        waves[pl.ds(pl.multiple_of(base + row, 16), 16), start : start + wide] = horner(
            COS_TERMS, square
        ).astype(BF16)
        waves[pl.ds(pl.multiple_of(base + own + row, 16), 16), start : start + wide] = (
            horner(SIN_TERMS, square) * turns
        ).astype(BF16)


def rows_of_share(index, shares, own):
    each = -(-own // (16 * shares))
    return [16 * jnp.minimum(index * each + p, own // 16 - 1) for p in range(each)]


def vector_columns(kvec):
    rows = kvec[...].astype(F32)
    if rows.shape[0] == 3:
        rows = jnp.concatenate([rows, jnp.zeros((5, rows.shape[1]), F32)], axis=0)
    return rows.T


def start_copies(sems, *moves):
    copies = [pltpu.make_async_copy(a, b, sems.at[i]) for i, (a, b) in enumerate(moves)]
    for copy in copies:
        copy.start()
    return copies


def prepare_kernel(
    coords_hbm, ids_hbm, recip_hbm, kvec_hbm, kfilt_hbm,
    waves, ids, coords, recip, kvec, kfilt, bounds, kcols, sems,
):
    atoms = coords.shape[1]
    own = kvec.shape[1]
    copies = start_copies(
        sems,
        (kvec_hbm, kvec),
        (coords_hbm, coords),
        (ids_hbm, ids.at[:, :atoms]),
        (recip_hbm, recip),
        (kfilt_hbm, kfilt),
    )
    ids[:, atoms:] = jnp.full((1, LANES), -1, jnp.int32)
    waves[:, atoms:] = jnp.zeros((waves.shape[0], LANES), BF16)
    for copy in copies[:3]:
        copy.wait()
    kcols[...] = vector_columns(kvec)
    numbers = ids[:, :atoms]
    before = 0
    for cell in range(bounds.shape[1]):
        count = jnp.sum((numbers == cell).astype(F32)).astype(jnp.int32)
        bounds[0, cell] = count
        bounds[1, cell] = before
        before = before + count

    def phase_rows(i, carry):
        fill_slice(waves, 0, own, kcols, 0, 16 * i, coords)
        return carry

    lax.fori_loop(0, own // 16, phase_rows, 0)
    for copy in copies[3:]:
        copy.wait()


def pair_kernel(kvec, other_kvec, kvecs):
    count = kvec.shape[0]
    for j in range(count):
        for at, source in ((j, kvec), (j + count, other_kvec)):
            rows = source[j].astype(F32)
            if rows.shape[0] == 3:
                rows = jnp.concatenate([rows, jnp.zeros((5, rows.shape[1]), F32)], axis=0)
            kvecs[at] = rows


def stack_kernel(near, far, out):
    count = near.shape[0]
    out[:count] = near[...].astype(out.dtype)
    out[count:] = far[...].astype(out.dtype)


def project_kernel(coords, kvecs, feats_hbm, w_in_hbm, waves, proj_t, feats, w_in, kcols, sems):
    atoms, chan = feats.shape
    own = kcols.shape[0]
    copies = start_copies(sems, (w_in_hbm, w_in), (feats_hbm, feats))
    waves[:, atoms:] = jnp.zeros((waves.shape[0], LANES), BF16)
    proj_t[:, atoms:] = jnp.zeros((chan, LANES), BF16)
    kcols[...] = vector_columns(kvecs.at[1])
    for copy in copies:
        copy.wait()
    tiles = atoms // TILE

    def project(t, carry):
        at = pl.ds(pl.multiple_of(t * TILE, TILE), TILE)
        proj_t[:, at] = mm(w_in[...], feats[at, :], 0, 1).astype(BF16)
        for row in rows_of_share(t, tiles, own):
            fill_slice(waves, 0, own, kcols, 0, row, coords)
        return carry

    lax.fori_loop(0, tiles, project, 0)


def waves_kernel(n_ka, *refs):
    bounds, first, second, proj_t, ids, coords, recip = refs[:7]
    waves, factors, quad, kcols = refs[-4:]
    kvecs = [ref.at[j] for ref in refs[7:-4] for j in range(ref.shape[0])]
    atoms = coords.shape[1]
    own = kvecs[0].shape[1]
    cells = recip.shape[0]
    most = most_steps(atoms)
    for j in range(2, n_ka):
        kcols[(j - 2) * own : (j - 1) * own, :] = vector_columns(kvecs[j])
    for j in range(n_ka):
        rows = kvecs[j][...]
        squared = jnp.zeros((cells, own), F32)
        for r in range(3):
            part = recip[:, 3 * r : 3 * r + 1] * rows[0:1, :]
            part = part + recip[:, 3 * r + 1 : 3 * r + 2] * rows[1:2, :]
            part = part + recip[:, 3 * r + 2 : 3 * r + 3] * rows[2:3, :]
            squared = squared + part * part
        quad[:, own * j : own * (j + 1)] = squared
    waves[4 * own :, atoms:] = jnp.zeros((2 * own * (n_ka - 2), LANES), BF16)

    def early(cell, carry):
        start, steps, _ = span_of(bounds, cell)

        def action(n):
            at = pl.ds(start, n * TILE)
            lhs = proj_t[:, at] * (ids[:, at] == cell).astype(F32).astype(BF16)
            factors[cell, :, : 2 * own] = mm(lhs, first[:, at], 1, 1)
            factors[cell, :, 2 * own : 4 * own] = mm(lhs, second[:, at], 1, 1)
            for j in range(2, n_ka):
                for row in rows_of_share(cell, cells, own):
                    fill_slice(waves, 2 * own * j, own, kcols, (j - 2) * own, row, coords)

        by_steps(steps, most, action)
        return carry

    lax.fori_loop(0, cells, early, 0)
    waves[: 2 * own, :] = first[...]
    waves[2 * own : 4 * own, :] = second[...]

    def late(cell, carry):
        start, steps, _ = span_of(bounds, cell)

        def action(n):
            at = pl.ds(start, n * TILE)
            lhs = proj_t[:, at] * (ids[:, at] == cell).astype(F32).astype(BF16)
            factors[cell, :, 4 * own :] = mm(lhs, waves[4 * own :, at], 1, 1)

        by_steps(steps, most, action)
        return carry

    lax.fori_loop(0, cells, late, 0)


def filters_first(filt_t, kfilts):
    chunk = 0
    for ref in kfilts:
        own = ref.shape[1]
        for j in range(ref.shape[0]):
            filt_t[:, chunk * own : (chunk + 1) * own] = ref[j].astype(F32).T
            chunk += 1
    return own


def message_kernel(n_ka, *refs):
    bounds, ids, quad, waves, factors, spread, cotan, w_out = refs[:8]
    act_t, mgrad_t, raw_out, raw_half, filt_t, width_cols, even, odd, mess_t = refs[-9:]
    atoms, chan = cotan.shape
    filters_first(filt_t, refs[8:-9])
    width_cols[...] = column_to_lanes(spread[...] * (-LOG2_E))
    spread_cells(n_ka, bounds, ids, quad, filt_t, width_cols, factors, waves, even, odd, mess_t)
    mgrad_t[:, atoms:] = jnp.zeros((chan, LANES), BF16)
    raw_out[...] = jnp.zeros_like(raw_out)

    wide = tile_of(atoms, 2 * TILE)

    def middle(t, carry):
        at = pl.ds(pl.multiple_of(t * wide, wide), wide)
        message = mess_t[:, at]
        sigma = jax.nn.sigmoid(message)
        activated = (message * sigma).astype(BF16)
        act_t[:, at] = activated
        cot = cotan[at, :]
        act_grad = mm(w_out[...], cot, 1, 1)
        mgrad_t[:, at] = (act_grad * (sigma * (1.0 + message * (1.0 - sigma)))).astype(BF16)
        raw_out[...] += mm(activated, cot)
        return carry

    lax.fori_loop(0, atoms // wide, middle, 0)
    raw_half[...] = raw_out[...].astype(BF16)


def adjoint_kernel(n_ka, *refs):
    bounds, ids, quad, waves, factors, mgrad_t, spread = refs[:7]
    sums, filter_grad, filter_half, width_cols, grad_t = refs[7:]
    atoms = mgrad_t.shape[1] - LANES
    cells, k_all = quad.shape
    own = k_all // n_ka
    width_cols[...] = column_to_lanes(spread[...] * (-LOG2_E))
    grad_t[...] = jnp.zeros_like(grad_t)

    most = most_steps(atoms)

    def collect(cell):
        scaled = shape_of(cell, quad, width_cols, 0, own) * inverse_count(bounds[0, cell])
        grad_t[...] += scaled * (
            factors[cell, :, :own] * sums[cell, :, :own]
            + factors[cell, :, own : 2 * own] * sums[cell, :, own : 2 * own]
        )

    def gather(cell, before):
        start, steps, _ = span_of(bounds, cell)

        def action(n):
            if before is not None:
                collect(before)
            at = pl.ds(start, n * TILE)
            lhs = mgrad_t[:, at] * (ids[:, at] == cell).astype(F32).astype(BF16)
            sums[cell] = mm(lhs, waves[:, at], 1, 1)

        by_steps(steps, most, action)

    gather(0, None)

    def cell_step(cell, carry):
        gather(cell, cell - 1)
        return carry

    lax.fori_loop(1, cells, cell_step, 0)
    collect(cells - 1)
    result = grad_t[...].T
    filter_grad[...] = result
    filter_half[...] = result.astype(BF16)


def update_kernel(n_ka, *refs):
    bounds, ids, quad, waves, sums, spread = refs[:6]
    update_t = refs[-11]
    filt_t, width_cols, even, odd, total_t, sems = refs[-6:]
    copies = start_copies(sems, *zip(refs[-15:-11], refs[-10:-6]))
    atoms = update_t.shape[1]
    filters_first(filt_t, refs[6:-15])
    width_cols[...] = column_to_lanes(spread[...] * (-LOG2_E))
    spread_cells(n_ka, bounds, ids, quad, filt_t, width_cols, sums, waves, even, odd, total_t)
    update_t[...] = total_t[:, :atoms].astype(BF16)
    for copy in copies:
        copy.wait()


def gradient_kernel(update_t, feats, raw_in_t):
    raw_in_t[...] = mm(update_t[...], feats[...])


def residual_kernel(transposed, base, values_t, weight, out):
    value = mm(values_t[...].T, weight[...], 1, 1 if transposed else 0)
    out[...] = (base[...].astype(F32) + value).astype(BF16)


def residual(transposed, base, values_t, weight):
    rows, chan = base.shape
    step = tile_of(rows, 512)
    by_rows = pl.BlockSpec((step, chan), lambda i: (i, 0))
    return pl.pallas_call(
        functools.partial(residual_kernel, transposed),
        out_shape=jax.ShapeDtypeStruct((rows, chan), BF16),
        grid=(rows // step,),
        in_specs=[
            by_rows,
            pl.BlockSpec((chan, step), lambda i: (0, i)),
            pl.BlockSpec((chan, chan), lambda i: (0, 0)),
        ],
        out_specs=by_rows,
        compiler_params=pltpu.CompilerParams(vmem_limit_bytes=SMALL),
        cost_estimate=pl.CostEstimate(
            flops=2 * FLOPS_PER_MICRO, bytes_accessed=0, transcendentals=0
        ),
    )(base, values_t, weight)


def join_kernel(raw_in_t, raw_out, other_out, pack):
    chan = raw_in_t.shape[0]
    pack[:chan, :] = raw_in_t[...]
    pack[chan:, :] = raw_out[...] + other_out[:chan, :].astype(F32)


def out_kernel(raw_out, other_out, filter_half, out_sum, packed):
    chan = raw_out.shape[0]
    value = raw_out[...] + other_out[:chan, :].astype(F32)
    out_sum[...] = value
    packed[:chan, :] = value.astype(BF16)
    packed[chan:, :] = filter_half[...]


def filter_kernel(*refs):
    own = refs[0].shape[0]
    value = refs[0][...]
    for ref in refs[1:-1]:
        value = value + ref[ref.shape[0] - own :, :].astype(F32)
    refs[-1][...] = value


def squares_kernel(filt, near, f_sum, f_squares):
    value = filt[...] + near[...]
    f_sum[...] = value
    f_squares[...] = jnp.broadcast_to(
        jnp.sum(jnp.sum(value * value, axis=0, keepdims=True), axis=1, keepdims=True),
        f_squares.shape,
    )


def chip_kernel(pack, near, in_sum, in_half, w_sum):
    chan = in_sum.shape[0]
    value = pack[:chan, :] + near[:chan, :]
    in_sum[...] = value
    in_half[...] = value.astype(BF16)
    w_sum[...] = pack[chan:, :] + near[chan:, :]


def total_of(first, others):
    value = first[...]
    for other in others:
        value = value + other[...].astype(F32)
    return value


def add_kernel(first, second, *outs):
    value = first[...] + second[...].astype(F32)
    for out in outs:
        out[...] = value.astype(out.dtype)


def final_kernel(n_chip, n_ka, *refs):
    in_parts = refs[:n_chip]
    raw_out, filt, squares, g_in, g_out, g_filt = refs[n_chip:]
    raw_in = total_of(in_parts[0], in_parts[1:])
    out = raw_out[...]
    both = raw_in * raw_in + out * out
    weight_squares = jnp.sum(jnp.sum(both, axis=0, keepdims=True), axis=1, keepdims=True)
    weight_scale = lax.rsqrt(weight_squares / (2 * raw_in.size) + 1e-06)
    filter_scale = lax.rsqrt(squares[0:1, 0:1] / (n_ka * filt.size) + 1e-06)
    g_in[...] = (raw_in * weight_scale).T
    g_out[...] = out * weight_scale
    g_filt[...] = filt[...] * filter_scale


def call(
    kernel, operands, smem, outs, scratch=(), limit=SMALL, micros=2, space=pltpu.VMEM, smem_outs=0
):
    vmem = pl.BlockSpec(memory_space=pltpu.VMEM)
    rest = len(operands) - smem
    spaces = space if isinstance(space, tuple) else (space,) * rest
    return pl.pallas_call(
        kernel,
        out_shape=tuple(jax.ShapeDtypeStruct(*o) for o in outs),
        in_specs=[pl.BlockSpec(memory_space=x) for x in (pltpu.SMEM,) * smem + spaces],
        out_specs=(vmem,) * (len(outs) - smem_outs)
        + (pl.BlockSpec(memory_space=pltpu.SMEM),) * smem_outs,
        scratch_shapes=list(scratch),
        compiler_params=pltpu.CompilerParams(vmem_limit_bytes=limit),
        cost_estimate=pl.CostEstimate(
            flops=micros * FLOPS_PER_MICRO, bytes_accessed=0, transcendentals=0
        ),
    )(*operands)


def in_hbm(value):
    return pltpu.with_memory_space_constraint(value, pltpu.HBM)


def send(value, axis, step):
    return lax.ppermute(value, axis, routes(step, lax.axis_size(axis)))


def doubling(first, size):
    return [first << i for i in range(size.bit_length()) if first << i < size]


def block(feats, coords, cell_ids, recip, kvec, w_in, w_out, kfilt, spread, cotan):
    n_ka = lax.axis_size("ka")
    n_dp = lax.axis_size("dp")
    atoms, chan = feats.shape
    own = kvec.shape[1]
    k_all = own * n_ka
    cells = recip.shape[1]
    long = atoms + LANES
    recip, spread = recip[0], spread[None]
    chips = range(2, n_dp, 2)
    vm = pltpu.VMEM
    dma = pltpu.SemaphoreType.DMA
    near_kvec = send(kvec[None], "ka", 1)
    near_kfilt = send(kfilt[None], "ka", 1)
    first, ids, coords, recip, kvec, kfilt, bounds = call(
        prepare_kernel,
        [in_hbm(x) for x in (coords, cell_ids, recip, kvec, kfilt)],
        0,
        [
            ((2 * own, long), BF16),
            ((1, long), jnp.int32),
            (coords.shape, F32),
            (recip.shape, F32),
            (kvec.shape, jnp.int32),
            (kfilt.shape, F32),
            ((2, cells), jnp.int32),
        ],
        [vm((own, 8), F32), dma((5,))],
        SMALL,
        3,
        pltpu.HBM,
        smem_outs=1,
    )
    kfilt = kfilt[None]
    (kvecs,) = call(pair_kernel, (kvec[None], near_kvec), 0, [((2, 8, own), F32)])
    far_kvecs, far_kfilts = [kvecs], [kfilt, near_kfilt]
    ka_steps = doubling(2, n_ka)
    for s in ka_steps:
        if s > 2:
            (kvecs,) = call(pair_kernel, (kvecs, far_kvecs[-1]), 0, [((s, 8, own), F32)])
        far_kvecs.append(send(kvecs, "ka", s))
    second, proj_t = call(
        project_kernel,
        (coords, far_kvecs[0], in_hbm(feats), in_hbm(w_in)),
        0,
        [((2 * own, long), BF16), ((chan, long), BF16)],
        [vm((atoms, chan), BF16), vm((chan, chan), BF16), vm((own, 8), F32), dma((2,))],
        SMALL,
        3,
        (pltpu.VMEM, pltpu.VMEM, pltpu.HBM, pltpu.HBM),
    )
    kfilts = kfilt
    for s in ka_steps:
        (kfilts,) = call(stack_kernel, (kfilts, far_kfilts[-1]), 0, [((s, own, chan), BF16)])
        far_kfilts.append(send(kfilts, "ka", s))
    waves, factors, quad = call(
        functools.partial(waves_kernel, n_ka),
        (bounds, first, second, proj_t, ids, coords, recip, *far_kvecs),
        1,
        [((2 * k_all, long), BF16), ((cells, chan, 2 * k_all), F32), ((cells, k_all), F32)],
        [vm((k_all - 2 * own, 8), F32)],
        LIMIT,
        8,
    )
    halves = [vm((chan, 2 * k_all), BF16)] * 2
    act_t, mgrad_t, raw_out, raw_half = call(
        functools.partial(message_kernel, n_ka),
        (bounds, ids, quad, waves, factors, spread, cotan, w_out, *far_kfilts),
        1,
        [((chan, atoms), BF16), ((chan, long), BF16), ((chan, chan), F32), ((chan, chan), BF16)],
        [vm((chan, k_all), F32), vm((chan, 8), F32), *halves, vm((chan, long), F32)],
        LIMIT,
        8,
    )
    out_steps = doubling(2, n_dp)
    out_part = send(raw_half, "dp", out_steps[0])
    sums, filter_grad, filter_half = call(
        functools.partial(adjoint_kernel, n_ka),
        (bounds, ids, quad, waves, factors, mgrad_t, spread),
        1,
        [((cells, chan, 2 * k_all), F32), ((own, chan), F32), ((own, chan), BF16)],
        [vm((chan, 8), F32), vm((chan, own), F32)],
        LIMIT,
        6,
    )
    raw_out, packed = call(
        out_kernel,
        (raw_out, out_part, filter_half),
        0,
        [((chan, chan), F32), ((chan + own, chan), BF16)],
    )
    filt_parts = [send(packed if s == 4 else filter_half, "dp", s) for s in chips]
    out_part = filt_parts[1]
    for s in out_steps[2:]:
        raw_out, raw_half = call(
            out_kernel,
            (raw_out, out_part, filter_half),
            0,
            [((chan, chan), F32), ((chan + own, chan), BF16)],
        )
        out_part = send(raw_half, "dp", s)
    held = (feats, cotan, w_in, w_out)
    update_t, feats, cotan, w_in, w_out = call(
        functools.partial(update_kernel, n_ka),
        (bounds, ids, quad, waves, sums, spread, *far_kfilts, *map(in_hbm, held)),
        1,
        [((chan, atoms), BF16), *((x.shape, BF16) for x in held)],
        [vm((chan, k_all), F32), vm((chan, 8), F32), *halves, vm((chan, long), F32), dma((4,))],
        LIMIT,
        8,
        (pltpu.VMEM,) * (5 + len(far_kfilts)) + (pltpu.HBM,) * 4,
    )
    (filt_sum,) = call(filter_kernel, (filter_grad, *filt_parts), 0, [((own, chan), F32)])
    filt_near = send(filt_sum, "dp", 1)
    (raw_in_t,) = call(gradient_kernel, (update_t, feats), 0, [((chan, chan), F32)])
    (pack,) = call(join_kernel, (raw_in_t, raw_out, out_part), 0, [((2 * chan, chan), F32)])
    near = send(pack, "dp", 1)
    f_sum, squares = call(
        squares_kernel, (filt_sum, filt_near), 0, [((own, chan), F32), ((8, LANES), F32)]
    )
    square_steps = doubling(1, n_ka)
    square_part = send(squares, "ka", square_steps[0])
    feat_grad = residual(True, cotan, update_t, w_in)
    in_sum, in_half, w_sum = call(
        chip_kernel,
        (pack, near),
        0,
        [((chan, chan), F32), ((chan, chan), BF16), ((chan, chan), F32)],
    )
    in_parts = [in_sum] + [send(in_half, "dp", s) for s in chips]
    for s in square_steps[1:] + [0]:
        (squares,) = call(add_kernel, (squares, square_part), 0, [((8, LANES), F32)])
        if s:
            square_part = send(squares, "ka", s)
    mixed = residual(False, feats, act_t, w_out)
    grads = call(
        functools.partial(final_kernel, len(in_parts), n_ka),
        (*in_parts, w_sum, f_sum, squares),
        0,
        [((chan, chan), F32), ((chan, chan), F32), ((own, chan), F32)],
    )
    return (mixed, feat_grad, *grads)


def solution(mesh):
    placed = (
        P("dp", None),
        P(None, "dp"),
        P("dp", None),
        P("dp", None, None),
        P(None, "ka"),
        P(),
        P(),
        P("ka", None),
        P(),
        P("dp", None),
    )
    return jax.shard_map(
        block,
        mesh=mesh,
        in_specs=placed,
        out_specs=(P("dp", None), P("dp", None), P(), P(), P("ka", None)),
        check_vma=False,
    )
```

```python
import functools

import jax
import jax.numpy as jnp
from jax import lax
from jax.experimental import pallas as pl
from jax.experimental.pallas import tpu as pltpu
from jax.sharding import PartitionSpec as P


F32 = jnp.float32
BF16 = jnp.bfloat16
LANES = 128
TILE = 256
MOST = 1024
LIMIT = 24 << 20
SMALL = 6 << 20
FLOPS_PER_MICRO = 1 << 30
LOG2_E = 1.4426950408889634
COS_TERMS = (
    0.9999999890590228,
    -19.73920449945383,
    64.93911745989081,
    -85.45013953079767,
    60.167630950263465,
    -25.967599245923743,
    6.52865815775625,
)
SIN_TERMS = (
    6.283184916495428,
    -41.34158923268831,
    81.59994332977429,
    -76.61447253115396,
    41.34288235413569,
    -12.471243534350362,
)
ROUNDER = 12582912.0


def mm(lhs, rhs, lhs_dim=1, rhs_dim=0):
    return lax.dot_general(
        lhs, rhs, (((lhs_dim,), (rhs_dim,)), ((), ())), preferred_element_type=F32
    )


def horner(terms, square):
    value = terms[-1] * square + terms[-2]
    for term in terms[-3::-1]:
        value = value * square + term
    return value


def routes(step, count):
    if count & (count - 1) == 0:
        return [(i, i ^ step) for i in range(count)]
    return [(i, (i + step) % count) for i in range(count)]


def tile_of(size, most):
    tile = most
    while size % tile:
        tile //= 2
    return tile


def column_to_lanes(row):
    return jnp.broadcast_to(row, (8, row.shape[1])).T


def span_of(bounds, cell):
    first = bounds[1, cell]
    start = lax.div(first, LANES) * LANES
    count = bounds[0, cell]
    steps = lax.div(first - start + count + (TILE - 1), TILE)
    return pl.multiple_of(start, LANES), steps, count


def most_steps(atoms):
    return -(-(min(MOST, atoms) + LANES - 1) // TILE)


def by_steps(steps, most, action):
    for n in range(1, most + 1):
        pl.when(steps == n)(functools.partial(action, n))


def weigh(cell, n_ka, bounds, quad, filt_t, width_cols, sums, weights):
    own = filt_t.shape[1] // n_ka
    inverse = inverse_count(bounds[0, cell])
    for j in range(n_ka):
        scaled = shape_of(cell, quad, width_cols, j * own, own) * inverse
        filt = filt_t[:, own * j : own * (j + 1)] * scaled
        for half in (2 * j, 2 * j + 1):
            at = slice(own * half, own * (half + 1))
            weights[:, at] = (filt * sums[cell, :, at]).astype(BF16)


def spread_cells(n_ka, bounds, ids, quad, filt_t, width_cols, sums, waves, even, odd, out):
    cells = quad.shape[0]
    most = most_steps(out.shape[1] - LANES)

    def one(cell, weights, after, target):
        start, steps, _ = span_of(bounds, cell)

        def action(n):
            if after is not None:
                weigh(after, n_ka, bounds, quad, filt_t, width_cols, sums, target)
            for t in range(n):
                at = pl.ds(pl.multiple_of(start + t * TILE, LANES), TILE)
                value = mm(weights[...], waves[:, at])
                out[:, at] = jnp.where(ids[:, at] == cell, value, out[:, at])

        by_steps(steps, most, action)

    weigh(0, n_ka, bounds, quad, filt_t, width_cols, sums, even)

    def two(i, carry):
        one(2 * i, even, jnp.minimum(2 * i + 1, cells - 1), odd)
        one(2 * i + 1, odd, jnp.minimum(2 * i + 2, cells - 1), even)
        return carry

    lax.fori_loop(0, cells // 2, two, 0)
    if cells % 2:
        one(cells - 1, even, None, None)


def inverse_count(count):
    return 1.0 / jnp.full((1, 1), count, jnp.int32).astype(F32)


def shape_of(cell, quad, width_cols, first, size):
    exponent = quad[pl.ds(cell, 1), :][:, first : first + size] * width_cols[:, 0:1]
    return jnp.exp2(exponent)


def fill_slice(waves, base, own, kcols, first, row, coords):
    atoms = coords.shape[1]
    wide = tile_of(atoms, 1024)
    row = pl.multiple_of(row, 16)
    kv = kcols[pl.ds(pl.multiple_of(first + row, 16), 16), :]
    for start in range(0, atoms, wide):
        frac = coords[:, start : start + wide]
        turns = kv[:, 0:1] * frac[0:1, :] + kv[:, 1:2] * frac[1:2, :]
        turns = turns + kv[:, 2:3] * frac[2:3, :]
        turns = turns - ((turns + ROUNDER) - ROUNDER)
        square = turns * turns
        waves[pl.ds(pl.multiple_of(base + row, 16), 16), start : start + wide] = horner(
            COS_TERMS, square
        ).astype(BF16)
        waves[pl.ds(pl.multiple_of(base + own + row, 16), 16), start : start + wide] = (
            horner(SIN_TERMS, square) * turns
        ).astype(BF16)


def rows_of_share(index, shares, own):
    each = -(-own // (16 * shares))
    return [16 * jnp.minimum(index * each + p, own // 16 - 1) for p in range(each)]


def vector_columns(kvec):
    rows = kvec[...].astype(F32)
    if rows.shape[0] == 3:
        rows = jnp.concatenate([rows, jnp.zeros((5, rows.shape[1]), F32)], axis=0)
    return rows.T


def start_copies(sems, *moves):
    copies = [pltpu.make_async_copy(a, b, sems.at[i]) for i, (a, b) in enumerate(moves)]
    for copy in copies:
        copy.start()
    return copies


def prepare_kernel(
    coords_hbm, ids_hbm, recip_hbm, kvec_hbm, kfilt_hbm,
    waves, ids, coords, recip, kvec, kfilt, bounds, kcols, sems,
):
    atoms = coords.shape[1]
    own = kvec.shape[1]
    copies = start_copies(
        sems,
        (kvec_hbm, kvec),
        (coords_hbm, coords),
        (ids_hbm, ids.at[:, :atoms]),
        (recip_hbm, recip),
        (kfilt_hbm, kfilt),
    )
    ids[:, atoms:] = jnp.full((1, LANES), -1, jnp.int32)
    waves[:, atoms:] = jnp.zeros((waves.shape[0], LANES), BF16)
    for copy in copies[:3]:
        copy.wait()
    kcols[...] = vector_columns(kvec)
    fill_slice(waves, 0, own, kcols, 0, 0, coords)
    numbers = ids[:, :atoms]
    before = 0
    for cell in range(bounds.shape[1]):
        count = jnp.sum((numbers == cell).astype(F32)).astype(jnp.int32)
        bounds[0, cell] = count
        bounds[1, cell] = before
        before = before + count

    def phase_rows(i, carry):
        fill_slice(waves, 0, own, kcols, 0, 16 * i, coords)
        return carry

    lax.fori_loop(1, own // 16, phase_rows, 0)
    for copy in copies[3:]:
        copy.wait()


def pair_kernel(kvec, other_kvec, kvecs):
    count = kvec.shape[0]
    for j in range(count):
        for at, source in ((j, kvec), (j + count, other_kvec)):
            rows = source[j].astype(F32)
            if rows.shape[0] == 3:
                rows = jnp.concatenate([rows, jnp.zeros((5, rows.shape[1]), F32)], axis=0)
            kvecs[at] = rows


def stack_kernel(near, far, out):
    count = near.shape[0]
    out[:count] = near[...].astype(out.dtype)
    out[count:] = far[...].astype(out.dtype)


def project_kernel(coords, kvecs, feats_hbm, w_in_hbm, waves, proj_t, feats, w_in, kcols, sems):
    atoms, chan = feats.shape
    own = kcols.shape[0]
    copies = start_copies(sems, (w_in_hbm, w_in), (feats_hbm, feats))
    waves[:, atoms:] = jnp.zeros((waves.shape[0], LANES), BF16)
    proj_t[:, atoms:] = jnp.zeros((chan, LANES), BF16)
    kcols[...] = vector_columns(kvecs.at[1])
    for copy in copies:
        copy.wait()
    tiles = atoms // TILE

    def project(t, carry):
        at = pl.ds(pl.multiple_of(t * TILE, TILE), TILE)
        proj_t[:, at] = mm(w_in[...], feats[at, :], 0, 1).astype(BF16)
        for row in rows_of_share(t, tiles, own):
            fill_slice(waves, 0, own, kcols, 0, row, coords)
        return carry

    lax.fori_loop(0, tiles, project, 0)


def waves_kernel(n_ka, *refs):
    bounds, first, second, proj_t, ids, coords, recip = refs[:7]
    waves, factors, quad, kcols = refs[-4:]
    kvecs = [ref.at[j] for ref in refs[7:-4] for j in range(ref.shape[0])]
    atoms = coords.shape[1]
    own = kvecs[0].shape[1]
    cells = recip.shape[0]
    most = most_steps(atoms)
    for j in range(2, n_ka):
        kcols[(j - 2) * own : (j - 1) * own, :] = vector_columns(kvecs[j])
    for j in range(n_ka):
        rows = kvecs[j][...]
        squared = jnp.zeros((cells, own), F32)
        for r in range(3):
            part = recip[:, 3 * r : 3 * r + 1] * rows[0:1, :]
            part = part + recip[:, 3 * r + 1 : 3 * r + 2] * rows[1:2, :]
            part = part + recip[:, 3 * r + 2 : 3 * r + 3] * rows[2:3, :]
            squared = squared + part * part
        quad[:, own * j : own * (j + 1)] = squared
    waves[4 * own :, atoms:] = jnp.zeros((2 * own * (n_ka - 2), LANES), BF16)

    def early(cell, carry):
        start, steps, _ = span_of(bounds, cell)

        def action(n):
            at = pl.ds(start, n * TILE)
            lhs = proj_t[:, at] * (ids[:, at] == cell).astype(F32).astype(BF16)
            factors[cell, :, : 2 * own] = mm(lhs, first[:, at], 1, 1)
            factors[cell, :, 2 * own : 4 * own] = mm(lhs, second[:, at], 1, 1)
            for j in range(2, n_ka):
                for row in rows_of_share(cell, cells, own):
                    fill_slice(waves, 2 * own * j, own, kcols, (j - 2) * own, row, coords)
            for row in rows_of_share(cell, cells, 2 * own):
                from_rows = pl.ds(pl.multiple_of(row, 16), 16)
                waves[from_rows, :] = first[from_rows, :]
                waves[pl.ds(pl.multiple_of(2 * own + row, 16), 16), :] = second[from_rows, :]

        by_steps(steps, most, action)
        return carry

    lax.fori_loop(0, cells, early, 0)

    def late(cell, carry):
        start, steps, _ = span_of(bounds, cell)

        def action(n):
            at = pl.ds(start, n * TILE)
            lhs = proj_t[:, at] * (ids[:, at] == cell).astype(F32).astype(BF16)
            factors[cell, :, 4 * own :] = mm(lhs, waves[4 * own :, at], 1, 1)

        by_steps(steps, most, action)
        return carry

    lax.fori_loop(0, cells, late, 0)


def filters_first(filt_t, kfilts):
    chunk = 0
    for ref in kfilts:
        own = ref.shape[1]
        for j in range(ref.shape[0]):
            filt_t[:, chunk * own : (chunk + 1) * own] = ref[j].astype(F32).T
            chunk += 1
    return own


def message_kernel(n_ka, *refs):
    bounds, ids, quad, waves, factors, spread, cotan, w_out = refs[:8]
    act_t, mgrad_t, raw_out, raw_half, filt_t, width_cols, even, odd, mess_t = refs[-9:]
    atoms, chan = cotan.shape
    filters_first(filt_t, refs[8:-9])
    width_cols[...] = column_to_lanes(spread[...] * (-LOG2_E))
    spread_cells(n_ka, bounds, ids, quad, filt_t, width_cols, factors, waves, even, odd, mess_t)
    mgrad_t[:, atoms:] = jnp.zeros((chan, LANES), BF16)
    raw_out[...] = jnp.zeros_like(raw_out)

    wide = tile_of(atoms, 2 * TILE)

    def middle(t, carry):
        at = pl.ds(pl.multiple_of(t * wide, wide), wide)
        message = mess_t[:, at]
        sigma = jax.nn.sigmoid(message)
        activated = (message * sigma).astype(BF16)
        act_t[:, at] = activated
        cot = cotan[at, :]
        act_grad = mm(w_out[...], cot, 1, 1)
        mgrad_t[:, at] = (act_grad * (sigma * (1.0 + message * (1.0 - sigma)))).astype(BF16)
        raw_out[...] += mm(activated, cot)
        return carry

    lax.fori_loop(0, atoms // wide, middle, 0)
    raw_half[...] = raw_out[...].astype(BF16)


def adjoint_kernel(n_ka, *refs):
    bounds, ids, quad, waves, factors, mgrad_t, spread = refs[:7]
    sums, filter_grad, filter_half, width_cols, grad_t = refs[7:]
    atoms = mgrad_t.shape[1] - LANES
    cells, k_all = quad.shape
    own = k_all // n_ka
    width_cols[...] = column_to_lanes(spread[...] * (-LOG2_E))
    grad_t[...] = jnp.zeros_like(grad_t)

    most = most_steps(atoms)

    def collect(cell):
        scaled = shape_of(cell, quad, width_cols, 0, own) * inverse_count(bounds[0, cell])
        grad_t[...] += scaled * (
            factors[cell, :, :own] * sums[cell, :, :own]
            + factors[cell, :, own : 2 * own] * sums[cell, :, own : 2 * own]
        )

    def gather(cell, before):
        start, steps, _ = span_of(bounds, cell)

        def action(n):
            if before is not None:
                collect(before)
            at = pl.ds(start, n * TILE)
            lhs = mgrad_t[:, at] * (ids[:, at] == cell).astype(F32).astype(BF16)
            sums[cell] = mm(lhs, waves[:, at], 1, 1)

        by_steps(steps, most, action)

    gather(0, None)

    def cell_step(cell, carry):
        gather(cell, cell - 1)
        return carry

    lax.fori_loop(1, cells, cell_step, 0)
    collect(cells - 1)
    result = grad_t[...].T
    filter_grad[...] = result
    filter_half[...] = result.astype(BF16)


def update_kernel(n_ka, *refs):
    bounds, ids, quad, waves, sums, spread = refs[:6]
    update_t = refs[-11]
    filt_t, width_cols, even, odd, total_t, sems = refs[-6:]
    copies = start_copies(sems, *zip(refs[-15:-11], refs[-10:-6]))
    atoms = update_t.shape[1]
    filters_first(filt_t, refs[6:-15])
    width_cols[...] = column_to_lanes(spread[...] * (-LOG2_E))
    spread_cells(n_ka, bounds, ids, quad, filt_t, width_cols, sums, waves, even, odd, total_t)
    update_t[...] = total_t[:, :atoms].astype(BF16)
    for copy in copies:
        copy.wait()


def gradient_kernel(update_t, feats, raw_in_t):
    raw_in_t[...] = mm(update_t[...], feats[...])


def residual_kernel(transposed, base, values_t, weight, out_hbm, out, sems):
    rows = base.shape[0]
    step = tile_of(rows, 512)
    copies = []
    for t in range(rows // step):
        at = slice(t * step, (t + 1) * step)
        value = mm(values_t[:, at].T, weight[...], 1, 1 if transposed else 0)
        out[at, :] = (base[at, :].astype(F32) + value).astype(BF16)
        copies.append(pltpu.make_async_copy(out.at[at, :], out_hbm.at[at, :], sems.at[t]))
        copies[-1].start()
    for copy in copies:
        copy.wait()


def residual(transposed, base, values_t, weight):
    rows, chan = base.shape
    vmem = pl.BlockSpec(memory_space=pltpu.VMEM)
    return pl.pallas_call(
        functools.partial(residual_kernel, transposed),
        out_shape=jax.ShapeDtypeStruct((rows, chan), BF16),
        in_specs=[vmem] * 3,
        out_specs=pl.BlockSpec(memory_space=pltpu.HBM),
        scratch_shapes=[
            pltpu.VMEM((rows, chan), BF16),
            pltpu.SemaphoreType.DMA((rows // tile_of(rows, 512),)),
        ],
        compiler_params=pltpu.CompilerParams(vmem_limit_bytes=SMALL),
        cost_estimate=pl.CostEstimate(
            flops=2 * FLOPS_PER_MICRO, bytes_accessed=0, transcendentals=0
        ),
    )(base, values_t, weight)


def last_out_kernel(raw_out, other_out, out_sum):
    out_sum[...] = raw_out[...] + other_out[: raw_out.shape[0], :].astype(F32)


def out_kernel(raw_out, other_out, filter_half, out_sum, packed):
    chan = raw_out.shape[0]
    value = raw_out[...] + other_out[:chan, :].astype(F32)
    out_sum[...] = value
    packed[:chan, :] = value.astype(BF16)
    packed[chan:, :] = filter_half[...]


def filter_kernel(*refs):
    own = refs[0].shape[0]
    value = refs[0][...]
    for ref in refs[1:-1]:
        value = value + ref[ref.shape[0] - own :, :].astype(F32)
    refs[-1][...] = value


def squares_kernel(filt, near, f_sum, f_squares):
    value = filt[...] + near[...]
    f_sum[...] = value
    f_squares[...] = jnp.broadcast_to(
        jnp.sum(jnp.sum(value * value, axis=0, keepdims=True), axis=1, keepdims=True),
        f_squares.shape,
    )


def chip_kernel(raw_in_t, near, in_sum, in_half):
    value = raw_in_t[...] + near[...]
    in_sum[...] = value
    in_half[...] = value.astype(BF16)


def total_of(first, others):
    value = first[...]
    for other in others:
        value = value + other[...].astype(F32)
    return value


def add_kernel(first, second, *outs):
    value = first[...] + second[...].astype(F32)
    for out in outs:
        out[...] = value.astype(out.dtype)


def final_kernel(n_chip, n_ka, *refs):
    in_parts = refs[:n_chip]
    raw_out, near_out, filt, squares, g_in, g_out, g_filt = refs[n_chip:]
    raw_in = total_of(in_parts[0], in_parts[1:])
    out = raw_out[...] + near_out[...]
    both = raw_in * raw_in + out * out
    weight_squares = jnp.sum(jnp.sum(both, axis=0, keepdims=True), axis=1, keepdims=True)
    weight_scale = lax.rsqrt(weight_squares / (2 * raw_in.size) + 1e-06)
    filter_scale = lax.rsqrt(squares[0:1, 0:1] / (n_ka * filt.size) + 1e-06)
    g_in[...] = (raw_in * weight_scale).T
    g_out[...] = out * weight_scale
    g_filt[...] = filt[...] * filter_scale


def call(
    kernel, operands, smem, outs, scratch=(), limit=SMALL, micros=2, space=pltpu.VMEM, smem_outs=0
):
    vmem = pl.BlockSpec(memory_space=pltpu.VMEM)
    rest = len(operands) - smem
    spaces = space if isinstance(space, tuple) else (space,) * rest
    return pl.pallas_call(
        kernel,
        out_shape=tuple(jax.ShapeDtypeStruct(*o) for o in outs),
        in_specs=[pl.BlockSpec(memory_space=x) for x in (pltpu.SMEM,) * smem + spaces],
        out_specs=(vmem,) * (len(outs) - smem_outs)
        + (pl.BlockSpec(memory_space=pltpu.SMEM),) * smem_outs,
        scratch_shapes=list(scratch),
        compiler_params=pltpu.CompilerParams(vmem_limit_bytes=limit),
        cost_estimate=pl.CostEstimate(
            flops=micros * FLOPS_PER_MICRO, bytes_accessed=0, transcendentals=0
        ),
    )(*operands)


def in_hbm(value):
    return pltpu.with_memory_space_constraint(value, pltpu.HBM)


def send(value, axis, step):
    return lax.ppermute(value, axis, routes(step, lax.axis_size(axis)))


def doubling(first, size):
    return [first << i for i in range(size.bit_length()) if first << i < size]


def block(feats, coords, cell_ids, recip, kvec, w_in, w_out, kfilt, spread, cotan):
    n_ka = lax.axis_size("ka")
    n_dp = lax.axis_size("dp")
    atoms, chan = feats.shape
    own = kvec.shape[1]
    k_all = own * n_ka
    cells = recip.shape[1]
    long = atoms + LANES
    recip, spread = recip[0], spread[None]
    chips = range(2, n_dp, 2)
    vm = pltpu.VMEM
    dma = pltpu.SemaphoreType.DMA
    near_kvec = send(kvec[None], "ka", 1)
    near_kfilt = send(kfilt[None], "ka", 1)
    first, ids, coords, recip, kvec, kfilt, bounds = call(
        prepare_kernel,
        [in_hbm(x) for x in (coords, cell_ids, recip, kvec, kfilt)],
        0,
        [
            ((2 * own, long), BF16),
            ((1, long), jnp.int32),
            (coords.shape, F32),
            (recip.shape, F32),
            (kvec.shape, jnp.int32),
            (kfilt.shape, F32),
            ((2, cells), jnp.int32),
        ],
        [vm((own, 8), F32), dma((5,))],
        SMALL,
        3,
        pltpu.HBM,
        smem_outs=1,
    )
    kfilt = kfilt[None]
    (kvecs,) = call(pair_kernel, (kvec[None], near_kvec), 0, [((2, 8, own), F32)])
    far_kvecs, far_kfilts = [kvecs], [kfilt, near_kfilt]
    ka_steps = doubling(2, n_ka)
    for s in ka_steps:
        if s > 2:
            (kvecs,) = call(pair_kernel, (kvecs, far_kvecs[-1]), 0, [((s, 8, own), F32)])
        far_kvecs.append(send(kvecs, "ka", s))
    second, proj_t = call(
        project_kernel,
        (coords, far_kvecs[0], in_hbm(feats), in_hbm(w_in)),
        0,
        [((2 * own, long), BF16), ((chan, long), BF16)],
        [vm((atoms, chan), BF16), vm((chan, chan), BF16), vm((own, 8), F32), dma((2,))],
        SMALL,
        3,
        (pltpu.VMEM, pltpu.VMEM, pltpu.HBM, pltpu.HBM),
    )
    kfilts = kfilt
    for s in ka_steps:
        (kfilts,) = call(stack_kernel, (kfilts, far_kfilts[-1]), 0, [((s, own, chan), F32)])
        far_kfilts.append(send(kfilts, "ka", s))
    waves, factors, quad = call(
        functools.partial(waves_kernel, n_ka),
        (bounds, first, second, proj_t, ids, coords, recip, *far_kvecs),
        1,
        [((2 * k_all, long), BF16), ((cells, chan, 2 * k_all), F32), ((cells, k_all), F32)],
        [vm((k_all - 2 * own, 8), F32)],
        LIMIT,
        8,
    )
    halves = [vm((chan, 2 * k_all), BF16)] * 2
    act_t, mgrad_t, raw_out, raw_half = call(
        functools.partial(message_kernel, n_ka),
        (bounds, ids, quad, waves, factors, spread, cotan, w_out, *far_kfilts),
        1,
        [((chan, atoms), BF16), ((chan, long), BF16), ((chan, chan), F32), ((chan, chan), BF16)],
        [vm((chan, k_all), F32), vm((chan, 8), F32), *halves, vm((chan, long), F32)],
        LIMIT,
        8,
    )
    out_steps = doubling(2, n_dp)
    out_part = send(raw_half, "dp", out_steps[0])
    sums, filter_grad, filter_half = call(
        functools.partial(adjoint_kernel, n_ka),
        (bounds, ids, quad, waves, factors, mgrad_t, spread),
        1,
        [((cells, chan, 2 * k_all), F32), ((own, chan), F32), ((own, chan), BF16)],
        [vm((chan, 8), F32), vm((chan, own), F32)],
        LIMIT,
        6,
    )
    raw_out, packed = call(
        out_kernel,
        (raw_out, out_part, filter_half),
        0,
        [((chan, chan), F32), ((chan + own, chan), BF16)],
    )
    filt_parts = [send(packed if s == 4 else filter_half, "dp", s) for s in chips]
    out_part = filt_parts[1]
    for s in out_steps[2:]:
        raw_out, raw_half = call(
            out_kernel,
            (raw_out, out_part, filter_half),
            0,
            [((chan, chan), F32), ((chan + own, chan), BF16)],
        )
        out_part = send(raw_half, "dp", s)
    held = (feats, cotan, w_in, w_out)
    update_t, feats, cotan, w_in, w_out = call(
        functools.partial(update_kernel, n_ka),
        (bounds, ids, quad, waves, sums, spread, *far_kfilts, *map(in_hbm, held)),
        1,
        [((chan, atoms), BF16), *((x.shape, BF16) for x in held)],
        [vm((chan, k_all), F32), vm((chan, 8), F32), *halves, vm((chan, long), F32), dma((4,))],
        LIMIT,
        8,
        (pltpu.VMEM,) * (5 + len(far_kfilts)) + (pltpu.HBM,) * 4,
    )
    (filt_sum,) = call(filter_kernel, (filter_grad, *filt_parts), 0, [((own, chan), F32)])
    filt_near = send(filt_sum, "dp", 1)
    (raw_in_t,) = call(gradient_kernel, (update_t, feats), 0, [((chan, chan), F32)])
    near = send(raw_in_t, "dp", 1)
    (out_sum,) = call(last_out_kernel, (raw_out, out_part), 0, [((chan, chan), F32)])
    f_sum, squares = call(
        squares_kernel, (filt_sum, filt_near), 0, [((own, chan), F32), ((8, LANES), F32)]
    )
    square_steps = doubling(1, n_ka)
    square_part = send(squares, "ka", square_steps[0])
    feat_grad = residual(True, cotan, update_t, w_in)
    in_sum, in_half = call(
        chip_kernel, (raw_in_t, near), 0, [((chan, chan), F32), ((chan, chan), BF16)]
    )
    in_parts = [in_sum] + [send(in_half, "dp", s) for s in chips]
    for s in square_steps[1:] + [0]:
        (squares,) = call(add_kernel, (squares, square_part), 0, [((8, LANES), F32)])
        if s:
            square_part = send(squares, "ka", s)
    near_out = send(out_sum, "dp", 1)
    mixed = residual(False, feats, act_t, w_out)
    grads = call(
        functools.partial(final_kernel, len(in_parts), n_ka),
        (*in_parts, out_sum, near_out, f_sum, squares),
        0,
        [((chan, chan), F32), ((chan, chan), F32), ((own, chan), F32)],
    )
    return (mixed, feat_grad, *grads)


def solution(mesh):
    placed = (
        P("dp", None),
        P(None, "dp"),
        P("dp", None),
        P("dp", None, None),
        P(None, "ka"),
        P(),
        P(),
        P("ka", None),
        P(),
        P("dp", None),
    )
    return jax.shard_map(
        block,
        mesh=mesh,
        in_specs=placed,
        out_specs=(P("dp", None), P("dp", None), P(), P(), P("ka", None)),
        check_vma=False,
    )
```

```python
import functools

import jax
import jax.numpy as jnp
from jax import lax
from jax.experimental import pallas as pl
from jax.experimental.pallas import tpu as pltpu
from jax.sharding import PartitionSpec as P


F32 = jnp.float32
BF16 = jnp.bfloat16
LANES = 128
TILE = 256
MOST = 1024
LIMIT = 24 << 20
SMALL = 6 << 20
FLOPS_PER_MICRO = 1 << 30
LOG2_E = 1.4426950408889634
COS_TERMS = (
    0.9999999890590228,
    -19.73920449945383,
    64.93911745989081,
    -85.45013953079767,
    60.167630950263465,
    -25.967599245923743,
    6.52865815775625,
)
SIN_TERMS = (
    6.283184916495428,
    -41.34158923268831,
    81.59994332977429,
    -76.61447253115396,
    41.34288235413569,
    -12.471243534350362,
)
ROUNDER = 12582912.0


def mm(lhs, rhs, lhs_dim=1, rhs_dim=0):
    return lax.dot_general(
        lhs, rhs, (((lhs_dim,), (rhs_dim,)), ((), ())), preferred_element_type=F32
    )


def horner(terms, square):
    value = terms[-1] * square + terms[-2]
    for term in terms[-3::-1]:
        value = value * square + term
    return value


def routes(step, count):
    if count & (count - 1) == 0:
        return [(i, i ^ step) for i in range(count)]
    return [(i, (i + step) % count) for i in range(count)]


def tile_of(size, most):
    tile = most
    while size % tile:
        tile //= 2
    return tile


def column_to_lanes(row):
    return jnp.broadcast_to(row, (8, row.shape[1])).T


def span_of(bounds, cell):
    first = bounds[1, cell]
    start = lax.div(first, LANES) * LANES
    count = bounds[0, cell]
    steps = lax.div(first - start + count + (TILE - 1), TILE)
    return pl.multiple_of(start, LANES), steps, count


def most_steps(atoms):
    return -(-(min(MOST, atoms) + LANES - 1) // TILE)


def by_steps(steps, most, action):
    for n in range(1, most + 1):
        pl.when(steps == n)(functools.partial(action, n))


def lanes_of(sums, cell, half, own):
    for ref in sums:
        held = ref.shape[2] // own
        if half < held:
            return ref[cell, :, own * half : own * (half + 1)]
        half -= held


def weigh(cell, n_ka, bounds, quad, filt_t, width_cols, sums, weights):
    own = filt_t.shape[1] // n_ka
    inverse = inverse_count(bounds[0, cell])
    for j in range(n_ka):
        scaled = shape_of(cell, quad, width_cols, j * own, own) * inverse
        filt = filt_t[:, own * j : own * (j + 1)] * scaled
        for half in (2 * j, 2 * j + 1):
            weights[half] = (filt * lanes_of(sums, cell, half, own)).astype(BF16)


def spread_cells(n_ka, bounds, ids, quad, filt_t, width_cols, sums, waves, even, odd, out):
    cells = quad.shape[0]
    most = most_steps(out.shape[1] - LANES)

    def one(cell, weights, after, target):
        start, steps, _ = span_of(bounds, cell)

        def action(n):
            if after is not None:
                weigh(after, n_ka, bounds, quad, filt_t, width_cols, sums, target)
            lhs = jnp.concatenate([weights[h] for h in range(2 * n_ka)], axis=1)
            for t in range(n):
                at = pl.ds(pl.multiple_of(start + t * TILE, LANES), TILE)
                value = mm(lhs, waves[:, at])
                out[:, at] = jnp.where(ids[:, at] == cell, value, out[:, at])

        by_steps(steps, most, action)

    weigh(0, n_ka, bounds, quad, filt_t, width_cols, sums, even)

    def two(i, carry):
        one(2 * i, even, jnp.minimum(2 * i + 1, cells - 1), odd)
        one(2 * i + 1, odd, jnp.minimum(2 * i + 2, cells - 1), even)
        return carry

    lax.fori_loop(0, cells // 2, two, 0)
    if cells % 2:
        one(cells - 1, even, None, None)


def inverse_count(count):
    return 1.0 / jnp.full((1, 1), count, jnp.int32).astype(F32)


def shape_of(cell, quad, width_cols, first, size):
    exponent = quad[pl.ds(cell, 1), :][:, first : first + size] * width_cols[:, 0:1]
    return jnp.exp2(exponent)


def fill_slice(waves, base, own, kcols, first, row, coords):
    atoms = coords.shape[1]
    wide = tile_of(atoms, 1024)
    row = pl.multiple_of(row, 16)
    kv = kcols[pl.ds(pl.multiple_of(first + row, 16), 16), :]
    for start in range(0, atoms, wide):
        frac = coords[:, start : start + wide]
        turns = kv[:, 0:1] * frac[0:1, :] + kv[:, 1:2] * frac[1:2, :]
        turns = turns + kv[:, 2:3] * frac[2:3, :]
        turns = turns - ((turns + ROUNDER) - ROUNDER)
        square = turns * turns
        waves[pl.ds(pl.multiple_of(base + row, 16), 16), start : start + wide] = horner(
            COS_TERMS, square
        ).astype(BF16)
        waves[pl.ds(pl.multiple_of(base + own + row, 16), 16), start : start + wide] = (
            horner(SIN_TERMS, square) * turns
        ).astype(BF16)


def rows_of_share(index, shares, own):
    each = -(-own // (16 * shares))
    return [16 * jnp.minimum(index * each + p, own // 16 - 1) for p in range(each)]


def vector_columns(kvec):
    rows = kvec[...].astype(F32)
    if rows.shape[0] == 3:
        rows = jnp.concatenate([rows, jnp.zeros((5, rows.shape[1]), F32)], axis=0)
    return rows.T


def start_copies(sems, *moves):
    copies = [pltpu.make_async_copy(a, b, sems.at[i]) for i, (a, b) in enumerate(moves)]
    for copy in copies:
        copy.start()
    return copies


def prepare_kernel(
    coords_hbm, ids_hbm, recip_hbm, kvec_hbm, kfilt_hbm,
    waves, ids, coords, recip, kvec, kfilt, bounds, kcols, sems,
):
    atoms = coords.shape[1]
    own = kvec.shape[1]
    copies = start_copies(
        sems,
        (kvec_hbm, kvec),
        (coords_hbm, coords),
        (ids_hbm, ids.at[:, :atoms]),
        (recip_hbm, recip),
        (kfilt_hbm, kfilt),
    )
    ids[:, atoms:] = jnp.full((1, LANES), -1, jnp.int32)
    waves[:, atoms:] = jnp.zeros((waves.shape[0], LANES), BF16)
    for copy in copies[:3]:
        copy.wait()
    kcols[...] = vector_columns(kvec)
    fill_slice(waves, 0, own, kcols, 0, 0, coords)
    numbers = ids[:, :atoms]
    before = 0
    for cell in range(bounds.shape[1]):
        count = jnp.sum((numbers == cell).astype(F32)).astype(jnp.int32)
        bounds[0, cell] = count
        bounds[1, cell] = before
        before = before + count

    def phase_rows(i, carry):
        fill_slice(waves, 0, own, kcols, 0, 16 * i, coords)
        return carry

    lax.fori_loop(1, own // 16, phase_rows, 0)
    for copy in copies[3:]:
        copy.wait()


def pair_kernel(kvec, other_kvec, kvecs):
    count = kvec.shape[0]
    for j in range(count):
        for at, source in ((j, kvec), (j + count, other_kvec)):
            rows = source[j].astype(F32)
            if rows.shape[0] == 3:
                rows = jnp.concatenate([rows, jnp.zeros((5, rows.shape[1]), F32)], axis=0)
            kvecs[at] = rows


def half_kernel(core, near, far, out):
    count = near.shape[0]
    half = out.shape[2]
    if near.shape[2] == half:
        out[:count] = near[...]
        out[count:] = far[...]
    else:
        at = pl.ds(pl.multiple_of(core[0] * half, half), half)
        for j in range(count):
            out[j] = near[j, :, at]
            out[j + count] = far[j, :, at]


def project_kernel(coords, kvecs, feats_hbm, w_in_hbm, waves, proj_t, feats, w_in, kcols, sems):
    atoms, chan = feats.shape
    own = kcols.shape[0]
    copies = start_copies(sems, (w_in_hbm, w_in), (feats_hbm, feats))
    waves[:, atoms:] = jnp.zeros((waves.shape[0], LANES), BF16)
    proj_t[:, atoms:] = jnp.zeros((chan, LANES), BF16)
    kcols[...] = vector_columns(kvecs.at[1])
    for copy in copies:
        copy.wait()
    tiles = atoms // TILE

    def project(t, carry):
        at = pl.ds(pl.multiple_of(t * TILE, TILE), TILE)
        proj_t[:, at] = mm(w_in[...], feats[at, :], 0, 1).astype(BF16)
        for row in rows_of_share(t, tiles, own):
            fill_slice(waves, 0, own, kcols, 0, row, coords)
        return carry

    lax.fori_loop(0, tiles, project, 0)


def waves_kernel(n_ka, *refs):
    bounds, first, second, proj_t, ids, coords, recip = refs[:7]
    waves, factors, quad, kcols = refs[-4:]
    kvecs = [ref.at[j] for ref in refs[7:-4] for j in range(ref.shape[0])]
    atoms = coords.shape[1]
    own = kvecs[0].shape[1]
    cells = recip.shape[0]
    most = most_steps(atoms)
    for j in range(2, n_ka):
        kcols[(j - 2) * own : (j - 1) * own, :] = vector_columns(kvecs[j])
    for j in range(n_ka):
        rows = kvecs[j][...]
        squared = jnp.zeros((cells, own), F32)
        for r in range(3):
            part = recip[:, 3 * r : 3 * r + 1] * rows[0:1, :]
            part = part + recip[:, 3 * r + 1 : 3 * r + 2] * rows[1:2, :]
            part = part + recip[:, 3 * r + 2 : 3 * r + 3] * rows[2:3, :]
            squared = squared + part * part
        quad[:, own * j : own * (j + 1)] = squared
    waves[4 * own :, atoms:] = jnp.zeros((2 * own * (n_ka - 2), LANES), BF16)

    def early(cell, carry):
        start, steps, _ = span_of(bounds, cell)

        def action(n):
            at = pl.ds(start, n * TILE)
            lhs = proj_t[:, at] * (ids[:, at] == cell).astype(F32).astype(BF16)
            factors[cell, :, : 2 * own] = mm(lhs, first[:, at], 1, 1)
            factors[cell, :, 2 * own : 4 * own] = mm(lhs, second[:, at], 1, 1)
            for j in range(2, n_ka):
                for row in rows_of_share(cell, cells, own):
                    fill_slice(waves, 2 * own * j, own, kcols, (j - 2) * own, row, coords)
            for row in rows_of_share(cell, cells, 2 * own):
                from_rows = pl.ds(pl.multiple_of(row, 16), 16)
                waves[from_rows, :] = first[from_rows, :]
                waves[pl.ds(pl.multiple_of(2 * own + row, 16), 16), :] = second[from_rows, :]

        by_steps(steps, most, action)
        return carry

    lax.fori_loop(0, cells, early, 0)


def late_kernel(bounds, proj_t, ids, waves, sums):
    cells, _, width = sums.shape
    atoms = proj_t.shape[1] - LANES
    first = waves.shape[0] - width

    def late(cell, carry):
        start, steps, _ = span_of(bounds, cell)

        def action(n):
            at = pl.ds(start, n * TILE)
            lhs = proj_t[:, at] * (ids[:, at] == cell).astype(F32).astype(BF16)
            sums[cell] = mm(lhs, waves[first:, at], 1, 1)

        by_steps(steps, most_steps(atoms), action)
        return carry

    lax.fori_loop(0, cells, late, 0)


def filters_first(filt_t, core, nears, fars, others):
    chunk = 0
    half = filt_t.shape[0] // 2
    for ref in nears:
        own = ref.shape[1]
        filt_t[:, chunk * own : (chunk + 1) * own] = ref[0].T
        chunk += 1
    for mine, other in zip(fars, others):
        for j in range(mine.shape[0]):
            at = slice(chunk * own, (chunk + 1) * own)
            filt_t[pl.ds(pl.multiple_of(core * half, half), half), at] = mine[j].T
            filt_t[pl.ds(pl.multiple_of((1 - core) * half, half), half), at] = other[j].T
            chunk += 1
    return own


def message_kernel(n_ka, *refs):
    bounds, core, ids, quad, waves, low, high, spread, cotan, w_out = refs[:10]
    act_t, mgrad_t, raw_out, raw_half, filt_t, width_cols, even, odd, mess_t = refs[-9:]
    atoms, chan = cotan.shape
    filters = refs[10:-9]
    steps = (len(filters) - 2) // 2
    filters_first(filt_t, core[0], filters[:2], filters[2 : 2 + steps], filters[2 + steps :])
    width_cols[...] = column_to_lanes(spread[...] * (-LOG2_E))
    spread_cells(n_ka, bounds, ids, quad, filt_t, width_cols, (low, high), waves, even, odd, mess_t)
    mgrad_t[:, atoms:] = jnp.zeros((chan, LANES), BF16)
    raw_out[...] = jnp.zeros_like(raw_out)

    wide = tile_of(atoms, 2 * TILE)

    def middle(t, carry):
        at = pl.ds(pl.multiple_of(t * wide, wide), wide)
        message = mess_t[:, at]
        sigma = jax.nn.sigmoid(message)
        activated = (message * sigma).astype(BF16)
        act_t[:, at] = activated
        cot = cotan[at, :]
        act_grad = mm(w_out[...], cot, 1, 1)
        mgrad_t[:, at] = (act_grad * (sigma * (1.0 + message * (1.0 - sigma)))).astype(BF16)
        raw_out[...] += mm(activated, cot)
        return carry

    lax.fori_loop(0, atoms // wide, middle, 0)
    raw_half[...] = raw_out[...].astype(BF16)


def adjoint_kernel(n_ka, *refs):
    bounds, ids, quad, waves, factors, mgrad_t, spread = refs[:7]
    sums, filter_grad, filter_half, width_cols, grad_t = refs[7:]
    atoms = mgrad_t.shape[1] - LANES
    cells, k_all = quad.shape
    own = k_all // n_ka
    width_cols[...] = column_to_lanes(spread[...] * (-LOG2_E))
    grad_t[...] = jnp.zeros_like(grad_t)

    most = most_steps(atoms)

    def collect(cell):
        scaled = shape_of(cell, quad, width_cols, 0, own) * inverse_count(bounds[0, cell])
        grad_t[...] += scaled * (
            factors[cell, :, :own] * sums[cell, :, :own]
            + factors[cell, :, own : 2 * own] * sums[cell, :, own : 2 * own]
        )

    def gather(cell, before):
        start, steps, _ = span_of(bounds, cell)

        def action(n):
            if before is not None:
                collect(before)
            at = pl.ds(start, n * TILE)
            lhs = mgrad_t[:, at] * (ids[:, at] == cell).astype(F32).astype(BF16)
            sums[cell] = mm(lhs, waves[:, at], 1, 1)

        by_steps(steps, most, action)

    gather(0, None)

    def cell_step(cell, carry):
        gather(cell, cell - 1)
        return carry

    lax.fori_loop(1, cells, cell_step, 0)
    collect(cells - 1)
    result = grad_t[...].T
    filter_grad[...] = result
    filter_half[...] = result.astype(BF16)


def update_kernel(n_ka, *refs):
    bounds, core, ids, quad, waves, sums, spread = refs[:7]
    update_t = refs[-11]
    filt_t, width_cols, even, odd, total_t, sems = refs[-6:]
    copies = start_copies(sems, *zip(refs[-15:-11], refs[-10:-6]))
    atoms = update_t.shape[1]
    filters = refs[7:-15]
    steps = (len(filters) - 2) // 2
    filters_first(filt_t, core[0], filters[:2], filters[2 : 2 + steps], filters[2 + steps :])
    width_cols[...] = column_to_lanes(spread[...] * (-LOG2_E))
    spread_cells(n_ka, bounds, ids, quad, filt_t, width_cols, (sums,), waves, even, odd, total_t)
    update_t[...] = total_t[:, :atoms].astype(BF16)
    for copy in copies:
        copy.wait()


def gradient_kernel(update_t, feats, raw_in_t):
    raw_in_t[...] = mm(update_t[...], feats[...])


def residual_kernel(transposed, base, values_t, weight, out_hbm, out, sems):
    rows = base.shape[0]
    step = tile_of(rows, 512)
    copies = []
    for t in range(rows // step):
        at = slice(t * step, (t + 1) * step)
        value = mm(values_t[:, at].T, weight[...], 1, 1 if transposed else 0)
        out[at, :] = (base[at, :].astype(F32) + value).astype(BF16)
        copies.append(pltpu.make_async_copy(out.at[at, :], out_hbm.at[at, :], sems.at[t]))
        copies[-1].start()
    for copy in copies:
        copy.wait()


def residual(transposed, base, values_t, weight):
    rows, chan = base.shape
    vmem = pl.BlockSpec(memory_space=pltpu.VMEM)
    return pl.pallas_call(
        functools.partial(residual_kernel, transposed),
        out_shape=jax.ShapeDtypeStruct((rows, chan), BF16),
        in_specs=[vmem] * 3,
        out_specs=pl.BlockSpec(memory_space=pltpu.HBM),
        scratch_shapes=[
            pltpu.VMEM((rows, chan), BF16),
            pltpu.SemaphoreType.DMA((rows // tile_of(rows, 512),)),
        ],
        compiler_params=pltpu.CompilerParams(vmem_limit_bytes=SMALL),
        cost_estimate=pl.CostEstimate(
            flops=2 * FLOPS_PER_MICRO, bytes_accessed=0, transcendentals=0
        ),
    )(base, values_t, weight)


def last_out_kernel(raw_out, other_out, out_sum):
    out_sum[...] = raw_out[...] + other_out[: raw_out.shape[0], :].astype(F32)


def out_kernel(raw_out, other_out, filter_half, out_sum, packed):
    chan = raw_out.shape[0]
    value = raw_out[...] + other_out[:chan, :].astype(F32)
    out_sum[...] = value
    packed[:chan, :] = value.astype(BF16)
    packed[chan:, :] = filter_half[...]


def filter_kernel(*refs):
    own = refs[0].shape[0]
    value = refs[0][...]
    for ref in refs[1:-1]:
        value = value + ref[ref.shape[0] - own :, :].astype(F32)
    refs[-1][...] = value


def squares_kernel(filt, near, f_sum, f_squares):
    value = filt[...] + near[...]
    f_sum[...] = value
    f_squares[...] = jnp.broadcast_to(
        jnp.sum(jnp.sum(value * value, axis=0, keepdims=True), axis=1, keepdims=True),
        f_squares.shape,
    )


def chip_kernel(raw_in_t, near, in_sum, in_half):
    value = raw_in_t[...] + near[...]
    in_sum[...] = value
    in_half[...] = value.astype(BF16)


def total_of(first, others):
    value = first[...]
    for other in others:
        value = value + other[...].astype(F32)
    return value


def add_kernel(first, second, *outs):
    value = first[...] + second[...].astype(F32)
    for out in outs:
        out[...] = value.astype(out.dtype)


def final_kernel(n_chip, n_ka, *refs):
    in_parts = refs[:n_chip]
    raw_out, near_out, filt, squares, g_in, g_out, g_filt = refs[n_chip:]
    raw_in = total_of(in_parts[0], in_parts[1:])
    out = raw_out[...] + near_out[...]
    both = raw_in * raw_in + out * out
    weight_squares = jnp.sum(jnp.sum(both, axis=0, keepdims=True), axis=1, keepdims=True)
    weight_scale = lax.rsqrt(weight_squares / (2 * raw_in.size) + 1e-06)
    filter_scale = lax.rsqrt(squares[0:1, 0:1] / (n_ka * filt.size) + 1e-06)
    g_in[...] = (raw_in * weight_scale).T
    g_out[...] = out * weight_scale
    g_filt[...] = filt[...] * filter_scale


def call(
    kernel, operands, smem, outs, scratch=(), limit=SMALL, micros=2, space=pltpu.VMEM, smem_outs=0
):
    vmem = pl.BlockSpec(memory_space=pltpu.VMEM)
    rest = len(operands) - smem
    spaces = space if isinstance(space, tuple) else (space,) * rest
    return pl.pallas_call(
        kernel,
        out_shape=tuple(jax.ShapeDtypeStruct(*o) for o in outs),
        in_specs=[pl.BlockSpec(memory_space=x) for x in (pltpu.SMEM,) * smem + spaces],
        out_specs=(vmem,) * (len(outs) - smem_outs)
        + (pl.BlockSpec(memory_space=pltpu.SMEM),) * smem_outs,
        scratch_shapes=list(scratch),
        compiler_params=pltpu.CompilerParams(vmem_limit_bytes=limit),
        cost_estimate=pl.CostEstimate(
            flops=micros * FLOPS_PER_MICRO, bytes_accessed=0, transcendentals=0
        ),
    )(*operands)


def in_hbm(value):
    return pltpu.with_memory_space_constraint(value, pltpu.HBM)


def send(value, axis, step):
    return lax.ppermute(value, axis, routes(step, lax.axis_size(axis)))


def doubling(first, size):
    return [first << i for i in range(size.bit_length()) if first << i < size]


def block(feats, coords, cell_ids, recip, kvec, w_in, w_out, kfilt, spread, cotan):
    n_ka = lax.axis_size("ka")
    n_dp = lax.axis_size("dp")
    atoms, chan = feats.shape
    own = kvec.shape[1]
    k_all = own * n_ka
    cells = recip.shape[1]
    long = atoms + LANES
    recip, spread = recip[0], spread[None]
    chips = range(2, n_dp, 2)
    vm = pltpu.VMEM
    dma = pltpu.SemaphoreType.DMA
    near_kvec = send(kvec[None], "ka", 1)
    near_kfilt = send(kfilt[None], "ka", 1)
    first, ids, coords, recip, kvec, kfilt, bounds = call(
        prepare_kernel,
        [in_hbm(x) for x in (coords, cell_ids, recip, kvec, kfilt)],
        0,
        [
            ((2 * own, long), BF16),
            ((1, long), jnp.int32),
            (coords.shape, F32),
            (recip.shape, F32),
            (kvec.shape, jnp.int32),
            (kfilt.shape, F32),
            ((2, cells), jnp.int32),
        ],
        [vm((own, 8), F32), dma((5,))],
        SMALL,
        3,
        pltpu.HBM,
        smem_outs=1,
    )
    kfilt = kfilt[None]
    (kvecs,) = call(pair_kernel, (kvec[None], near_kvec), 0, [((2, 8, own), F32)])
    far_kvecs = [kvecs]
    ka_steps = doubling(2, n_ka)
    for s in ka_steps:
        if s > 2:
            (kvecs,) = call(pair_kernel, (kvecs, far_kvecs[-1]), 0, [((s, 8, own), F32)])
        far_kvecs.append(send(kvecs, "ka", s))
    second, proj_t = call(
        project_kernel,
        (coords, far_kvecs[0], in_hbm(feats), in_hbm(w_in)),
        0,
        [((2 * own, long), BF16), ((chan, long), BF16)],
        [vm((atoms, chan), BF16), vm((chan, chan), BF16), vm((own, 8), F32), dma((2,))],
        SMALL,
        3,
        (pltpu.VMEM, pltpu.VMEM, pltpu.HBM, pltpu.HBM),
    )
    core = lax.rem(lax.axis_index("dp"), 2).astype(jnp.int32).reshape(1)
    kfilts, far = kfilt, near_kfilt
    halves_far = []
    for s in ka_steps:
        (kfilts,) = call(half_kernel, (core, kfilts, far), 1, [((s, own, chan // 2), F32)])
        far = send(kfilts, "ka", s)
        halves_far.append(far)
    waves, low, quad = call(
        functools.partial(waves_kernel, n_ka),
        (bounds, first, second, proj_t, ids, coords, recip, *far_kvecs),
        1,
        [((2 * k_all, long), BF16), ((cells, chan, 4 * own), F32), ((cells, k_all), F32)],
        [vm((k_all - 2 * own, 8), F32)],
        LIMIT,
        8,
    )
    halves_other = [send(x, "dp", 1) for x in halves_far]
    (high,) = call(
        late_kernel,
        (bounds, proj_t, ids, waves),
        1,
        [((cells, chan, 2 * k_all - 4 * own), F32)],
        [],
        SMALL,
        3,
    )
    far_kfilts = [kfilt, near_kfilt, *halves_far, *halves_other]
    halves = [vm((2 * n_ka, chan, own), BF16)] * 2
    act_t, mgrad_t, raw_out, raw_half = call(
        functools.partial(message_kernel, n_ka),
        (bounds, core, ids, quad, waves, low, high, spread, cotan, w_out, *far_kfilts),
        2,
        [((chan, atoms), BF16), ((chan, long), BF16), ((chan, chan), F32), ((chan, chan), BF16)],
        [vm((chan, k_all), F32), vm((chan, 8), F32), *halves, vm((chan, long), F32)],
        LIMIT,
        8,
    )
    out_steps = doubling(2, n_dp)
    out_part = send(raw_half, "dp", out_steps[0])
    sums, filter_grad, filter_half = call(
        functools.partial(adjoint_kernel, n_ka),
        (bounds, ids, quad, waves, low, mgrad_t, spread),
        1,
        [((cells, chan, 2 * k_all), F32), ((own, chan), F32), ((own, chan), BF16)],
        [vm((chan, 8), F32), vm((chan, own), F32)],
        LIMIT,
        6,
    )
    raw_out, packed = call(
        out_kernel,
        (raw_out, out_part, filter_half),
        0,
        [((chan, chan), F32), ((chan + own, chan), BF16)],
    )
    filt_parts = [send(packed if s == 4 else filter_half, "dp", s) for s in chips]
    out_part = filt_parts[1]
    for s in out_steps[2:]:
        raw_out, raw_half = call(
            out_kernel,
            (raw_out, out_part, filter_half),
            0,
            [((chan, chan), F32), ((chan + own, chan), BF16)],
        )
        out_part = send(raw_half, "dp", s)
    held = (feats, cotan, w_in, w_out)
    update_t, feats, cotan, w_in, w_out = call(
        functools.partial(update_kernel, n_ka),
        (bounds, core, ids, quad, waves, sums, spread, *far_kfilts, *map(in_hbm, held)),
        2,
        [((chan, atoms), BF16), *((x.shape, BF16) for x in held)],
        [vm((chan, k_all), F32), vm((chan, 8), F32), *halves, vm((chan, long), F32), dma((4,))],
        LIMIT,
        8,
        (pltpu.VMEM,) * (5 + len(far_kfilts)) + (pltpu.HBM,) * 4,
    )
    (filt_sum,) = call(filter_kernel, (filter_grad, *filt_parts), 0, [((own, chan), F32)])
    filt_near = send(filt_sum, "dp", 1)
    (raw_in_t,) = call(gradient_kernel, (update_t, feats), 0, [((chan, chan), F32)])
    near = send(raw_in_t, "dp", 1)
    (out_sum,) = call(last_out_kernel, (raw_out, out_part), 0, [((chan, chan), F32)])
    near_out = send(out_sum, "dp", 1)
    f_sum, squares = call(
        squares_kernel, (filt_sum, filt_near), 0, [((own, chan), F32), ((8, LANES), F32)]
    )
    square_steps = doubling(1, n_ka)
    square_part = send(squares, "ka", square_steps[0])
    feat_grad = residual(True, cotan, update_t, w_in)
    in_sum, in_half = call(
        chip_kernel, (raw_in_t, near), 0, [((chan, chan), F32), ((chan, chan), BF16)]
    )
    in_parts = [in_sum] + [send(in_half, "dp", s) for s in chips]
    for s in square_steps[1:] + [0]:
        (squares,) = call(add_kernel, (squares, square_part), 0, [((8, LANES), F32)])
        if s:
            square_part = send(squares, "ka", s)
    mixed = residual(False, feats, act_t, w_out)
    grads = call(
        functools.partial(final_kernel, len(in_parts), n_ka),
        (*in_parts, out_sum, near_out, f_sum, squares),
        0,
        [((chan, chan), F32), ((chan, chan), F32), ((own, chan), F32)],
    )
    return (mixed, feat_grad, *grads)


def solution(mesh):
    placed = (
        P("dp", None),
        P(None, "dp"),
        P("dp", None),
        P("dp", None, None),
        P(None, "ka"),
        P(),
        P(),
        P("ka", None),
        P(),
        P("dp", None),
    )
    return jax.shard_map(
        block,
        mesh=mesh,
        in_specs=placed,
        out_specs=(P("dp", None), P("dp", None), P(), P(), P("ka", None)),
        check_vma=False,
    )
```

```python
import functools

import jax
import jax.numpy as jnp
from jax import lax
from jax.experimental import pallas as pl
from jax.experimental.pallas import tpu as pltpu
from jax.sharding import PartitionSpec as P


F32 = jnp.float32
BF16 = jnp.bfloat16
LANES = 128
TILE = 256
MOST = 1024
LIMIT = 24 << 20
SMALL = 6 << 20
FLOPS_PER_MICRO = 1 << 30
LOG2_E = 1.4426950408889634
COS_TERMS = (
    0.9999999890590228,
    -19.73920449945383,
    64.93911745989081,
    -85.45013953079767,
    60.167630950263465,
    -25.967599245923743,
    6.52865815775625,
)
SIN_TERMS = (
    6.283184916495428,
    -41.34158923268831,
    81.59994332977429,
    -76.61447253115396,
    41.34288235413569,
    -12.471243534350362,
)
CODES = 32767.0
ROUNDER = 12582912.0


def mm(lhs, rhs, lhs_dim=1, rhs_dim=0):
    return lax.dot_general(
        lhs, rhs, (((lhs_dim,), (rhs_dim,)), ((), ())), preferred_element_type=F32
    )


def horner(terms, square):
    value = terms[-1] * square + terms[-2]
    for term in terms[-3::-1]:
        value = value * square + term
    return value


def routes(step, count):
    if count & (count - 1) == 0:
        return [(i, i ^ step) for i in range(count)]
    return [(i, (i + step) % count) for i in range(count)]


def tile_of(size, most):
    tile = most
    while size % tile:
        tile //= 2
    return tile


def column_to_lanes(row):
    return jnp.broadcast_to(row, (8, row.shape[1])).T


def span_of(bounds, cell):
    first = bounds[1, cell]
    start = lax.div(first, LANES) * LANES
    count = bounds[0, cell]
    steps = lax.div(first - start + count + (TILE - 1), TILE)
    return pl.multiple_of(start, LANES), steps, count


def most_steps(atoms):
    return -(-(min(MOST, atoms) + LANES - 1) // TILE)


def by_steps(steps, most, action):
    for n in range(1, most + 1):
        pl.when(steps == n)(functools.partial(action, n))


def weigh(cell, n_ka, bounds, quad, filt_t, width_cols, sums, weights):
    own = filt_t.shape[1] // n_ka
    inverse = inverse_count(bounds[0, cell])
    for j in range(n_ka):
        scaled = shape_of(cell, quad, width_cols, j * own, own) * inverse
        filt = filt_t[:, own * j : own * (j + 1)] * scaled
        for half in (2 * j, 2 * j + 1):
            at = slice(own * half, own * (half + 1))
            weights[:, at] = (filt * sums[cell, :, at]).astype(BF16)


def spread_cells(n_ka, bounds, ids, quad, filt_t, width_cols, sums, waves, even, odd, out):
    cells = quad.shape[0]
    most = most_steps(out.shape[1] - LANES)

    def one(cell, weights, after, target):
        start, steps, _ = span_of(bounds, cell)

        def action(n):
            if after is not None:
                weigh(after, n_ka, bounds, quad, filt_t, width_cols, sums, target)
            for t in range(n):
                at = pl.ds(pl.multiple_of(start + t * TILE, LANES), TILE)
                value = mm(weights[...], waves[:, at])
                out[:, at] = jnp.where(ids[:, at] == cell, value, out[:, at])

        by_steps(steps, most, action)

    weigh(0, n_ka, bounds, quad, filt_t, width_cols, sums, even)

    def two(i, carry):
        one(2 * i, even, jnp.minimum(2 * i + 1, cells - 1), odd)
        one(2 * i + 1, odd, jnp.minimum(2 * i + 2, cells - 1), even)
        return carry

    lax.fori_loop(0, cells // 2, two, 0)
    if cells % 2:
        one(cells - 1, even, None, None)


def inverse_count(count):
    return 1.0 / jnp.full((1, 1), count, jnp.int32).astype(F32)


def shape_of(cell, quad, width_cols, first, size):
    exponent = quad[pl.ds(cell, 1), :][:, first : first + size] * width_cols[:, 0:1]
    return jnp.exp2(exponent)


def fill_slice(waves, base, own, kcols, first, row, coords):
    atoms = coords.shape[1]
    wide = tile_of(atoms, 1024)
    row = pl.multiple_of(row, 16)
    kv = kcols[pl.ds(pl.multiple_of(first + row, 16), 16), :]
    for start in range(0, atoms, wide):
        frac = coords[:, start : start + wide]
        turns = kv[:, 0:1] * frac[0:1, :] + kv[:, 1:2] * frac[1:2, :]
        turns = turns + kv[:, 2:3] * frac[2:3, :]
        turns = turns - ((turns + ROUNDER) - ROUNDER)
        square = turns * turns
        waves[pl.ds(pl.multiple_of(base + row, 16), 16), start : start + wide] = horner(
            COS_TERMS, square
        ).astype(BF16)
        waves[pl.ds(pl.multiple_of(base + own + row, 16), 16), start : start + wide] = (
            horner(SIN_TERMS, square) * turns
        ).astype(BF16)


def rows_of_share(index, shares, own):
    each = -(-own // (16 * shares))
    return [16 * jnp.minimum(index * each + p, own // 16 - 1) for p in range(each)]


def vector_columns(kvec):
    rows = kvec[...].astype(F32)
    if rows.shape[0] == 3:
        rows = jnp.concatenate([rows, jnp.zeros((5, rows.shape[1]), F32)], axis=0)
    return rows.T


def start_copies(sems, *moves):
    copies = [pltpu.make_async_copy(a, b, sems.at[i]) for i, (a, b) in enumerate(moves)]
    for copy in copies:
        copy.start()
    return copies


def prepare_kernel(
    coords_hbm, ids_hbm, recip_hbm, kvec_hbm, kfilt_hbm,
    waves, ids, coords, recip, kvec, kfilt, bounds, kcols, sems,
):
    atoms = coords.shape[1]
    own = kvec.shape[1]
    copies = start_copies(
        sems,
        (kvec_hbm, kvec),
        (coords_hbm, coords),
        (ids_hbm, ids.at[:, :atoms]),
        (recip_hbm, recip),
        (kfilt_hbm, kfilt),
    )
    ids[:, atoms:] = jnp.full((1, LANES), -1, jnp.int32)
    waves[:, atoms:] = jnp.zeros((waves.shape[0], LANES), BF16)
    for copy in copies[:3]:
        copy.wait()
    kcols[...] = vector_columns(kvec)
    fill_slice(waves, 0, own, kcols, 0, 0, coords)
    numbers = ids[:, :atoms]
    before = 0
    for cell in range(bounds.shape[1]):
        count = jnp.sum((numbers == cell).astype(F32)).astype(jnp.int32)
        bounds[0, cell] = count
        bounds[1, cell] = before
        before = before + count

    def phase_rows(i, carry):
        fill_slice(waves, 0, own, kcols, 0, 16 * i, coords)
        return carry

    lax.fori_loop(1, own // 16, phase_rows, 0)
    for copy in copies[3:]:
        copy.wait()


def pair_kernel(kvec, other_kvec, kvecs):
    count = kvec.shape[0]
    for j in range(count):
        for at, source in ((j, kvec), (j + count, other_kvec)):
            rows = source[j].astype(F32)
            if rows.shape[0] == 3:
                rows = jnp.concatenate([rows, jnp.zeros((5, rows.shape[1]), F32)], axis=0)
            kvecs[at] = rows


def code_kernel(near, far, out):
    chan = near.shape[2]
    for j, ref in enumerate((near, far)):
        values = ref[0].T
        largest = jnp.max(jnp.abs(values), axis=0, keepdims=True)
        power = jnp.ceil(jnp.log2(jnp.maximum(largest, 1e-30)) + 1e-3)
        coded = values * (CODES * jnp.exp2(-power))
        coded = (coded + ROUNDER) - ROUNDER
        out[j, :chan, :] = coded.astype(jnp.int32).astype(jnp.int16)
        powers = jnp.broadcast_to(power, (16, power.shape[1]))
        out[j, chan:, :] = powers.astype(jnp.int32).astype(jnp.int16)


def stack_kernel(near, far, out):
    count = near.shape[0]
    out[:count] = near[...]
    out[count:] = far[...]


def project_kernel(coords, kvecs, feats_hbm, w_in_hbm, waves, proj_t, feats, w_in, kcols, sems):
    atoms, chan = feats.shape
    own = kcols.shape[0]
    copies = start_copies(sems, (w_in_hbm, w_in), (feats_hbm, feats))
    waves[:, atoms:] = jnp.zeros((waves.shape[0], LANES), BF16)
    proj_t[:, atoms:] = jnp.zeros((chan, LANES), BF16)
    kcols[...] = vector_columns(kvecs.at[1])
    for copy in copies:
        copy.wait()
    tiles = atoms // TILE

    def project(t, carry):
        at = pl.ds(pl.multiple_of(t * TILE, TILE), TILE)
        proj_t[:, at] = mm(w_in[...], feats[at, :], 0, 1).astype(BF16)
        for row in rows_of_share(t, tiles, own):
            fill_slice(waves, 0, own, kcols, 0, row, coords)
        return carry

    lax.fori_loop(0, tiles, project, 0)


def waves_kernel(n_ka, *refs):
    bounds, first, second, proj_t, ids, coords, recip = refs[:7]
    waves, factors, quad, kcols = refs[-4:]
    kvecs = [ref.at[j] for ref in refs[7:-4] for j in range(ref.shape[0])]
    atoms = coords.shape[1]
    own = kvecs[0].shape[1]
    cells = recip.shape[0]
    most = most_steps(atoms)
    for j in range(2, n_ka):
        kcols[(j - 2) * own : (j - 1) * own, :] = vector_columns(kvecs[j])
    for j in range(n_ka):
        rows = kvecs[j][...]
        squared = jnp.zeros((cells, own), F32)
        for r in range(3):
            part = recip[:, 3 * r : 3 * r + 1] * rows[0:1, :]
            part = part + recip[:, 3 * r + 1 : 3 * r + 2] * rows[1:2, :]
            part = part + recip[:, 3 * r + 2 : 3 * r + 3] * rows[2:3, :]
            squared = squared + part * part
        quad[:, own * j : own * (j + 1)] = squared
    waves[4 * own :, atoms:] = jnp.zeros((2 * own * (n_ka - 2), LANES), BF16)

    def early(cell, carry):
        start, steps, _ = span_of(bounds, cell)

        def action(n):
            at = pl.ds(start, n * TILE)
            lhs = proj_t[:, at] * (ids[:, at] == cell).astype(F32).astype(BF16)
            factors[cell, :, : 2 * own] = mm(lhs, first[:, at], 1, 1)
            factors[cell, :, 2 * own : 4 * own] = mm(lhs, second[:, at], 1, 1)
            for j in range(2, n_ka):
                for row in rows_of_share(cell, cells, own):
                    fill_slice(waves, 2 * own * j, own, kcols, (j - 2) * own, row, coords)

        by_steps(steps, most, action)
        return carry

    lax.fori_loop(0, cells, early, 0)
    waves[: 2 * own, :] = first[...]
    waves[2 * own : 4 * own, :] = second[...]

    def late(cell, carry):
        start, steps, _ = span_of(bounds, cell)

        def action(n):
            at = pl.ds(start, n * TILE)
            lhs = proj_t[:, at] * (ids[:, at] == cell).astype(F32).astype(BF16)
            factors[cell, :, 4 * own :] = mm(lhs, waves[4 * own :, at], 1, 1)

        by_steps(steps, most, action)
        return carry

    lax.fori_loop(0, cells, late, 0)


def filters_first(filt_t, refs):
    chan = filt_t.shape[0]
    chunk = 0
    for ref in refs:
        for j in range(ref.shape[0]):
            if ref.dtype == F32:
                own = ref.shape[1]
                values = ref[j].T
            else:
                coded = ref[j].astype(jnp.int32).astype(F32)
                values = coded[:chan, :] * (jnp.exp2(coded[chan : chan + 1, :]) * (1.0 / CODES))
            filt_t[:, chunk * own : (chunk + 1) * own] = values
            chunk += 1
    return own


def message_kernel(n_ka, *refs):
    bounds, ids, quad, waves, factors, spread, cotan, w_out = refs[:8]
    act_t, mgrad_t, raw_out, raw_half, filt_t, width_cols, even, odd, mess_t = refs[-9:]
    atoms, chan = cotan.shape
    filters_first(filt_t, refs[8:-9])
    width_cols[...] = column_to_lanes(spread[...] * (-LOG2_E))
    spread_cells(n_ka, bounds, ids, quad, filt_t, width_cols, factors, waves, even, odd, mess_t)
    mgrad_t[:, atoms:] = jnp.zeros((chan, LANES), BF16)
    raw_out[...] = jnp.zeros_like(raw_out)

    wide = tile_of(atoms, 2 * TILE)

    def middle(t, carry):
        at = pl.ds(pl.multiple_of(t * wide, wide), wide)
        message = mess_t[:, at]
        sigma = jax.nn.sigmoid(message)
        activated = (message * sigma).astype(BF16)
        act_t[:, at] = activated
        cot = cotan[at, :]
        act_grad = mm(w_out[...], cot, 1, 1)
        mgrad_t[:, at] = (act_grad * (sigma * (1.0 + message * (1.0 - sigma)))).astype(BF16)
        raw_out[...] += mm(activated, cot)
        return carry

    lax.fori_loop(0, atoms // wide, middle, 0)
    raw_half[...] = raw_out[...].astype(BF16)


def adjoint_kernel(n_ka, *refs):
    bounds, ids, quad, waves, factors, mgrad_t, spread = refs[:7]
    sums, filter_grad, filter_half, width_cols, grad_t = refs[7:]
    atoms = mgrad_t.shape[1] - LANES
    cells, k_all = quad.shape
    own = k_all // n_ka
    width_cols[...] = column_to_lanes(spread[...] * (-LOG2_E))
    grad_t[...] = jnp.zeros_like(grad_t)

    most = most_steps(atoms)

    def collect(cell):
        scaled = shape_of(cell, quad, width_cols, 0, own) * inverse_count(bounds[0, cell])
        grad_t[...] += scaled * (
            factors[cell, :, :own] * sums[cell, :, :own]
            + factors[cell, :, own : 2 * own] * sums[cell, :, own : 2 * own]
        )

    def gather(cell, before):
        start, steps, _ = span_of(bounds, cell)

        def action(n):
            if before is not None:
                collect(before)
            at = pl.ds(start, n * TILE)
            lhs = mgrad_t[:, at] * (ids[:, at] == cell).astype(F32).astype(BF16)
            sums[cell] = mm(lhs, waves[:, at], 1, 1)

        by_steps(steps, most, action)

    gather(0, None)

    def cell_step(cell, carry):
        gather(cell, cell - 1)
        return carry

    lax.fori_loop(1, cells, cell_step, 0)
    collect(cells - 1)
    result = grad_t[...].T
    filter_grad[...] = result
    filter_half[...] = result.astype(BF16)


def update_kernel(n_ka, *refs):
    bounds, ids, quad, waves, sums, spread = refs[:6]
    update_t = refs[-11]
    filt_t, width_cols, even, odd, total_t, sems = refs[-6:]
    copies = start_copies(sems, *zip(refs[-15:-11], refs[-10:-6]))
    atoms = update_t.shape[1]
    filters_first(filt_t, refs[6:-15])
    width_cols[...] = column_to_lanes(spread[...] * (-LOG2_E))
    spread_cells(n_ka, bounds, ids, quad, filt_t, width_cols, sums, waves, even, odd, total_t)
    update_t[...] = total_t[:, :atoms].astype(BF16)
    for copy in copies:
        copy.wait()


def gradient_kernel(update_t, feats, raw_in_t):
    raw_in_t[...] = mm(update_t[...], feats[...])


def residual_kernel(transposed, base, values_t, weight, out_hbm, out, sems):
    rows = base.shape[0]
    step = tile_of(rows, 512)
    copies = []
    for t in range(rows // step):
        at = slice(t * step, (t + 1) * step)
        value = mm(values_t[:, at].T, weight[...], 1, 1 if transposed else 0)
        out[at, :] = (base[at, :].astype(F32) + value).astype(BF16)
        copies.append(pltpu.make_async_copy(out.at[at, :], out_hbm.at[at, :], sems.at[t]))
        copies[-1].start()
    for copy in copies:
        copy.wait()


def residual(transposed, base, values_t, weight):
    rows, chan = base.shape
    vmem = pl.BlockSpec(memory_space=pltpu.VMEM)
    return pl.pallas_call(
        functools.partial(residual_kernel, transposed),
        out_shape=jax.ShapeDtypeStruct((rows, chan), BF16),
        in_specs=[vmem] * 3,
        out_specs=pl.BlockSpec(memory_space=pltpu.HBM),
        scratch_shapes=[
            pltpu.VMEM((rows, chan), BF16),
            pltpu.SemaphoreType.DMA((rows // tile_of(rows, 512),)),
        ],
        compiler_params=pltpu.CompilerParams(vmem_limit_bytes=SMALL),
        cost_estimate=pl.CostEstimate(
            flops=2 * FLOPS_PER_MICRO, bytes_accessed=0, transcendentals=0
        ),
    )(base, values_t, weight)


def last_out_kernel(raw_out, other_out, out_sum):
    out_sum[...] = raw_out[...] + other_out[: raw_out.shape[0], :].astype(F32)


def out_kernel(raw_out, other_out, filter_half, out_sum, packed):
    chan = raw_out.shape[0]
    value = raw_out[...] + other_out[:chan, :].astype(F32)
    out_sum[...] = value
    packed[:chan, :] = value.astype(BF16)
    packed[chan:, :] = filter_half[...]


def filter_kernel(*refs):
    own = refs[0].shape[0]
    value = refs[0][...]
    for ref in refs[1:-1]:
        value = value + ref[ref.shape[0] - own :, :].astype(F32)
    refs[-1][...] = value


def squares_kernel(filt, near, f_sum, f_squares):
    value = filt[...] + near[...]
    f_sum[...] = value
    f_squares[...] = jnp.broadcast_to(
        jnp.sum(jnp.sum(value * value, axis=0, keepdims=True), axis=1, keepdims=True),
        f_squares.shape,
    )


def chip_kernel(raw_in_t, near, in_sum, in_half):
    value = raw_in_t[...] + near[...]
    in_sum[...] = value
    in_half[...] = value.astype(BF16)


def total_of(first, others):
    value = first[...]
    for other in others:
        value = value + other[...].astype(F32)
    return value


def add_kernel(first, second, *outs):
    value = first[...] + second[...].astype(F32)
    for out in outs:
        out[...] = value.astype(out.dtype)


def final_kernel(n_chip, n_ka, *refs):
    in_parts = refs[:n_chip]
    raw_out, near_out, filt, squares, g_in, g_out, g_filt = refs[n_chip:]
    raw_in = total_of(in_parts[0], in_parts[1:])
    out = raw_out[...] + near_out[...]
    both = raw_in * raw_in + out * out
    weight_squares = jnp.sum(jnp.sum(both, axis=0, keepdims=True), axis=1, keepdims=True)
    weight_scale = lax.rsqrt(weight_squares / (2 * raw_in.size) + 1e-06)
    filter_scale = lax.rsqrt(squares[0:1, 0:1] / (n_ka * filt.size) + 1e-06)
    g_in[...] = (raw_in * weight_scale).T
    g_out[...] = out * weight_scale
    g_filt[...] = filt[...] * filter_scale


def call(
    kernel, operands, smem, outs, scratch=(), limit=SMALL, micros=2, space=pltpu.VMEM, smem_outs=0
):
    vmem = pl.BlockSpec(memory_space=pltpu.VMEM)
    rest = len(operands) - smem
    spaces = space if isinstance(space, tuple) else (space,) * rest
    return pl.pallas_call(
        kernel,
        out_shape=tuple(jax.ShapeDtypeStruct(*o) for o in outs),
        in_specs=[pl.BlockSpec(memory_space=x) for x in (pltpu.SMEM,) * smem + spaces],
        out_specs=(vmem,) * (len(outs) - smem_outs)
        + (pl.BlockSpec(memory_space=pltpu.SMEM),) * smem_outs,
        scratch_shapes=list(scratch),
        compiler_params=pltpu.CompilerParams(vmem_limit_bytes=limit),
        cost_estimate=pl.CostEstimate(
            flops=micros * FLOPS_PER_MICRO, bytes_accessed=0, transcendentals=0
        ),
    )(*operands)


def in_hbm(value):
    return pltpu.with_memory_space_constraint(value, pltpu.HBM)


def send(value, axis, step):
    return lax.ppermute(value, axis, routes(step, lax.axis_size(axis)))


def doubling(first, size):
    return [first << i for i in range(size.bit_length()) if first << i < size]


def block(feats, coords, cell_ids, recip, kvec, w_in, w_out, kfilt, spread, cotan):
    n_ka = lax.axis_size("ka")
    n_dp = lax.axis_size("dp")
    atoms, chan = feats.shape
    own = kvec.shape[1]
    k_all = own * n_ka
    cells = recip.shape[1]
    long = atoms + LANES
    recip, spread = recip[0], spread[None]
    chips = range(2, n_dp, 2)
    vm = pltpu.VMEM
    dma = pltpu.SemaphoreType.DMA
    near_kvec = send(kvec[None], "ka", 1)
    near_kfilt = send(kfilt[None], "ka", 1)
    first, ids, coords, recip, kvec, kfilt, bounds = call(
        prepare_kernel,
        [in_hbm(x) for x in (coords, cell_ids, recip, kvec, kfilt)],
        0,
        [
            ((2 * own, long), BF16),
            ((1, long), jnp.int32),
            (coords.shape, F32),
            (recip.shape, F32),
            (kvec.shape, jnp.int32),
            (kfilt.shape, F32),
            ((2, cells), jnp.int32),
        ],
        [vm((own, 8), F32), dma((5,))],
        SMALL,
        3,
        pltpu.HBM,
        smem_outs=1,
    )
    kfilt = kfilt[None]
    (kvecs,) = call(pair_kernel, (kvec[None], near_kvec), 0, [((2, 8, own), F32)])
    far_kvecs, far_kfilts = [kvecs], [kfilt, near_kfilt]
    ka_steps = doubling(2, n_ka)
    for s in ka_steps:
        if s > 2:
            (kvecs,) = call(pair_kernel, (kvecs, far_kvecs[-1]), 0, [((s, 8, own), F32)])
        far_kvecs.append(send(kvecs, "ka", s))
    second, proj_t = call(
        project_kernel,
        (coords, far_kvecs[0], in_hbm(feats), in_hbm(w_in)),
        0,
        [((2 * own, long), BF16), ((chan, long), BF16)],
        [vm((atoms, chan), BF16), vm((chan, chan), BF16), vm((own, 8), F32), dma((2,))],
        SMALL,
        3,
        (pltpu.VMEM, pltpu.VMEM, pltpu.HBM, pltpu.HBM),
    )
    kfilts = kfilt
    for s in ka_steps:
        (kfilts,) = call(
            code_kernel if s == 2 else stack_kernel,
            (kfilts, far_kfilts[-1]),
            0,
            [((s, chan + 16, own), jnp.int16)],
        )
        far_kfilts.append(send(kfilts, "ka", s))
    waves, factors, quad = call(
        functools.partial(waves_kernel, n_ka),
        (bounds, first, second, proj_t, ids, coords, recip, *far_kvecs),
        1,
        [((2 * k_all, long), BF16), ((cells, chan, 2 * k_all), F32), ((cells, k_all), F32)],
        [vm((k_all - 2 * own, 8), F32)],
        LIMIT,
        8,
    )
    halves = [vm((chan, 2 * k_all), BF16)] * 2
    act_t, mgrad_t, raw_out, raw_half = call(
        functools.partial(message_kernel, n_ka),
        (bounds, ids, quad, waves, factors, spread, cotan, w_out, *far_kfilts),
        1,
        [((chan, atoms), BF16), ((chan, long), BF16), ((chan, chan), F32), ((chan, chan), BF16)],
        [vm((chan, k_all), F32), vm((chan, 8), F32), *halves, vm((chan, long), F32)],
        LIMIT,
        8,
    )
    out_steps = doubling(2, n_dp)
    out_part = send(raw_half, "dp", out_steps[0])
    sums, filter_grad, filter_half = call(
        functools.partial(adjoint_kernel, n_ka),
        (bounds, ids, quad, waves, factors, mgrad_t, spread),
        1,
        [((cells, chan, 2 * k_all), F32), ((own, chan), F32), ((own, chan), BF16)],
        [vm((chan, 8), F32), vm((chan, own), F32)],
        LIMIT,
        6,
    )
    raw_out, packed = call(
        out_kernel,
        (raw_out, out_part, filter_half),
        0,
        [((chan, chan), F32), ((chan + own, chan), BF16)],
    )
    filt_parts = [send(packed if s == 4 else filter_half, "dp", s) for s in chips]
    out_part = filt_parts[1]
    for s in out_steps[2:]:
        raw_out, raw_half = call(
            out_kernel,
            (raw_out, out_part, filter_half),
            0,
            [((chan, chan), F32), ((chan + own, chan), BF16)],
        )
        out_part = send(raw_half, "dp", s)
    held = (feats, cotan, w_in, w_out)
    update_t, feats, cotan, w_in, w_out = call(
        functools.partial(update_kernel, n_ka),
        (bounds, ids, quad, waves, sums, spread, *far_kfilts, *map(in_hbm, held)),
        1,
        [((chan, atoms), BF16), *((x.shape, BF16) for x in held)],
        [vm((chan, k_all), F32), vm((chan, 8), F32), *halves, vm((chan, long), F32), dma((4,))],
        LIMIT,
        8,
        (pltpu.VMEM,) * (5 + len(far_kfilts)) + (pltpu.HBM,) * 4,
    )
    (filt_sum,) = call(filter_kernel, (filter_grad, *filt_parts), 0, [((own, chan), F32)])
    filt_near = send(filt_sum, "dp", 1)
    (raw_in_t,) = call(gradient_kernel, (update_t, feats), 0, [((chan, chan), F32)])
    near = send(raw_in_t, "dp", 1)
    (out_sum,) = call(last_out_kernel, (raw_out, out_part), 0, [((chan, chan), F32)])
    near_out = send(out_sum, "dp", 1)
    f_sum, squares = call(
        squares_kernel, (filt_sum, filt_near), 0, [((own, chan), F32), ((8, LANES), F32)]
    )
    square_steps = doubling(1, n_ka)
    square_part = send(squares, "ka", square_steps[0])
    feat_grad = residual(True, cotan, update_t, w_in)
    in_sum, in_half = call(
        chip_kernel, (raw_in_t, near), 0, [((chan, chan), F32), ((chan, chan), BF16)]
    )
    in_parts = [in_sum] + [send(in_half, "dp", s) for s in chips]
    for s in square_steps[1:] + [0]:
        (squares,) = call(add_kernel, (squares, square_part), 0, [((8, LANES), F32)])
        if s:
            square_part = send(squares, "ka", s)
    mixed = residual(False, feats, act_t, w_out)
    grads = call(
        functools.partial(final_kernel, len(in_parts), n_ka),
        (*in_parts, out_sum, near_out, f_sum, squares),
        0,
        [((chan, chan), F32), ((chan, chan), F32), ((own, chan), F32)],
    )
    return (mixed, feat_grad, *grads)


def solution(mesh):
    placed = (
        P("dp", None),
        P(None, "dp"),
        P("dp", None),
        P("dp", None, None),
        P(None, "ka"),
        P(),
        P(),
        P("ka", None),
        P(),
        P("dp", None),
    )
    return jax.shard_map(
        block,
        mesh=mesh,
        in_specs=placed,
        out_specs=(P("dp", None), P("dp", None), P(), P(), P("ka", None)),
        check_vma=False,
    )
```

```python
import functools

import jax
import jax.numpy as jnp
from jax import lax
from jax.experimental import pallas as pl
from jax.experimental.pallas import tpu as pltpu
from jax.sharding import PartitionSpec as P


F32 = jnp.float32
BF16 = jnp.bfloat16
LANES = 128
TILE = 256
MOST = 1024
LIMIT = 24 << 20
SMALL = 6 << 20
FLOPS_PER_MICRO = 1 << 30
LOG2_E = 1.4426950408889634
COS_TERMS = (
    0.9999999890590228,
    -19.73920449945383,
    64.93911745989081,
    -85.45013953079767,
    60.167630950263465,
    -25.967599245923743,
    6.52865815775625,
)
SIN_TERMS = (
    6.283184916495428,
    -41.34158923268831,
    81.59994332977429,
    -76.61447253115396,
    41.34288235413569,
    -12.471243534350362,
)
CODES = 32767.0
ROUNDER = 12582912.0


def mm(lhs, rhs, lhs_dim=1, rhs_dim=0):
    return lax.dot_general(
        lhs, rhs, (((lhs_dim,), (rhs_dim,)), ((), ())), preferred_element_type=F32
    )


def horner(terms, square):
    value = terms[-1] * square + terms[-2]
    for term in terms[-3::-1]:
        value = value * square + term
    return value


def routes(step, count):
    if count & (count - 1) == 0:
        return [(i, i ^ step) for i in range(count)]
    return [(i, (i + step) % count) for i in range(count)]


def tile_of(size, most):
    tile = most
    while size % tile:
        tile //= 2
    return tile


def column_to_lanes(row):
    return jnp.broadcast_to(row, (8, row.shape[1])).T


def span_of(bounds, cell):
    first = bounds[1, cell]
    start = lax.div(first, LANES) * LANES
    count = bounds[0, cell]
    steps = lax.div(first - start + count + (TILE - 1), TILE)
    return pl.multiple_of(start, LANES), steps, count


def most_steps(atoms):
    return -(-(min(MOST, atoms) + LANES - 1) // TILE)


def by_steps(steps, most, action):
    for n in range(1, most + 1):
        pl.when(steps == n)(functools.partial(action, n))


def weigh(cell, n_ka, bounds, quad, filt_t, width_cols, sums, weights):
    own = filt_t.shape[1] // n_ka
    inverse = inverse_count(bounds[0, cell])
    for j in range(n_ka):
        scaled = shape_of(cell, quad, width_cols, j * own, own) * inverse
        filt = filt_t[:, own * j : own * (j + 1)] * scaled
        for half in (2 * j, 2 * j + 1):
            at = slice(own * half, own * (half + 1))
            weights[:, at] = (filt * sums[cell, :, at]).astype(BF16)


def spread_cells(n_ka, bounds, ids, quad, filt_t, width_cols, sums, waves, even, odd, out):
    cells = quad.shape[0]
    most = most_steps(out.shape[1] - LANES)

    def one(cell, weights, after, target):
        start, steps, _ = span_of(bounds, cell)

        def action(n):
            if after is not None:
                weigh(after, n_ka, bounds, quad, filt_t, width_cols, sums, target)
            for t in range(n):
                at = pl.ds(pl.multiple_of(start + t * TILE, LANES), TILE)
                value = mm(weights[...], waves[:, at])
                out[:, at] = jnp.where(ids[:, at] == cell, value, out[:, at])

        by_steps(steps, most, action)

    weigh(0, n_ka, bounds, quad, filt_t, width_cols, sums, even)

    def two(i, carry):
        one(2 * i, even, jnp.minimum(2 * i + 1, cells - 1), odd)
        one(2 * i + 1, odd, jnp.minimum(2 * i + 2, cells - 1), even)
        return carry

    lax.fori_loop(0, cells // 2, two, 0)
    if cells % 2:
        one(cells - 1, even, None, None)


def inverse_count(count):
    return 1.0 / jnp.full((1, 1), count, jnp.int32).astype(F32)


def shape_of(cell, quad, width_cols, first, size):
    exponent = quad[pl.ds(cell, 1), :][:, first : first + size] * width_cols[:, 0:1]
    return jnp.exp2(exponent)


def fill_slice(waves, base, own, kcols, first, row, coords):
    atoms = coords.shape[1]
    wide = tile_of(atoms, 1024)
    row = pl.multiple_of(row, 16)
    kv = kcols[pl.ds(pl.multiple_of(first + row, 16), 16), :]
    for start in range(0, atoms, wide):
        frac = coords[:, start : start + wide]
        turns = kv[:, 0:1] * frac[0:1, :] + kv[:, 1:2] * frac[1:2, :]
        turns = turns + kv[:, 2:3] * frac[2:3, :]
        turns = turns - ((turns + ROUNDER) - ROUNDER)
        square = turns * turns
        waves[pl.ds(pl.multiple_of(base + row, 16), 16), start : start + wide] = horner(
            COS_TERMS, square
        ).astype(BF16)
        waves[pl.ds(pl.multiple_of(base + own + row, 16), 16), start : start + wide] = (
            horner(SIN_TERMS, square) * turns
        ).astype(BF16)


def rows_of_share(index, shares, own):
    each = -(-own // (16 * shares))
    return [16 * jnp.minimum(index * each + p, own // 16 - 1) for p in range(each)]


def vector_columns(kvec):
    rows = kvec[...].astype(F32)
    if rows.shape[0] == 3:
        rows = jnp.concatenate([rows, jnp.zeros((5, rows.shape[1]), F32)], axis=0)
    return rows.T


def start_copies(sems, *moves):
    copies = [pltpu.make_async_copy(a, b, sems.at[i]) for i, (a, b) in enumerate(moves)]
    for copy in copies:
        copy.start()
    return copies


def prepare_kernel(
    coords_hbm, ids_hbm, recip_hbm, kvec_hbm, kfilt_hbm,
    waves, ids, coords, recip, kvec, kfilt, bounds, kcols, sems,
):
    atoms = coords.shape[1]
    own = kvec.shape[1]
    copies = start_copies(
        sems,
        (kvec_hbm, kvec),
        (coords_hbm, coords),
        (ids_hbm, ids.at[:, :atoms]),
        (recip_hbm, recip),
        (kfilt_hbm, kfilt),
    )
    ids[:, atoms:] = jnp.full((1, LANES), -1, jnp.int32)
    waves[:, atoms:] = jnp.zeros((waves.shape[0], LANES), BF16)
    for copy in copies[:3]:
        copy.wait()
    kcols[...] = vector_columns(kvec)
    fill_slice(waves, 0, own, kcols, 0, 0, coords)
    numbers = ids[:, :atoms]
    before = 0
    for cell in range(bounds.shape[1]):
        count = jnp.sum((numbers == cell).astype(F32)).astype(jnp.int32)
        bounds[0, cell] = count
        bounds[1, cell] = before
        before = before + count

    def phase_rows(i, carry):
        fill_slice(waves, 0, own, kcols, 0, 16 * i, coords)
        return carry

    lax.fori_loop(1, own // 16, phase_rows, 0)
    for copy in copies[3:]:
        copy.wait()


def pair_kernel(kvec, other_kvec, kvecs):
    count = kvec.shape[0]
    for j in range(count):
        for at, source in ((j, kvec), (j + count, other_kvec)):
            rows = source[j].astype(F32)
            if rows.shape[0] == 3:
                rows = jnp.concatenate([rows, jnp.zeros((5, rows.shape[1]), F32)], axis=0)
            kvecs[at] = rows


def code_kernel(near, far, out):
    chan = near.shape[2]
    for j, ref in enumerate((near, far)):
        values = ref[0].T
        largest = jnp.max(jnp.abs(values), axis=0, keepdims=True)
        power = jnp.ceil(jnp.log2(jnp.maximum(largest, 1e-30)) + 0.02)
        coded = values * (CODES / jnp.exp2(power))
        coded = (coded + ROUNDER) - ROUNDER
        out[j, :chan, :] = coded.astype(jnp.int32).astype(jnp.int16)
        powers = jnp.broadcast_to(power, (16, power.shape[1]))
        out[j, chan:, :] = powers.astype(jnp.int32).astype(jnp.int16)


def stack_kernel(near, far, out):
    count = near.shape[0]
    out[:count] = near[...]
    out[count:] = far[...]


def project_kernel(coords, kvecs, feats_hbm, w_in_hbm, waves, proj_t, feats, w_in, kcols, sems):
    atoms, chan = feats.shape
    own = kcols.shape[0]
    copies = start_copies(sems, (w_in_hbm, w_in), (feats_hbm, feats))
    waves[:, atoms:] = jnp.zeros((waves.shape[0], LANES), BF16)
    proj_t[:, atoms:] = jnp.zeros((chan, LANES), BF16)
    kcols[...] = vector_columns(kvecs.at[1])
    for copy in copies:
        copy.wait()
    tiles = atoms // TILE

    def project(t, carry):
        at = pl.ds(pl.multiple_of(t * TILE, TILE), TILE)
        proj_t[:, at] = mm(w_in[...], feats[at, :], 0, 1).astype(BF16)
        for row in rows_of_share(t, tiles, own):
            fill_slice(waves, 0, own, kcols, 0, row, coords)
        return carry

    lax.fori_loop(0, tiles, project, 0)


def waves_kernel(n_ka, *refs):
    bounds, first, second, proj_t, ids, coords, recip = refs[:7]
    waves, factors, quad, kcols = refs[-4:]
    kvecs = [ref.at[j] for ref in refs[7:-4] for j in range(ref.shape[0])]
    atoms = coords.shape[1]
    own = kvecs[0].shape[1]
    cells = recip.shape[0]
    most = most_steps(atoms)
    for j in range(2, n_ka):
        kcols[(j - 2) * own : (j - 1) * own, :] = vector_columns(kvecs[j])
    for j in range(n_ka):
        rows = kvecs[j][...]
        squared = jnp.zeros((cells, own), F32)
        for r in range(3):
            part = recip[:, 3 * r : 3 * r + 1] * rows[0:1, :]
            part = part + recip[:, 3 * r + 1 : 3 * r + 2] * rows[1:2, :]
            part = part + recip[:, 3 * r + 2 : 3 * r + 3] * rows[2:3, :]
            squared = squared + part * part
        quad[:, own * j : own * (j + 1)] = squared
    waves[4 * own :, atoms:] = jnp.zeros((2 * own * (n_ka - 2), LANES), BF16)

    def early(cell, carry):
        start, steps, _ = span_of(bounds, cell)

        def action(n):
            at = pl.ds(start, n * TILE)
            lhs = proj_t[:, at] * (ids[:, at] == cell).astype(F32).astype(BF16)
            factors[cell, :, : 2 * own] = mm(lhs, first[:, at], 1, 1)
            factors[cell, :, 2 * own : 4 * own] = mm(lhs, second[:, at], 1, 1)
            for j in range(2, n_ka):
                for row in rows_of_share(cell, cells, own):
                    fill_slice(waves, 2 * own * j, own, kcols, (j - 2) * own, row, coords)

        by_steps(steps, most, action)
        return carry

    lax.fori_loop(0, cells, early, 0)
    waves[: 2 * own, :] = first[...]
    waves[2 * own : 4 * own, :] = second[...]

    def late(cell, carry):
        start, steps, _ = span_of(bounds, cell)

        def action(n):
            at = pl.ds(start, n * TILE)
            lhs = proj_t[:, at] * (ids[:, at] == cell).astype(F32).astype(BF16)
            factors[cell, :, 4 * own :] = mm(lhs, waves[4 * own :, at], 1, 1)

        by_steps(steps, most, action)
        return carry

    lax.fori_loop(0, cells, late, 0)


def filters_first(filt_t, refs):
    chan = filt_t.shape[0]
    chunk = 0
    for ref in refs:
        for j in range(ref.shape[0]):
            if ref.dtype == F32:
                own = ref.shape[1]
                values = ref[j].T
            else:
                coded = ref[j].astype(jnp.int32).astype(F32)
                values = coded[:chan, :] * (jnp.exp2(coded[chan : chan + 1, :]) / CODES)
            filt_t[:, chunk * own : (chunk + 1) * own] = values
            chunk += 1
    return own


def message_kernel(n_ka, *refs):
    bounds, ids, quad, waves, factors, spread, cotan, w_out = refs[:8]
    act_t, mgrad_t, raw_out, raw_half, filt_t, width_cols, even, odd, mess_t = refs[-9:]
    atoms, chan = cotan.shape
    filters_first(filt_t, refs[8:-9])
    width_cols[...] = column_to_lanes(spread[...] * (-LOG2_E))
    spread_cells(n_ka, bounds, ids, quad, filt_t, width_cols, factors, waves, even, odd, mess_t)
    mgrad_t[:, atoms:] = jnp.zeros((chan, LANES), BF16)
    raw_out[...] = jnp.zeros_like(raw_out)

    wide = tile_of(atoms, 2 * TILE)

    def middle(t, carry):
        at = pl.ds(pl.multiple_of(t * wide, wide), wide)
        message = mess_t[:, at]
        sigma = jax.nn.sigmoid(message)
        activated = (message * sigma).astype(BF16)
        act_t[:, at] = activated
        cot = cotan[at, :]
        act_grad = mm(w_out[...], cot, 1, 1)
        mgrad_t[:, at] = (act_grad * (sigma * (1.0 + message * (1.0 - sigma)))).astype(BF16)
        raw_out[...] += mm(activated, cot)
        return carry

    lax.fori_loop(0, atoms // wide, middle, 0)
    raw_half[...] = raw_out[...].astype(BF16)


def adjoint_kernel(n_ka, *refs):
    bounds, ids, quad, waves, factors, mgrad_t, spread = refs[:7]
    sums, filter_grad, filter_half, width_cols, grad_t = refs[7:]
    atoms = mgrad_t.shape[1] - LANES
    cells, k_all = quad.shape
    own = k_all // n_ka
    width_cols[...] = column_to_lanes(spread[...] * (-LOG2_E))
    grad_t[...] = jnp.zeros_like(grad_t)

    most = most_steps(atoms)

    def collect(cell):
        scaled = shape_of(cell, quad, width_cols, 0, own) * inverse_count(bounds[0, cell])
        grad_t[...] += scaled * (
            factors[cell, :, :own] * sums[cell, :, :own]
            + factors[cell, :, own : 2 * own] * sums[cell, :, own : 2 * own]
        )

    def gather(cell, before):
        start, steps, _ = span_of(bounds, cell)

        def action(n):
            if before is not None:
                collect(before)
            at = pl.ds(start, n * TILE)
            lhs = mgrad_t[:, at] * (ids[:, at] == cell).astype(F32).astype(BF16)
            sums[cell] = mm(lhs, waves[:, at], 1, 1)

        by_steps(steps, most, action)

    gather(0, None)

    def cell_step(cell, carry):
        gather(cell, cell - 1)
        return carry

    lax.fori_loop(1, cells, cell_step, 0)
    collect(cells - 1)
    result = grad_t[...].T
    filter_grad[...] = result
    filter_half[...] = result.astype(BF16)


def update_kernel(n_ka, *refs):
    bounds, ids, quad, waves, sums, spread = refs[:6]
    update_t = refs[-11]
    filt_t, width_cols, even, odd, total_t, sems = refs[-6:]
    copies = start_copies(sems, *zip(refs[-15:-11], refs[-10:-6]))
    atoms = update_t.shape[1]
    filters_first(filt_t, refs[6:-15])
    width_cols[...] = column_to_lanes(spread[...] * (-LOG2_E))
    spread_cells(n_ka, bounds, ids, quad, filt_t, width_cols, sums, waves, even, odd, total_t)
    update_t[...] = total_t[:, :atoms].astype(BF16)
    for copy in copies:
        copy.wait()


def gradient_kernel(update_t, feats, raw_in_t):
    raw_in_t[...] = mm(update_t[...], feats[...])


def residual_kernel(transposed, base, values_t, weight, out_hbm, out, sems):
    rows = base.shape[0]
    step = tile_of(rows, 512)
    copies = []
    for t in range(rows // step):
        at = slice(t * step, (t + 1) * step)
        value = mm(values_t[:, at].T, weight[...], 1, 1 if transposed else 0)
        out[at, :] = (base[at, :].astype(F32) + value).astype(BF16)
        copies.append(pltpu.make_async_copy(out.at[at, :], out_hbm.at[at, :], sems.at[t]))
        copies[-1].start()
    for copy in copies:
        copy.wait()


def residual(transposed, base, values_t, weight):
    rows, chan = base.shape
    vmem = pl.BlockSpec(memory_space=pltpu.VMEM)
    return pl.pallas_call(
        functools.partial(residual_kernel, transposed),
        out_shape=jax.ShapeDtypeStruct((rows, chan), BF16),
        in_specs=[vmem] * 3,
        out_specs=pl.BlockSpec(memory_space=pltpu.HBM),
        scratch_shapes=[
            pltpu.VMEM((rows, chan), BF16),
            pltpu.SemaphoreType.DMA((rows // tile_of(rows, 512),)),
        ],
        compiler_params=pltpu.CompilerParams(vmem_limit_bytes=SMALL),
        cost_estimate=pl.CostEstimate(
            flops=2 * FLOPS_PER_MICRO, bytes_accessed=0, transcendentals=0
        ),
    )(base, values_t, weight)


def last_out_kernel(raw_out, other_out, out_sum):
    out_sum[...] = raw_out[...] + other_out[: raw_out.shape[0], :].astype(F32)


def out_kernel(raw_out, other_out, filter_half, out_sum, packed):
    chan = raw_out.shape[0]
    value = raw_out[...] + other_out[:chan, :].astype(F32)
    out_sum[...] = value
    packed[:chan, :] = value.astype(BF16)
    packed[chan:, :] = filter_half[...]


def filter_kernel(*refs):
    own = refs[0].shape[0]
    value = refs[0][...]
    for ref in refs[1:-1]:
        value = value + ref[ref.shape[0] - own :, :].astype(F32)
    refs[-1][...] = value


def squares_kernel(filt, near, f_sum, f_squares):
    value = filt[...] + near[...]
    f_sum[...] = value
    f_squares[...] = jnp.broadcast_to(
        jnp.sum(jnp.sum(value * value, axis=0, keepdims=True), axis=1, keepdims=True),
        f_squares.shape,
    )


def chip_kernel(raw_in_t, near, in_sum, in_half):
    value = raw_in_t[...] + near[...]
    in_sum[...] = value
    in_half[...] = value.astype(BF16)


def total_of(first, others):
    value = first[...]
    for other in others:
        value = value + other[...].astype(F32)
    return value


def add_kernel(first, second, *outs):
    value = first[...] + second[...].astype(F32)
    for out in outs:
        out[...] = value.astype(out.dtype)


def final_kernel(n_chip, n_ka, *refs):
    in_parts = refs[:n_chip]
    raw_out, near_out, filt, squares, g_in, g_out, g_filt = refs[n_chip:]
    raw_in = total_of(in_parts[0], in_parts[1:])
    out = raw_out[...] + near_out[...]
    both = raw_in * raw_in + out * out
    weight_squares = jnp.sum(jnp.sum(both, axis=0, keepdims=True), axis=1, keepdims=True)
    weight_scale = lax.rsqrt(weight_squares / (2 * raw_in.size) + 1e-06)
    filter_scale = lax.rsqrt(squares[0:1, 0:1] / (n_ka * filt.size) + 1e-06)
    g_in[...] = (raw_in * weight_scale).T
    g_out[...] = out * weight_scale
    g_filt[...] = filt[...] * filter_scale


def call(
    kernel, operands, smem, outs, scratch=(), limit=SMALL, micros=2, space=pltpu.VMEM, smem_outs=0
):
    vmem = pl.BlockSpec(memory_space=pltpu.VMEM)
    rest = len(operands) - smem
    spaces = space if isinstance(space, tuple) else (space,) * rest
    return pl.pallas_call(
        kernel,
        out_shape=tuple(jax.ShapeDtypeStruct(*o) for o in outs),
        in_specs=[pl.BlockSpec(memory_space=x) for x in (pltpu.SMEM,) * smem + spaces],
        out_specs=(vmem,) * (len(outs) - smem_outs)
        + (pl.BlockSpec(memory_space=pltpu.SMEM),) * smem_outs,
        scratch_shapes=list(scratch),
        compiler_params=pltpu.CompilerParams(vmem_limit_bytes=limit),
        cost_estimate=pl.CostEstimate(
            flops=micros * FLOPS_PER_MICRO, bytes_accessed=0, transcendentals=0
        ),
    )(*operands)


def in_hbm(value):
    return pltpu.with_memory_space_constraint(value, pltpu.HBM)


def send(value, axis, step):
    return lax.ppermute(value, axis, routes(step, lax.axis_size(axis)))


def doubling(first, size):
    return [first << i for i in range(size.bit_length()) if first << i < size]


def block(feats, coords, cell_ids, recip, kvec, w_in, w_out, kfilt, spread, cotan):
    n_ka = lax.axis_size("ka")
    n_dp = lax.axis_size("dp")
    atoms, chan = feats.shape
    own = kvec.shape[1]
    k_all = own * n_ka
    cells = recip.shape[1]
    long = atoms + LANES
    recip, spread = recip[0], spread[None]
    chips = range(2, n_dp, 2)
    vm = pltpu.VMEM
    dma = pltpu.SemaphoreType.DMA
    near_kvec = send(kvec[None], "ka", 1)
    near_kfilt = send(kfilt[None], "ka", 1)
    first, ids, coords, recip, kvec, kfilt, bounds = call(
        prepare_kernel,
        [in_hbm(x) for x in (coords, cell_ids, recip, kvec, kfilt)],
        0,
        [
            ((2 * own, long), BF16),
            ((1, long), jnp.int32),
            (coords.shape, F32),
            (recip.shape, F32),
            (kvec.shape, jnp.int32),
            (kfilt.shape, F32),
            ((2, cells), jnp.int32),
        ],
        [vm((own, 8), F32), dma((5,))],
        SMALL,
        3,
        pltpu.HBM,
        smem_outs=1,
    )
    kfilt = kfilt[None]
    (kvecs,) = call(pair_kernel, (kvec[None], near_kvec), 0, [((2, 8, own), F32)])
    far_kvecs, far_kfilts = [kvecs], [kfilt, near_kfilt]
    ka_steps = doubling(2, n_ka)
    for s in ka_steps:
        if s > 2:
            (kvecs,) = call(pair_kernel, (kvecs, far_kvecs[-1]), 0, [((s, 8, own), F32)])
        far_kvecs.append(send(kvecs, "ka", s))
    second, proj_t = call(
        project_kernel,
        (coords, far_kvecs[0], in_hbm(feats), in_hbm(w_in)),
        0,
        [((2 * own, long), BF16), ((chan, long), BF16)],
        [vm((atoms, chan), BF16), vm((chan, chan), BF16), vm((own, 8), F32), dma((2,))],
        SMALL,
        3,
        (pltpu.VMEM, pltpu.VMEM, pltpu.HBM, pltpu.HBM),
    )
    kfilts = kfilt
    for s in ka_steps:
        (kfilts,) = call(
            code_kernel if s == 2 else stack_kernel,
            (kfilts, far_kfilts[-1]),
            0,
            [((s, chan + 16, own), jnp.int16)],
        )
        far_kfilts.append(send(kfilts, "ka", s))
    waves, factors, quad = call(
        functools.partial(waves_kernel, n_ka),
        (bounds, first, second, proj_t, ids, coords, recip, *far_kvecs),
        1,
        [((2 * k_all, long), BF16), ((cells, chan, 2 * k_all), F32), ((cells, k_all), F32)],
        [vm((k_all - 2 * own, 8), F32)],
        LIMIT,
        8,
    )
    halves = [vm((chan, 2 * k_all), BF16)] * 2
    act_t, mgrad_t, raw_out, raw_half = call(
        functools.partial(message_kernel, n_ka),
        (bounds, ids, quad, waves, factors, spread, cotan, w_out, *far_kfilts),
        1,
        [((chan, atoms), BF16), ((chan, long), BF16), ((chan, chan), F32), ((chan, chan), BF16)],
        [vm((chan, k_all), F32), vm((chan, 8), F32), *halves, vm((chan, long), F32)],
        LIMIT,
        8,
    )
    out_steps = doubling(2, n_dp)
    out_part = send(raw_half, "dp", out_steps[0])
    sums, filter_grad, filter_half = call(
        functools.partial(adjoint_kernel, n_ka),
        (bounds, ids, quad, waves, factors, mgrad_t, spread),
        1,
        [((cells, chan, 2 * k_all), F32), ((own, chan), F32), ((own, chan), BF16)],
        [vm((chan, 8), F32), vm((chan, own), F32)],
        LIMIT,
        6,
    )
    raw_out, packed = call(
        out_kernel,
        (raw_out, out_part, filter_half),
        0,
        [((chan, chan), F32), ((chan + own, chan), BF16)],
    )
    filt_parts = [send(packed if s == 4 else filter_half, "dp", s) for s in chips]
    out_part = filt_parts[1]
    for s in out_steps[2:]:
        raw_out, raw_half = call(
            out_kernel,
            (raw_out, out_part, filter_half),
            0,
            [((chan, chan), F32), ((chan + own, chan), BF16)],
        )
        out_part = send(raw_half, "dp", s)
    held = (feats, cotan, w_in, w_out)
    update_t, feats, cotan, w_in, w_out = call(
        functools.partial(update_kernel, n_ka),
        (bounds, ids, quad, waves, sums, spread, *far_kfilts, *map(in_hbm, held)),
        1,
        [((chan, atoms), BF16), *((x.shape, BF16) for x in held)],
        [vm((chan, k_all), F32), vm((chan, 8), F32), *halves, vm((chan, long), F32), dma((4,))],
        LIMIT,
        8,
        (pltpu.VMEM,) * (5 + len(far_kfilts)) + (pltpu.HBM,) * 4,
    )
    (filt_sum,) = call(filter_kernel, (filter_grad, *filt_parts), 0, [((own, chan), F32)])
    filt_near = send(filt_sum, "dp", 1)
    (raw_in_t,) = call(gradient_kernel, (update_t, feats), 0, [((chan, chan), F32)])
    near = send(raw_in_t, "dp", 1)
    (out_sum,) = call(last_out_kernel, (raw_out, out_part), 0, [((chan, chan), F32)])
    near_out = send(out_sum, "dp", 1)
    f_sum, squares = call(
        squares_kernel, (filt_sum, filt_near), 0, [((own, chan), F32), ((8, LANES), F32)]
    )
    square_steps = doubling(1, n_ka)
    square_part = send(squares, "ka", square_steps[0])
    feat_grad = residual(True, cotan, update_t, w_in)
    in_sum, in_half = call(
        chip_kernel, (raw_in_t, near), 0, [((chan, chan), F32), ((chan, chan), BF16)]
    )
    in_parts = [in_sum] + [send(in_half, "dp", s) for s in chips]
    for s in square_steps[1:] + [0]:
        (squares,) = call(add_kernel, (squares, square_part), 0, [((8, LANES), F32)])
        if s:
            square_part = send(squares, "ka", s)
    mixed = residual(False, feats, act_t, w_out)
    grads = call(
        functools.partial(final_kernel, len(in_parts), n_ka),
        (*in_parts, out_sum, near_out, f_sum, squares),
        0,
        [((chan, chan), F32), ((chan, chan), F32), ((own, chan), F32)],
    )
    return (mixed, feat_grad, *grads)


def solution(mesh):
    placed = (
        P("dp", None),
        P(None, "dp"),
        P("dp", None),
        P("dp", None, None),
        P(None, "ka"),
        P(),
        P(),
        P("ka", None),
        P(),
        P("dp", None),
    )
    return jax.shard_map(
        block,
        mesh=mesh,
        in_specs=placed,
        out_specs=(P("dp", None), P("dp", None), P(), P(), P("ka", None)),
        check_vma=False,
    )
```

```python
import functools

import jax
import jax.numpy as jnp
from jax import lax
from jax.experimental import pallas as pl
from jax.experimental.pallas import tpu as pltpu
from jax.sharding import PartitionSpec as P


F32 = jnp.float32
BF16 = jnp.bfloat16
LANES = 128
TILE = 256
MOST = 1024
LIMIT = 24 << 20
SMALL = 6 << 20
FLOPS_PER_MICRO = 1 << 30
LOG2_E = 1.4426950408889634
COS_TERMS = (
    0.9999999890590228,
    -19.73920449945383,
    64.93911745989081,
    -85.45013953079767,
    60.167630950263465,
    -25.967599245923743,
    6.52865815775625,
)
SIN_TERMS = (
    6.283184916495428,
    -41.34158923268831,
    81.59994332977429,
    -76.61447253115396,
    41.34288235413569,
    -12.471243534350362,
)
CODES = 32767.0
ROUNDER = 12582912.0


def mm(lhs, rhs, lhs_dim=1, rhs_dim=0):
    return lax.dot_general(
        lhs, rhs, (((lhs_dim,), (rhs_dim,)), ((), ())), preferred_element_type=F32
    )


def horner(terms, square):
    value = terms[-1] * square + terms[-2]
    for term in terms[-3::-1]:
        value = value * square + term
    return value


def routes(step, count):
    if count & (count - 1) == 0:
        return [(i, i ^ step) for i in range(count)]
    return [(i, (i + step) % count) for i in range(count)]


def tile_of(size, most):
    tile = most
    while size % tile:
        tile //= 2
    return tile


def column_to_lanes(row):
    return jnp.broadcast_to(row, (8, row.shape[1])).T


def span_of(bounds, cell):
    first = bounds[1, cell]
    start = lax.div(first, LANES) * LANES
    count = bounds[0, cell]
    steps = lax.div(first - start + count + (TILE - 1), TILE)
    return pl.multiple_of(start, LANES), steps, count


def most_steps(atoms):
    return -(-(min(MOST, atoms) + LANES - 1) // TILE)


def by_steps(steps, most, action):
    for n in range(1, most + 1):
        pl.when(steps == n)(functools.partial(action, n))


def weigh(cell, n_ka, bounds, quad, filt_t, width_cols, sums, weights):
    own = filt_t.shape[1] // n_ka
    inverse = inverse_count(bounds[0, cell])
    for j in range(n_ka):
        scaled = shape_of(cell, quad, width_cols, j * own, own) * inverse
        filt = filt_t[:, own * j : own * (j + 1)] * scaled
        for half in (2 * j, 2 * j + 1):
            at = slice(own * half, own * (half + 1))
            weights[half] = (filt * sums[cell, :, at]).astype(BF16)


def spread_cells(n_ka, bounds, ids, quad, filt_t, width_cols, sums, waves, even, odd, out):
    cells = quad.shape[0]
    most = most_steps(out.shape[1] - LANES)

    def one(cell, weights, after, target):
        start, steps, _ = span_of(bounds, cell)

        def action(n):
            if after is not None:
                weigh(after, n_ka, bounds, quad, filt_t, width_cols, sums, target)
            lhs = jnp.concatenate([weights[h] for h in range(2 * n_ka)], axis=1)
            for t in range(n):
                at = pl.ds(pl.multiple_of(start + t * TILE, LANES), TILE)
                value = mm(lhs, waves[:, at])
                out[:, at] = jnp.where(ids[:, at] == cell, value, out[:, at])

        by_steps(steps, most, action)

    weigh(0, n_ka, bounds, quad, filt_t, width_cols, sums, even)

    def two(i, carry):
        one(2 * i, even, jnp.minimum(2 * i + 1, cells - 1), odd)
        one(2 * i + 1, odd, jnp.minimum(2 * i + 2, cells - 1), even)
        return carry

    lax.fori_loop(0, cells // 2, two, 0)
    if cells % 2:
        one(cells - 1, even, None, None)


def inverse_count(count):
    return 1.0 / jnp.full((1, 1), count, jnp.int32).astype(F32)


def shape_of(cell, quad, width_cols, first, size):
    exponent = quad[pl.ds(cell, 1), :][:, first : first + size] * width_cols[:, 0:1]
    return jnp.exp2(exponent)


def fill_slice(waves, base, own, kcols, first, row, coords):
    atoms = coords.shape[1]
    wide = tile_of(atoms, 1024)
    row = pl.multiple_of(row, 16)
    kv = kcols[pl.ds(pl.multiple_of(first + row, 16), 16), :]
    for start in range(0, atoms, wide):
        frac = coords[:, start : start + wide]
        turns = kv[:, 0:1] * frac[0:1, :] + kv[:, 1:2] * frac[1:2, :]
        turns = turns + kv[:, 2:3] * frac[2:3, :]
        turns = turns - ((turns + ROUNDER) - ROUNDER)
        square = turns * turns
        waves[pl.ds(pl.multiple_of(base + row, 16), 16), start : start + wide] = horner(
            COS_TERMS, square
        ).astype(BF16)
        waves[pl.ds(pl.multiple_of(base + own + row, 16), 16), start : start + wide] = (
            horner(SIN_TERMS, square) * turns
        ).astype(BF16)


def rows_of_share(index, shares, own):
    each = -(-own // (16 * shares))
    return [16 * jnp.minimum(index * each + p, own // 16 - 1) for p in range(each)]


def vector_columns(kvec):
    rows = kvec[...].astype(F32)
    if rows.shape[0] == 3:
        rows = jnp.concatenate([rows, jnp.zeros((5, rows.shape[1]), F32)], axis=0)
    return rows.T


def start_copies(sems, *moves):
    copies = [pltpu.make_async_copy(a, b, sems.at[i]) for i, (a, b) in enumerate(moves)]
    for copy in copies:
        copy.start()
    return copies


def prepare_kernel(
    coords_hbm, ids_hbm, recip_hbm, kvec_hbm, kfilt_hbm,
    waves, ids, coords, recip, kvec, kfilt, bounds, kcols, sems,
):
    atoms = coords.shape[1]
    own = kvec.shape[1]
    copies = start_copies(
        sems,
        (kvec_hbm, kvec),
        (coords_hbm, coords),
        (ids_hbm, ids.at[:, :atoms]),
        (recip_hbm, recip),
        (kfilt_hbm, kfilt),
    )
    ids[:, atoms:] = jnp.full((1, LANES), -1, jnp.int32)
    waves[:, atoms:] = jnp.zeros((waves.shape[0], LANES), BF16)
    for copy in copies[:3]:
        copy.wait()
    kcols[...] = vector_columns(kvec)
    fill_slice(waves, 0, own, kcols, 0, 0, coords)
    numbers = ids[:, :atoms]
    before = 0
    for cell in range(bounds.shape[1]):
        count = jnp.sum((numbers == cell).astype(F32)).astype(jnp.int32)
        bounds[0, cell] = count
        bounds[1, cell] = before
        before = before + count

    def phase_rows(i, carry):
        fill_slice(waves, 0, own, kcols, 0, 16 * i, coords)
        return carry

    lax.fori_loop(1, own // 16, phase_rows, 0)
    for copy in copies[3:]:
        copy.wait()


def pair_kernel(kvec, other_kvec, kvecs):
    count = kvec.shape[0]
    for j in range(count):
        for at, source in ((j, kvec), (j + count, other_kvec)):
            rows = source[j].astype(F32)
            if rows.shape[0] == 3:
                rows = jnp.concatenate([rows, jnp.zeros((5, rows.shape[1]), F32)], axis=0)
            kvecs[at] = rows


def code_kernel(near, far, out):
    chan = near.shape[2]
    for j, ref in enumerate((near, far)):
        values = ref[0].T
        largest = jnp.max(jnp.abs(values), axis=0, keepdims=True)
        power = jnp.ceil(jnp.log2(jnp.maximum(largest, 1e-30)) + 0.02)
        coded = values * (CODES / jnp.exp2(power))
        coded = (coded + ROUNDER) - ROUNDER
        out[j, :chan, :] = coded.astype(jnp.int32).astype(jnp.int16)
        powers = jnp.broadcast_to(power, (16, power.shape[1]))
        out[j, chan:, :] = powers.astype(jnp.int32).astype(jnp.int16)


def stack_kernel(near, far, out):
    count = near.shape[0]
    out[:count] = near[...]
    out[count:] = far[...]


def project_kernel(coords, kvecs, feats_hbm, w_in_hbm, waves, proj_t, feats, w_in, kcols, sems):
    atoms, chan = feats.shape
    own = kcols.shape[0]
    copies = start_copies(sems, (w_in_hbm, w_in), (feats_hbm, feats))
    waves[:, atoms:] = jnp.zeros((waves.shape[0], LANES), BF16)
    proj_t[:, atoms:] = jnp.zeros((chan, LANES), BF16)
    kcols[...] = vector_columns(kvecs.at[1])
    for copy in copies:
        copy.wait()
    tiles = atoms // TILE

    def project(t, carry):
        at = pl.ds(pl.multiple_of(t * TILE, TILE), TILE)
        proj_t[:, at] = mm(w_in[...], feats[at, :], 0, 1).astype(BF16)
        for row in rows_of_share(t, tiles, own):
            fill_slice(waves, 0, own, kcols, 0, row, coords)
        return carry

    lax.fori_loop(0, tiles, project, 0)


def waves_kernel(n_ka, *refs):
    bounds, first, second, proj_t, ids, coords, recip = refs[:7]
    waves, factors, quad, kcols = refs[-4:]
    kvecs = [ref.at[j] for ref in refs[7:-4] for j in range(ref.shape[0])]
    atoms = coords.shape[1]
    own = kvecs[0].shape[1]
    cells = recip.shape[0]
    most = most_steps(atoms)
    for j in range(2, n_ka):
        kcols[(j - 2) * own : (j - 1) * own, :] = vector_columns(kvecs[j])
    for j in range(n_ka):
        rows = kvecs[j][...]
        squared = jnp.zeros((cells, own), F32)
        for r in range(3):
            part = recip[:, 3 * r : 3 * r + 1] * rows[0:1, :]
            part = part + recip[:, 3 * r + 1 : 3 * r + 2] * rows[1:2, :]
            part = part + recip[:, 3 * r + 2 : 3 * r + 3] * rows[2:3, :]
            squared = squared + part * part
        quad[:, own * j : own * (j + 1)] = squared
    waves[4 * own :, atoms:] = jnp.zeros((2 * own * (n_ka - 2), LANES), BF16)

    def early(cell, carry):
        start, steps, _ = span_of(bounds, cell)

        def action(n):
            at = pl.ds(start, n * TILE)
            lhs = proj_t[:, at] * (ids[:, at] == cell).astype(F32).astype(BF16)
            factors[cell, :, : 2 * own] = mm(lhs, first[:, at], 1, 1)
            factors[cell, :, 2 * own : 4 * own] = mm(lhs, second[:, at], 1, 1)
            for j in range(2, n_ka):
                for row in rows_of_share(cell, cells, own):
                    fill_slice(waves, 2 * own * j, own, kcols, (j - 2) * own, row, coords)

        by_steps(steps, most, action)
        return carry

    lax.fori_loop(0, cells, early, 0)
    waves[: 2 * own, :] = first[...]
    waves[2 * own : 4 * own, :] = second[...]

    def late(cell, carry):
        start, steps, _ = span_of(bounds, cell)

        def action(n):
            at = pl.ds(start, n * TILE)
            lhs = proj_t[:, at] * (ids[:, at] == cell).astype(F32).astype(BF16)
            factors[cell, :, 4 * own :] = mm(lhs, waves[4 * own :, at], 1, 1)

        by_steps(steps, most, action)
        return carry

    lax.fori_loop(0, cells, late, 0)


def filters_first(filt_t, refs):
    chan = filt_t.shape[0]
    chunk = 0
    for ref in refs:
        for j in range(ref.shape[0]):
            if ref.dtype == F32:
                own = ref.shape[1]
                values = ref[j].T
            else:
                coded = ref[j].astype(jnp.int32).astype(F32)
                values = coded[:chan, :] * (jnp.exp2(coded[chan : chan + 1, :]) / CODES)
            filt_t[:, chunk * own : (chunk + 1) * own] = values
            chunk += 1
    return own


def message_kernel(n_ka, *refs):
    bounds, ids, quad, waves, factors, spread, cotan, w_out = refs[:8]
    act_t, mgrad_t, raw_out, raw_half, filt_t, width_cols, even, odd, mess_t = refs[-9:]
    atoms, chan = cotan.shape
    filters_first(filt_t, refs[8:-9])
    width_cols[...] = column_to_lanes(spread[...] * (-LOG2_E))
    spread_cells(n_ka, bounds, ids, quad, filt_t, width_cols, factors, waves, even, odd, mess_t)
    mgrad_t[:, atoms:] = jnp.zeros((chan, LANES), BF16)
    raw_out[...] = jnp.zeros_like(raw_out)

    wide = tile_of(atoms, 2 * TILE)

    def middle(t, carry):
        at = pl.ds(pl.multiple_of(t * wide, wide), wide)
        message = mess_t[:, at]
        sigma = jax.nn.sigmoid(message)
        activated = (message * sigma).astype(BF16)
        act_t[:, at] = activated
        cot = cotan[at, :]
        act_grad = mm(w_out[...], cot, 1, 1)
        mgrad_t[:, at] = (act_grad * (sigma * (1.0 + message * (1.0 - sigma)))).astype(BF16)
        raw_out[...] += mm(activated, cot)
        return carry

    lax.fori_loop(0, atoms // wide, middle, 0)
    raw_half[...] = raw_out[...].astype(BF16)


def adjoint_kernel(n_ka, *refs):
    bounds, ids, quad, waves, factors, mgrad_t, spread = refs[:7]
    sums, filter_grad, filter_half, width_cols, grad_t = refs[7:]
    atoms = mgrad_t.shape[1] - LANES
    cells, k_all = quad.shape
    own = k_all // n_ka
    width_cols[...] = column_to_lanes(spread[...] * (-LOG2_E))
    grad_t[...] = jnp.zeros_like(grad_t)

    most = most_steps(atoms)

    def collect(cell):
        scaled = shape_of(cell, quad, width_cols, 0, own) * inverse_count(bounds[0, cell])
        grad_t[...] += scaled * (
            factors[cell, :, :own] * sums[cell, :, :own]
            + factors[cell, :, own : 2 * own] * sums[cell, :, own : 2 * own]
        )

    def gather(cell, before):
        start, steps, _ = span_of(bounds, cell)

        def action(n):
            if before is not None:
                collect(before)
            at = pl.ds(start, n * TILE)
            lhs = mgrad_t[:, at] * (ids[:, at] == cell).astype(F32).astype(BF16)
            sums[cell] = mm(lhs, waves[:, at], 1, 1)

        by_steps(steps, most, action)

    gather(0, None)

    def cell_step(cell, carry):
        gather(cell, cell - 1)
        return carry

    lax.fori_loop(1, cells, cell_step, 0)
    collect(cells - 1)
    result = grad_t[...].T
    filter_grad[...] = result
    filter_half[...] = result.astype(BF16)


def update_kernel(n_ka, *refs):
    bounds, ids, quad, waves, sums, spread = refs[:6]
    update_t = refs[-11]
    filt_t, width_cols, even, odd, total_t, sems = refs[-6:]
    copies = start_copies(sems, *zip(refs[-15:-11], refs[-10:-6]))
    atoms = update_t.shape[1]
    filters_first(filt_t, refs[6:-15])
    width_cols[...] = column_to_lanes(spread[...] * (-LOG2_E))
    spread_cells(n_ka, bounds, ids, quad, filt_t, width_cols, sums, waves, even, odd, total_t)
    update_t[...] = total_t[:, :atoms].astype(BF16)
    for copy in copies:
        copy.wait()


def gradient_kernel(update_t, feats, raw_in_t):
    raw_in_t[...] = mm(update_t[...], feats[...])


def residual_kernel(transposed, base, values_t, weight, out_hbm, out, sems):
    rows = base.shape[0]
    step = tile_of(rows, 512)
    copies = []
    for t in range(rows // step):
        at = slice(t * step, (t + 1) * step)
        value = mm(values_t[:, at].T, weight[...], 1, 1 if transposed else 0)
        out[at, :] = (base[at, :].astype(F32) + value).astype(BF16)
        copies.append(pltpu.make_async_copy(out.at[at, :], out_hbm.at[at, :], sems.at[t]))
        copies[-1].start()
    for copy in copies:
        copy.wait()


def residual(transposed, base, values_t, weight):
    rows, chan = base.shape
    vmem = pl.BlockSpec(memory_space=pltpu.VMEM)
    return pl.pallas_call(
        functools.partial(residual_kernel, transposed),
        out_shape=jax.ShapeDtypeStruct((rows, chan), BF16),
        in_specs=[vmem] * 3,
        out_specs=pl.BlockSpec(memory_space=pltpu.HBM),
        scratch_shapes=[
            pltpu.VMEM((rows, chan), BF16),
            pltpu.SemaphoreType.DMA((rows // tile_of(rows, 512),)),
        ],
        compiler_params=pltpu.CompilerParams(vmem_limit_bytes=SMALL),
        cost_estimate=pl.CostEstimate(
            flops=2 * FLOPS_PER_MICRO, bytes_accessed=0, transcendentals=0
        ),
    )(base, values_t, weight)


def last_out_kernel(raw_out, other_out, out_sum):
    out_sum[...] = raw_out[...] + other_out[: raw_out.shape[0], :].astype(F32)


def out_kernel(raw_out, other_out, filter_half, out_sum, packed):
    chan = raw_out.shape[0]
    value = raw_out[...] + other_out[:chan, :].astype(F32)
    out_sum[...] = value
    packed[:chan, :] = value.astype(BF16)
    packed[chan:, :] = filter_half[...]


def filter_kernel(*refs):
    own = refs[0].shape[0]
    value = refs[0][...]
    for ref in refs[1:-1]:
        value = value + ref[ref.shape[0] - own :, :].astype(F32)
    refs[-1][...] = value


def squares_kernel(filt, near, f_sum, f_squares):
    value = filt[...] + near[...]
    f_sum[...] = value
    f_squares[...] = jnp.broadcast_to(
        jnp.sum(jnp.sum(value * value, axis=0, keepdims=True), axis=1, keepdims=True),
        f_squares.shape,
    )


def chip_kernel(raw_in_t, near, in_sum, in_half):
    value = raw_in_t[...] + near[...]
    in_sum[...] = value
    in_half[...] = value.astype(BF16)


def total_of(first, others):
    value = first[...]
    for other in others:
        value = value + other[...].astype(F32)
    return value


def add_kernel(first, second, *outs):
    value = first[...] + second[...].astype(F32)
    for out in outs:
        out[...] = value.astype(out.dtype)


def final_kernel(n_chip, n_ka, *refs):
    in_parts = refs[:n_chip]
    raw_out, near_out, filt, squares, g_in, g_out, g_filt = refs[n_chip:]
    raw_in = total_of(in_parts[0], in_parts[1:])
    out = raw_out[...] + near_out[...]
    both = raw_in * raw_in + out * out
    weight_squares = jnp.sum(jnp.sum(both, axis=0, keepdims=True), axis=1, keepdims=True)
    weight_scale = lax.rsqrt(weight_squares / (2 * raw_in.size) + 1e-06)
    filter_scale = lax.rsqrt(squares[0:1, 0:1] / (n_ka * filt.size) + 1e-06)
    g_in[...] = (raw_in * weight_scale).T
    g_out[...] = out * weight_scale
    g_filt[...] = filt[...] * filter_scale


def call(
    kernel, operands, smem, outs, scratch=(), limit=SMALL, micros=2, space=pltpu.VMEM, smem_outs=0
):
    vmem = pl.BlockSpec(memory_space=pltpu.VMEM)
    rest = len(operands) - smem
    spaces = space if isinstance(space, tuple) else (space,) * rest
    return pl.pallas_call(
        kernel,
        out_shape=tuple(jax.ShapeDtypeStruct(*o) for o in outs),
        in_specs=[pl.BlockSpec(memory_space=x) for x in (pltpu.SMEM,) * smem + spaces],
        out_specs=(vmem,) * (len(outs) - smem_outs)
        + (pl.BlockSpec(memory_space=pltpu.SMEM),) * smem_outs,
        scratch_shapes=list(scratch),
        compiler_params=pltpu.CompilerParams(vmem_limit_bytes=limit),
        cost_estimate=pl.CostEstimate(
            flops=micros * FLOPS_PER_MICRO, bytes_accessed=0, transcendentals=0
        ),
    )(*operands)


def in_hbm(value):
    return pltpu.with_memory_space_constraint(value, pltpu.HBM)


def send(value, axis, step):
    return lax.ppermute(value, axis, routes(step, lax.axis_size(axis)))


def doubling(first, size):
    return [first << i for i in range(size.bit_length()) if first << i < size]


def block(feats, coords, cell_ids, recip, kvec, w_in, w_out, kfilt, spread, cotan):
    n_ka = lax.axis_size("ka")
    n_dp = lax.axis_size("dp")
    atoms, chan = feats.shape
    own = kvec.shape[1]
    k_all = own * n_ka
    cells = recip.shape[1]
    long = atoms + LANES
    recip, spread = recip[0], spread[None]
    chips = range(2, n_dp, 2)
    vm = pltpu.VMEM
    dma = pltpu.SemaphoreType.DMA
    near_kvec = send(kvec[None], "ka", 1)
    near_kfilt = send(kfilt[None], "ka", 1)
    first, ids, coords, recip, kvec, kfilt, bounds = call(
        prepare_kernel,
        [in_hbm(x) for x in (coords, cell_ids, recip, kvec, kfilt)],
        0,
        [
            ((2 * own, long), BF16),
            ((1, long), jnp.int32),
            (coords.shape, F32),
            (recip.shape, F32),
            (kvec.shape, jnp.int32),
            (kfilt.shape, F32),
            ((2, cells), jnp.int32),
        ],
        [vm((own, 8), F32), dma((5,))],
        SMALL,
        3,
        pltpu.HBM,
        smem_outs=1,
    )
    kfilt = kfilt[None]
    (kvecs,) = call(pair_kernel, (kvec[None], near_kvec), 0, [((2, 8, own), F32)])
    far_kvecs, far_kfilts = [kvecs], [kfilt, near_kfilt]
    ka_steps = doubling(2, n_ka)
    for s in ka_steps:
        if s > 2:
            (kvecs,) = call(pair_kernel, (kvecs, far_kvecs[-1]), 0, [((s, 8, own), F32)])
        far_kvecs.append(send(kvecs, "ka", s))
    second, proj_t = call(
        project_kernel,
        (coords, far_kvecs[0], in_hbm(feats), in_hbm(w_in)),
        0,
        [((2 * own, long), BF16), ((chan, long), BF16)],
        [vm((atoms, chan), BF16), vm((chan, chan), BF16), vm((own, 8), F32), dma((2,))],
        SMALL,
        3,
        (pltpu.VMEM, pltpu.VMEM, pltpu.HBM, pltpu.HBM),
    )
    kfilts = kfilt
    for s in ka_steps:
        (kfilts,) = call(
            code_kernel if s == 2 else stack_kernel,
            (kfilts, far_kfilts[-1]),
            0,
            [((s, chan + 16, own), jnp.int16)],
        )
        far_kfilts.append(send(kfilts, "ka", s))
    waves, factors, quad = call(
        functools.partial(waves_kernel, n_ka),
        (bounds, first, second, proj_t, ids, coords, recip, *far_kvecs),
        1,
        [((2 * k_all, long), BF16), ((cells, chan, 2 * k_all), F32), ((cells, k_all), F32)],
        [vm((k_all - 2 * own, 8), F32)],
        LIMIT,
        8,
    )
    halves = [vm((2 * n_ka, chan, own), BF16)] * 2
    act_t, mgrad_t, raw_out, raw_half = call(
        functools.partial(message_kernel, n_ka),
        (bounds, ids, quad, waves, factors, spread, cotan, w_out, *far_kfilts),
        1,
        [((chan, atoms), BF16), ((chan, long), BF16), ((chan, chan), F32), ((chan, chan), BF16)],
        [vm((chan, k_all), F32), vm((chan, 8), F32), *halves, vm((chan, long), F32)],
        LIMIT,
        8,
    )
    out_steps = doubling(2, n_dp)
    out_part = send(raw_half, "dp", out_steps[0])
    sums, filter_grad, filter_half = call(
        functools.partial(adjoint_kernel, n_ka),
        (bounds, ids, quad, waves, factors, mgrad_t, spread),
        1,
        [((cells, chan, 2 * k_all), F32), ((own, chan), F32), ((own, chan), BF16)],
        [vm((chan, 8), F32), vm((chan, own), F32)],
        LIMIT,
        6,
    )
    raw_out, packed = call(
        out_kernel,
        (raw_out, out_part, filter_half),
        0,
        [((chan, chan), F32), ((chan + own, chan), BF16)],
    )
    filt_parts = [send(packed if s == 4 else filter_half, "dp", s) for s in chips]
    out_part = filt_parts[1]
    for s in out_steps[2:]:
        raw_out, raw_half = call(
            out_kernel,
            (raw_out, out_part, filter_half),
            0,
            [((chan, chan), F32), ((chan + own, chan), BF16)],
        )
        out_part = send(raw_half, "dp", s)
    held = (feats, cotan, w_in, w_out)
    update_t, feats, cotan, w_in, w_out = call(
        functools.partial(update_kernel, n_ka),
        (bounds, ids, quad, waves, sums, spread, *far_kfilts, *map(in_hbm, held)),
        1,
        [((chan, atoms), BF16), *((x.shape, BF16) for x in held)],
        [vm((chan, k_all), F32), vm((chan, 8), F32), *halves, vm((chan, long), F32), dma((4,))],
        LIMIT,
        8,
        (pltpu.VMEM,) * (5 + len(far_kfilts)) + (pltpu.HBM,) * 4,
    )
    (filt_sum,) = call(filter_kernel, (filter_grad, *filt_parts), 0, [((own, chan), F32)])
    filt_near = send(filt_sum, "dp", 1)
    (raw_in_t,) = call(gradient_kernel, (update_t, feats), 0, [((chan, chan), F32)])
    near = send(raw_in_t, "dp", 1)
    (out_sum,) = call(last_out_kernel, (raw_out, out_part), 0, [((chan, chan), F32)])
    near_out = send(out_sum, "dp", 1)
    f_sum, squares = call(
        squares_kernel, (filt_sum, filt_near), 0, [((own, chan), F32), ((8, LANES), F32)]
    )
    square_steps = doubling(1, n_ka)
    square_part = send(squares, "ka", square_steps[0])
    feat_grad = residual(True, cotan, update_t, w_in)
    in_sum, in_half = call(
        chip_kernel, (raw_in_t, near), 0, [((chan, chan), F32), ((chan, chan), BF16)]
    )
    in_parts = [in_sum] + [send(in_half, "dp", s) for s in chips]
    for s in square_steps[1:] + [0]:
        (squares,) = call(add_kernel, (squares, square_part), 0, [((8, LANES), F32)])
        if s:
            square_part = send(squares, "ka", s)
    mixed = residual(False, feats, act_t, w_out)
    grads = call(
        functools.partial(final_kernel, len(in_parts), n_ka),
        (*in_parts, out_sum, near_out, f_sum, squares),
        0,
        [((chan, chan), F32), ((chan, chan), F32), ((own, chan), F32)],
    )
    return (mixed, feat_grad, *grads)


def solution(mesh):
    placed = (
        P("dp", None),
        P(None, "dp"),
        P("dp", None),
        P("dp", None, None),
        P(None, "ka"),
        P(),
        P(),
        P("ka", None),
        P(),
        P("dp", None),
    )
    return jax.shard_map(
        block,
        mesh=mesh,
        in_specs=placed,
        out_specs=(P("dp", None), P("dp", None), P(), P(), P("ka", None)),
        check_vma=False,
    )
```
